32 devices in a mesh: dp: 8 (over y, x, core), fsdp: 4 (over z).
Axes of the slice: x: 2, y: 2, z: 4, core: 2. Of those that a mesh axis runs over, the one named last changes fastest.
Arguments:
- images: bfloat16 [64, 256, 1152], P(('dp', 'fsdp')), may hold values from -6 to 6
- time_vector: bfloat16 [64, 1152], P(('dp', 'fsdp')), may hold values from -6 to 6
- timesteps: int32 [64], P(('dp', 'fsdp')), may hold values from 0 to 999
- offset_index: int32 [256, 256], replicated, may hold values from 0 to 960
- query_weight: bfloat16 [1152, 1152], P('dp', 'fsdp'), may hold values from -0.1875 to 0.1875
- key_weight: bfloat16 [1152, 1152], P('dp', 'fsdp'), may hold values from -0.1875 to 0.1875
- value_weight: bfloat16 [1152, 1152], P('dp', 'fsdp'), may hold values from -0.1875 to 0.1875
- tquery_weight: bfloat16 [1152, 1152], P('dp', 'fsdp'), may hold values from -0.1875 to 0.1875
- tvalue_weight: bfloat16 [1152, 1152], P('dp', 'fsdp'), may hold values from -0.1875 to 0.1875
- proj_weight: bfloat16 [1152, 1152], P('dp', 'fsdp'), may hold values from -0.5 to 0.5
- proj_bias: bfloat16 [1152], P('fsdp'), may hold values from -4 to 4
- first_gain: bfloat16 [1152], P('fsdp'), may hold values from 0.5 to 1.5
- first_shift: bfloat16 [1152], P('fsdp'), may hold values from -4 to 4
- second_gain: bfloat16 [1152], P('fsdp'), may hold values from 0.5 to 1.5
- second_shift: bfloat16 [1152], P('fsdp'), may hold values from -4 to 4
- up_weight: bfloat16 [1152, 4608], P('dp', 'fsdp'), may hold values from -0.1875 to 0.1875
- down_weight: bfloat16 [4608, 1152], P('dp', 'fsdp'), may hold values from -0.125 to 0.125
- up_bias: bfloat16 [4608], P('fsdp'), may hold values from -6 to 6
- down_bias: bfloat16 [1152], P('fsdp'), may hold values from -4 to 4
- bias_table: bfloat16 [16, 961], P('fsdp'), may hold values from -6 to 6
- cotangent: bfloat16 [64, 256, 1152], P(('dp', 'fsdp')), may hold values from -6 to 6
Outputs:
- layer_out: bfloat16 [64, 256, 1152], P(('dp', 'fsdp'))
- images_grad: bfloat16 [64, 256, 1152], P(('dp', 'fsdp'))
- time_grad: float32 [64, 1152], P(('dp', 'fsdp'))
- query_grad: float32 [1152, 1152], P('dp', 'fsdp')
- key_grad: float32 [1152, 1152], P('dp', 'fsdp')
- value_grad: float32 [1152, 1152], P('dp', 'fsdp')
- tquery_grad: float32 [1152, 1152], P('dp', 'fsdp')
- tvalue_grad: float32 [1152, 1152], P('dp', 'fsdp')
- proj_grad: float32 [1152, 1152], P('dp', 'fsdp')
- proj_bias_grad: float32 [1152], P('fsdp')
- first_gain_grad: float32 [1152], P('fsdp')
- first_shift_grad: float32 [1152], P('fsdp')
- second_gain_grad: float32 [1152], P('fsdp')
- second_shift_grad: float32 [1152], P('fsdp')
- up_grad: float32 [1152, 4608], P('dp', 'fsdp')
- down_grad: float32 [4608, 1152], P('dp', 'fsdp')
- up_bias_grad: float32 [4608], P('fsdp')
- down_bias_grad: float32 [1152], P('fsdp')
- table_grad: float32 [16, 961], P('fsdp')
The draws below stay inside these ranges and needn't reach their ends.
All inputs are finite; a program needn't handle non-finite values.
Results may differ from the reference program's by a relative error of at most 0.017.
Values may be sent and summed in bfloat16 or wider, within the bound.
No kernel may reach another device: no remote copies, remote signals or barrier semaphores. Data moves between devices by JAX's collectives and lax.ppermute only.
A program may use at most 384 MiB of HBM per device.

```python
import math
import jax
import jax.numpy as jnp
from jax import lax

D = 1152
H = 16
FF = 4608
P_SIZE = 256
NB = 961
IMAGES = 64


def place_ends(array, rng, low, high):
    shape = array.shape
    index_at = [jax.random.randint(jax.random.fold_in(rng, axis), (), 0, shape[axis]) for axis in range(len(shape))]
    array = array.at[tuple(index_at)].set(low)
    longest = shape.index(max(shape))
    index_at[longest] = (index_at[longest] + 1) % shape[longest]
    return array.at[tuple(index_at)].set(high)


def spiked(entries, own_key, source, target, shards_of, factor):
    def block_of(dim):
        return (jnp.arange(entries.shape[dim]) // (entries.shape[dim] // shards_of)).reshape((-1,) + (1,) * (entries.ndim - 1 - dim))

    first = jax.random.permutation(own_key, shards_of)[block_of(target)]
    other_side = (block_of(target) + shards_of // 2) % shards_of
    return jnp.where((block_of(source) == first) | (block_of(source) == other_side), factor * entries, entries)


def level_of(rng, shape, shards, low, high):
    def one(dim, blocks):
        draws = jax.random.uniform(jax.random.fold_in(jax.random.fold_in(rng, 6), dim), (blocks,), jnp.float32, low / len(shards), high / len(shards))
        return jnp.repeat(jnp.exp(draws), shape[dim] // blocks).reshape((-1,) + (1,) * (len(shape) - dim - 1))

    factor_of = one(*shards[0])
    for cut in shards[1:]:
        factor_of = factor_of * one(*cut)
    return factor_of


def centred(stream_key, extent, spread, most, cuts=(), held_as=jnp.bfloat16):
    entries = spread * jax.random.normal(stream_key, extent, jnp.float32)
    if cuts:
        entries = entries * level_of(stream_key, extent, cuts, -0.22, 0.18)
    return jnp.clip(entries, -most, most).astype(held_as)


def gaussian_with(stream_key, shape, width, bound, pieces, heavy, dtype=jnp.bfloat16):
    drawn = width * jax.random.normal(stream_key, shape, jnp.float32)
    if pieces:
        drawn = drawn * level_of(stream_key, shape, pieces, -0.22, 0.18)
    return jnp.clip(spiked(drawn, jax.random.fold_in(stream_key, 3), *heavy), -bound, bound).astype(dtype)


def setup_inputs(seed: int = 0) -> dict:
    seeds = jax.random.split(jax.random.key(seed), 22)
    return {
        "images": centred(seeds[0], (IMAGES, P_SIZE, D), 1.0, 6.0, ((0, 32),)),
        "time_vector": centred(seeds[1], (IMAGES, D), 1.0, 6.0, ((0, 32),)),
        "timesteps": place_ends(jax.random.randint(seeds[2], (IMAGES,), 0, 1000), jax.random.fold_in(seeds[2], 1), 0, 999).astype(jnp.int32),
        "offset_index": place_ends(jax.random.randint(seeds[3], (P_SIZE, P_SIZE), 0, NB), jax.random.fold_in(seeds[3], 1), 0, NB - 1).astype(jnp.int32),
        "query_weight": centred(seeds[4], (D, D), D ** -0.5, 0.1875, ((0, 8), (1, 4))),
        "key_weight": centred(seeds[5], (D, D), D ** -0.5, 0.1875, ((0, 8), (1, 4))),
        "value_weight": centred(seeds[6], (D, D), D ** -0.5, 0.1875, ((0, 8), (1, 4))),
        "tquery_weight": centred(seeds[7], (D, D), D ** -0.5, 0.1875, ((0, 8), (1, 4))),
        "tvalue_weight": centred(seeds[8], (D, D), D ** -0.5, 0.1875, ((0, 8), (1, 4))),
        "proj_weight": centred(seeds[9], (D, D), (D // 8) ** -0.5, 0.5, ((0, 8), (1, 4))),
        "proj_bias": centred(seeds[10], (D,), 0.3, 4.0, ((0, 4),)),
        "first_gain": jnp.clip(1.0 + 0.1 * jax.random.normal(seeds[11], (D,), jnp.float32), 0.5, 1.5).astype(jnp.bfloat16),
        "first_shift": centred(seeds[12], (D,), 0.3, 4.0, ((0, 4),)),
        "second_gain": jnp.clip(1.0 + 0.1 * jax.random.normal(seeds[13], (D,), jnp.float32), 0.5, 1.5).astype(jnp.bfloat16),
        "second_shift": centred(seeds[14], (D,), 0.3, 4.0, ((0, 4),)),
        "up_weight": centred(seeds[15], (D, FF), D ** -0.5, 0.1875, ((0, 8), (1, 4))),
        "down_weight": centred(seeds[16], (FF, D), (FF // 2) ** -0.5, 0.125, ((0, 8), (1, 4))),
        "up_bias": centred(seeds[17], (FF,), 0.5, 6.0, ((0, 4),)),
        "down_bias": centred(seeds[18], (D,), 0.3, 4.0, ((0, 4),)),
        "bias_table": centred(seeds[19], (H, NB), 1.0, 6.0, ((0, 4),)),
        "cotangent": gaussian_with(seeds[20], (IMAGES, P_SIZE, D), 1.0, 6.0, ((0, 32),), (0, 2, 32, 2.75)),
    }


@jax.custom_vjp
def low(v):
    return lax.optimization_barrier(v.astype(jnp.bfloat16)).astype(jnp.float32)

@jax.custom_vjp
def low_back(v):
    return v

def low_keep(v):
    return (low(v), None)

def low_pass(kept, grad):
    return (grad,)

def back_keep(v):
    return (v, None)

def back_low(kept, grad):
    return (low(grad),)
low.defvjp(low_keep, low_pass)
low_back.defvjp(back_keep, back_low)

def sinusoid(steps, model_width):
    half_width = model_width // 2
    frequency = jnp.exp(-math.log(10000.0) * jnp.arange(half_width).astype(jnp.float32) / half_width)
    angles = steps.astype(jnp.float32)[:, None] * frequency[None, :]
    return jnp.concatenate([jnp.sin(angles), jnp.cos(angles)], axis=1)

def matmul(left, right):
    return jnp.einsum('...d,de->...e', left, right, precision=lax.Precision.HIGHEST)

def normalize(values, gain, shift):
    row_mean = lax.optimization_barrier(jnp.mean(values, axis=-1, keepdims=True))
    centered = values - row_mean
    inv_std = lax.rsqrt(lax.optimization_barrier(jnp.mean(centered * centered, axis=-1, keepdims=True)) + 1e-06)
    return centered * inv_std * gain + shift

def layer(params, offset_index, group_in):
    image_rows, time_rows, step_rows = group_in
    query_weight, key_weight, value_weight, tquery_weight, tvalue_weight, proj_weight, proj_bias, first_gain, first_shift, second_gain, second_shift, up_weight, down_weight, up_bias, down_bias, bias_table = params
    count, tokens, model_width = image_rows.shape
    head_count = bias_table.shape[0]
    head_dim = model_width // head_count
    time_low = low(time_rows + sinusoid(step_rows, model_width))
    normed = low(normalize(image_rows, first_gain, first_shift))
    time_query = low_back(matmul(time_low, tquery_weight))
    time_value = low_back(matmul(time_low, tvalue_weight))
    query = low(low_back(matmul(normed, query_weight) + time_query[:, None, :]))
    keys = low(low_back(matmul(normed, key_weight)))
    values = low(low_back(matmul(normed, value_weight) + time_value[:, None, :]))
    split_shape = (count, tokens, head_count, head_dim)
    scores = jnp.einsum('bqhd,bkhd->bhqk', query.reshape(split_shape), keys.reshape(split_shape), precision=lax.Precision.HIGHEST) * (1.0 / math.sqrt(head_dim))
    scores = low_back(scores + bias_table[:, offset_index][None])
    peak = lax.optimization_barrier(jnp.max(scores, axis=-1, keepdims=True))
    expo = jnp.exp(scores - peak)
    probs = expo / lax.optimization_barrier(jnp.sum(expo, axis=-1, keepdims=True))
    mixed = jnp.einsum('bhqk,bkhd->bqhd', low(probs), values.reshape(split_shape), precision=lax.Precision.HIGHEST).reshape(count, tokens, model_width)
    mixed = low(low_back(mixed))
    hidden = image_rows + low_back(matmul(mixed, proj_weight) + proj_bias)
    second = low(normalize(hidden, second_gain, second_shift))
    pre_act = low_back(matmul(second, up_weight) + up_bias)
    activ = low(jax.nn.gelu(pre_act, approximate=False))
    return hidden + low_back(matmul(activ, down_weight) + down_bias)

def reference(images, time_vector, timesteps, offset_index, query_weight, key_weight, value_weight, tquery_weight, tvalue_weight, proj_weight, proj_bias, first_gain, first_shift, second_gain, second_shift, up_weight, down_weight, up_bias, down_bias, bias_table, cotangent):
    params = tuple((weight.astype(jnp.float32) for weight in (query_weight, key_weight, value_weight, tquery_weight, tvalue_weight, proj_weight, proj_bias, first_gain, first_shift, second_gain, second_shift, up_weight, down_weight, up_bias, down_bias, bias_table)))
    count_all, tokens, model_width = images.shape
    group = math.gcd(count_all, max(1, 4096 // tokens))
    blocks = count_all // group
    steps_grouped = timesteps.reshape(blocks, group)

    def whole(param_set, image_all, time_all):

        def group_step(carry, group_in):
            return (carry, layer(param_set, offset_index, group_in))
        inputs = (image_all.reshape(blocks, group, tokens, model_width), time_all.reshape(blocks, group, model_width), steps_grouped)
        final_carry, outputs = lax.scan(jax.checkpoint(group_step), None, inputs)
        return outputs.reshape(count_all, tokens, model_width)
    layer_out, pullback = jax.vjp(whole, params, images.astype(jnp.float32), time_vector.astype(jnp.float32))
    param_grads, images_grad, time_grad = pullback(cotangent.astype(jnp.float32))
    return (layer_out.astype(jnp.bfloat16), images_grad.astype(jnp.bfloat16), time_grad, param_grads[0], param_grads[1], param_grads[2], param_grads[3], param_grads[4], param_grads[5], param_grads[6], param_grads[7], param_grads[8], param_grads[9], param_grads[10], param_grads[11], param_grads[12], param_grads[13], param_grads[14], param_grads[15])
```

```python
import math

import jax
import jax.numpy as jnp
from jax import lax
from jax.experimental import pallas as pl
from jax.experimental.pallas import tpu as pltpu
from jax.sharding import PartitionSpec as P

LANES = 128
BOTH = ("dp", "fsdp")
VMEM_LIMIT = 58 * 1024 * 1024


def sinusoid(steps, model_width):
    half_width = model_width // 2
    frequency = jnp.exp(
        -math.log(10000.0) * jnp.arange(half_width).astype(jnp.float32) / half_width
    )
    angles = steps.astype(jnp.float32)[:, None] * frequency[None, :]
    return jnp.concatenate([jnp.sin(angles), jnp.cos(angles)], axis=1)


def matmul(left, right):
    return jnp.dot(left, right, preferred_element_type=jnp.float32)


def contract_rows(left, right):
    return lax.dot_general(
        left, right, (((0,), (0,)), ((), ())), preferred_element_type=jnp.float32
    )


def times_transposed(left, right):
    return lax.dot_general(
        left, right, (((1,), (1,)), ((), ())), preferred_element_type=jnp.float32
    )


def normalize(values, gain, shift):
    row_mean = jnp.mean(values, axis=-1, keepdims=True)
    centered = values - row_mean
    inv_std = lax.rsqrt(jnp.mean(centered * centered, axis=-1, keepdims=True) + 1e-06)
    unit_rows = centered * inv_std
    return (unit_rows * gain + shift, unit_rows, inv_std)


def norm_back(grad_rows, unit_rows, inv_std, gain):
    scaled = grad_rows * gain
    return inv_std * (
        scaled
        - jnp.mean(scaled, axis=-1, keepdims=True)
        - unit_rows * jnp.mean(scaled * unit_rows, axis=-1, keepdims=True)
    )


def gelu_slope(pre_act):
    return 0.5 * (1.0 + lax.erf(pre_act * (1.0 / math.sqrt(2.0)))) + pre_act * jnp.exp(
        -0.5 * pre_act * pre_act
    ) * (1.0 / math.sqrt(2.0 * math.pi))


def params(count=1):
    return pltpu.CompilerParams(
        dimension_semantics=("arbitrary",) * count, vmem_limit_bytes=VMEM_LIMIT
    )


def bias_kernel(index_ref, table_ref, bias_ref):
    chunks = table_ref.shape[2] // LANES
    rows = index_ref.shape[0]
    for head in range(table_ref.shape[0]):
        line = table_ref[head]
        pieces = [
            jnp.broadcast_to(line[:, c * LANES : (c + 1) * LANES], (8, LANES))
            for c in range(chunks)
        ]

        def some_rows(step, carry, head=head, pieces=pieces):
            for part in range(2):
                at = pl.multiple_of(step * 16 + part * 8, 8)
                for col in range(index_ref.shape[1] // LANES):
                    lanes = slice(col * LANES, (col + 1) * LANES)
                    index = index_ref[pl.ds(at, 8), lanes]
                    low = index & (LANES - 1)
                    high = index >> 7
                    found = jnp.take_along_axis(pieces[0], low, axis=1)
                    for c in range(1, chunks):
                        found = jnp.where(
                            high == c, jnp.take_along_axis(pieces[c], low, axis=1), found
                        )
                    bias_ref[head, pl.ds(at, 8), lanes] = found
            return carry

        lax.fori_loop(0, rows // 16, some_rows, 0)


def position_bias(index, table):
    heads, padded = table.shape
    tokens = index.shape[0]
    group = heads // 4
    return pl.pallas_call(
        bias_kernel,
        grid=(4,),
        in_specs=[
            pl.BlockSpec((tokens, tokens), lambda f: (0, 0)),
            pl.BlockSpec((group, 1, padded), lambda f: (f, 0, 0)),
        ],
        out_specs=pl.BlockSpec((group, tokens, tokens), lambda f: (f, 0, 0)),
        out_shape=jax.ShapeDtypeStruct((heads, tokens, tokens), jnp.float32),
        compiler_params=params(),
        name="position_bias",
    )(index, table.reshape(heads, 1, padded))


def table_kernel(index_ref, pairs_ref, out_ref):
    heads = pairs_ref.shape[0]
    tokens = index_ref.shape[1]
    rows = index_ref.shape[0]

    @pl.when(pl.program_id(0) == 0)
    def _():
        out_ref[...] = jnp.zeros_like(out_ref)

    sub = lax.broadcasted_iota(jnp.int32, (8, tokens), 0)
    lane_of = lax.broadcasted_iota(jnp.int32, (LANES, tokens), 0)

    def one_row(row, total):
        index = index_ref[pl.ds(row, 1), :]
        low = jnp.broadcast_to(index & (LANES - 1), (LANES, tokens))
        high = jnp.broadcast_to(index >> 7, (8, tokens))
        hit = sub == high
        left = jnp.concatenate(
            [
                jnp.where(hit, jnp.broadcast_to(pairs_ref[h, pl.ds(row, 1), :], (8, tokens)), 0.0)
                for h in range(heads)
            ],
            axis=0,
        ).astype(jnp.bfloat16)
        right = jnp.where(lane_of == low, 1.0, 0.0).astype(jnp.bfloat16)
        return total + times_transposed(left, right)

    def two_rows(step, total):
        return one_row(step * 2 + 1, one_row(step * 2, total))

    out_ref[...] += lax.fori_loop(
        0, rows // 2, two_rows, jnp.zeros((heads * 8, LANES), jnp.float32)
    )


def table_gradient(index, pairs):
    heads, tokens, _ = pairs.shape
    block = 64
    return pl.pallas_call(
        table_kernel,
        grid=(tokens // block,),
        in_specs=[
            pl.BlockSpec((block, tokens), lambda i: (i, 0)),
            pl.BlockSpec((heads, block, tokens), lambda i: (0, i, 0)),
        ],
        out_specs=pl.BlockSpec((heads * 8, LANES), lambda i: (0, 0)),
        out_shape=jax.ShapeDtypeStruct((heads * 8, LANES), jnp.float32),
        compiler_params=params(),
        name="table_gradient",
    )(index, pairs)


def attend_kernel(normed_ref, weight_ref, add_ref, bias_ref, qkv_ref, probs_ref, mixed_ref):
    images, heads = probs_ref.shape[1], probs_ref.shape[2]
    tokens = probs_ref.shape[3]
    width = mixed_ref.shape[2]
    size = width // heads
    scale = 1.0 / math.sqrt(size)
    kept = qkv_ref.shape[2]
    for image in range(images):
        rows = slice(image * tokens, (image + 1) * tokens)
        acc = matmul(normed_ref[rows, :], weight_ref[0, :, :kept])
        qkv_ref[0, rows, :] = (acc + add_ref[0, image : image + 1, :]).astype(jnp.bfloat16)
    for image in range(images):
        rows = slice(image * tokens, (image + 1) * tokens)
        both = qkv_ref[0, rows, :]
        outs = []
        for head in range(heads):
            at = head * size
            query = both[:, at : at + size]
            keys = both[:, width + at : width + at + size]
            values = both[:, 2 * width + at : 2 * width + at + size]
            scores = times_transposed(query, keys) * scale + bias_ref[head]
            peak = jnp.max(scores, axis=-1, keepdims=True)
            expo = jnp.exp(scores - peak)
            total = jnp.sum(expo, axis=-1, keepdims=True)
            probs = (expo / total).astype(jnp.bfloat16)
            probs_ref[0, image, head] = probs
            outs.append(matmul(probs, values))
        mixed_ref[0, rows, :] = jnp.concatenate(outs, axis=1).astype(jnp.bfloat16)


def attend(normed, weight, add, bias, images, tokens):
    groups, depth, packed = weight.shape
    heads = bias.shape[0] // groups
    width = packed // groups
    kept = add.shape[2]
    rows = images * tokens
    return pl.pallas_call(
        attend_kernel,
        grid=(groups,),
        in_specs=[
            pl.BlockSpec((rows, depth), lambda f: (0, 0)),
            pl.BlockSpec((1, depth, packed), lambda f: (f, 0, 0)),
            pl.BlockSpec((1, images, kept), lambda f: (f, 0, 0)),
            pl.BlockSpec((heads, tokens, tokens), lambda f: (f, 0, 0)),
        ],
        out_specs=[
            pl.BlockSpec((1, rows, kept), lambda f: (f, 0, 0)),
            pl.BlockSpec((1, images, heads, tokens, tokens), lambda f: (f, 0, 0, 0, 0)),
            pl.BlockSpec((1, rows, width), lambda f: (f, 0, 0)),
        ],
        out_shape=[
            jax.ShapeDtypeStruct((groups, rows, kept), jnp.bfloat16),
            jax.ShapeDtypeStruct((groups, images, heads, tokens, tokens), jnp.bfloat16),
            jax.ShapeDtypeStruct((groups, rows, width), jnp.bfloat16),
        ],
        compiler_params=params(),
        name="attend",
    )(normed, weight, add, bias)


def attend_back_kernel(grad_ref, qkv_ref, probs_ref, hidden_ref, out_ref, pairs_ref):
    images, heads = probs_ref.shape[1], probs_ref.shape[2]
    tokens = probs_ref.shape[3]
    width = grad_ref.shape[2]
    size = width // heads
    scale = 1.0 / math.sqrt(size)
    for image in range(images):
        rows = slice(image * tokens, (image + 1) * tokens)
        both = qkv_ref[0, rows, :]
        grads = grad_ref[0, rows, :]
        d_query, d_keys, d_values = [], [], []
        for head in range(heads):
            at = head * size
            query = both[:, at : at + size]
            keys = both[:, width + at : width + at + size]
            values = both[:, 2 * width + at : 2 * width + at + size]
            grad = grads[:, at : at + size]
            probs_low = probs_ref[0, image, head]
            probs = probs_low.astype(jnp.float32)
            d_values.append(contract_rows(probs_low, grad))
            d_probs = times_transposed(grad, values)
            moved = probs * d_probs
            d_scores = moved - probs * jnp.sum(moved, axis=-1, keepdims=True)
            d_low = d_scores.astype(jnp.bfloat16)
            if image == 0:
                pairs_ref[head] = d_low.astype(jnp.float32)
            else:
                pairs_ref[head] += d_low.astype(jnp.float32)
            d_query.append(matmul(d_low, keys) * scale)
            d_keys.append(contract_rows(d_low, query) * scale)
        out_ref[0, rows, :] = jnp.concatenate(
            d_query + d_keys + d_values + [hidden_ref[0, rows, :].astype(jnp.float32)], axis=1
        ).astype(jnp.bfloat16)


def attend_back(grad, qkv, probs, hidden):
    groups, rows, width = grad.shape
    kept = qkv.shape[2]
    _, images, heads, tokens, _ = probs.shape
    packed = 4 * width
    return pl.pallas_call(
        attend_back_kernel,
        grid=(groups,),
        in_specs=[
            pl.BlockSpec((1, rows, width), lambda f: (f, 0, 0)),
            pl.BlockSpec((1, rows, kept), lambda f: (f, 0, 0)),
            pl.BlockSpec((1, images, heads, tokens, tokens), lambda f: (f, 0, 0, 0, 0)),
            pl.BlockSpec((1, rows, width), lambda f: (f, 0, 0)),
        ],
        out_specs=[
            pl.BlockSpec((1, rows, packed), lambda f: (f, 0, 0)),
            pl.BlockSpec((heads, tokens, tokens), lambda f: (f, 0, 0)),
        ],
        out_shape=[
            jax.ShapeDtypeStruct((groups, rows, packed), jnp.bfloat16),
            jax.ShapeDtypeStruct((groups * heads, tokens, tokens), jnp.float32),
        ],
        compiler_params=params(),
        name="attend_back",
    )(grad, qkv, probs, hidden)


def pair_grad_kernel(one_ref, two_ref, right_ref, out_ref):
    cut = 3 * (right_ref.shape[2] // 4)
    below = cut // LANES * LANES
    above = below + LANES
    right = right_ref[0]
    first = matmul(one_ref[...], right[:, :above])
    last = matmul(two_ref[...], right[:, below:])
    lane = lax.broadcasted_iota(jnp.int32, (first.shape[0], LANES), 1)
    out_ref[0, :, :below] = first[:, :below].astype(jnp.bfloat16)
    out_ref[0, :, below:above] = jnp.where(
        lane < cut - below, first[:, below:], last[:, :LANES]
    ).astype(jnp.bfloat16)
    out_ref[0, :, above:] = last[:, LANES:].astype(jnp.bfloat16)


def pair_grad(normed_t, mixed_t, right):
    groups, rows, packed = right.shape
    depth = normed_t.shape[0]
    return pl.pallas_call(
        pair_grad_kernel,
        grid=(groups,),
        in_specs=[
            pl.BlockSpec((depth, rows), lambda f: (0, 0)),
            pl.BlockSpec((depth, rows), lambda f: (0, 0)),
            pl.BlockSpec((1, rows, packed), lambda f: (f, 0, 0)),
        ],
        out_specs=pl.BlockSpec((1, depth, packed), lambda f: (f, 0, 0)),
        out_shape=jax.ShapeDtypeStruct((groups, depth, packed), jnp.bfloat16),
        compiler_params=params(),
        name="pair_grad",
    )(normed_t, mixed_t, right)


def pack_down_kernel(in_ref, out_ref):
    groups, _, rows, packed = out_ref.shape
    width = packed // groups
    count = in_ref.shape[0] // rows
    for g in range(count):
        block = in_ref[g * rows : (g + 1) * rows, :]
        for f in range(groups):
            out_ref[f, 0, :, g * width : (g + 1) * width] = block[:, f * width : (f + 1) * width]


def unpack_down_kernel(in_ref, out_ref):
    groups, _, rows, packed = in_ref.shape
    width = packed // groups
    count = out_ref.shape[0] // rows
    for f in range(groups):
        block = in_ref[f, 0]
        for g in range(count):
            out_ref[g * rows : (g + 1) * rows, f * width : (f + 1) * width] = block[
                :, g * width : (g + 1) * width
            ]


def pack_down(natural, groups, parts, rows):
    total, width = natural.shape
    count = total // (parts * rows)
    if rows % 16:
        split = natural.reshape(parts, count, rows, groups, width // groups)
        return split.transpose(3, 0, 2, 1, 4).reshape(groups, parts, rows, width)
    return pl.pallas_call(
        pack_down_kernel,
        grid=(parts,),
        in_specs=[pl.BlockSpec((count * rows, width), lambda d: (d, 0))],
        out_specs=pl.BlockSpec((groups, 1, rows, width), lambda d: (0, d, 0, 0)),
        out_shape=jax.ShapeDtypeStruct((groups, parts, rows, width), natural.dtype),
        compiler_params=params(),
        name="pack_down",
    )(natural)


def unpack_down(packed):
    groups, parts, rows, width = packed.shape
    count = 4
    if rows % 16:
        split = packed.reshape(groups, parts, rows, count, width // count)
        return split.transpose(1, 3, 2, 0, 4).reshape(parts * count * rows, width)
    return pl.pallas_call(
        unpack_down_kernel,
        grid=(parts,),
        in_specs=[pl.BlockSpec((groups, 1, rows, width), lambda d: (0, d, 0, 0))],
        out_specs=pl.BlockSpec((count * rows, width), lambda d: (d, 0)),
        out_shape=jax.ShapeDtypeStruct((parts * count * rows, width), packed.dtype),
        compiler_params=params(),
        name="unpack_down",
    )(packed)


def take_proj_kernel(in_ref, out_ref):
    groups = in_ref.shape[0]
    width = out_ref.shape[1] // groups
    skip = in_ref.shape[2] - width
    for f in range(groups):
        out_ref[:, f * width : (f + 1) * width] = in_ref[f][:, skip:]


def take_proj(packed):
    groups, depth, width = packed.shape
    block = 288
    tail = width // 3
    return pl.pallas_call(
        take_proj_kernel,
        grid=(depth // block,),
        in_specs=[pl.BlockSpec((groups, block, tail), lambda d: (0, d, 2))],
        out_specs=pl.BlockSpec((block, width), lambda d: (d, 0)),
        out_shape=jax.ShapeDtypeStruct((depth, width), packed.dtype),
        compiler_params=params(),
        name="take_proj",
    )(packed)


def gather_shards(shard):
    rows, width = shard.shape
    groups, parts = lax.axis_size("fsdp"), lax.axis_size("dp")
    full = lax.all_gather(shard, ("fsdp", "dp"), axis=0, tiled=True)
    return full.reshape(groups, parts, rows, width)


def scatter_sum(terms):
    groups, parts, rows, width = terms.shape
    return lax.psum_scatter(
        terms.reshape(groups * parts * rows, width),
        ("fsdp", "dp"),
        scatter_dimension=0,
        tiled=True,
    )


def body(
    images,
    time_vector,
    timesteps,
    offset_index,
    query_weight,
    key_weight,
    value_weight,
    tquery_weight,
    tvalue_weight,
    proj_weight,
    proj_bias,
    first_gain,
    first_shift,
    second_gain,
    second_shift,
    up_weight,
    down_weight,
    up_bias,
    down_bias,
    bias_table,
    cotangent,
):
    low = jnp.bfloat16
    wide = jnp.float32
    count, tokens, width = images.shape
    rows = count * tokens
    groups, parts = lax.axis_size("fsdp"), lax.axis_size("dp")
    shard_rows, shard_cols = query_weight.shape
    group_heads, table_rows = bias_table.shape
    heads = group_heads * groups
    fold = down_weight.shape[0] // shard_rows
    own_part = lax.axis_index("dp")
    own_group = lax.axis_index("fsdp")

    wire_attn = jnp.concatenate([query_weight, key_weight, value_weight, proj_weight], axis=1)
    wire_down = jnp.concatenate(
        [down_weight[g * shard_rows : (g + 1) * shard_rows] for g in range(fold)], axis=1
    )
    small = jnp.concatenate(
        [
            proj_bias,
            first_gain,
            first_shift,
            second_gain,
            second_shift,
            down_bias,
            up_bias,
            bias_table.reshape(-1),
        ]
    )
    small = jnp.pad(small, (0, -small.shape[0] % 1024))
    small_all = lax.all_gather(small, "fsdp", axis=0, tiled=False)

    def vector_of(slot):
        return small_all[:, slot * shard_cols : (slot + 1) * shard_cols].reshape(-1).astype(wide)

    proj_b, gain_one, shift_one, gain_two, shift_two, down_b = (vector_of(i) for i in range(6))
    at = 6 * shard_cols
    up_b = small_all[:, at : at + up_bias.shape[0]].astype(wide)
    at = at + up_bias.shape[0]
    table = small_all[:, at : at + group_heads * table_rows].reshape(heads, table_rows)
    table = jnp.pad(table.astype(wide), ((0, 0), (0, -table_rows % LANES)))

    time_low = (time_vector.astype(wide) + sinusoid(timesteps, width)).astype(low)
    time_all = lax.all_gather(time_low, BOTH, axis=0, tiled=True)
    all_images = time_all.shape[0]
    time_cols = lax.dynamic_slice(
        time_all, (0, own_part * shard_rows), (all_images, shard_rows)
    )
    time_weight = jnp.concatenate([tquery_weight, tvalue_weight], axis=1)
    time_sum = lax.psum_scatter(
        matmul(time_cols, time_weight), "dp", scatter_dimension=0, tiled=True
    )
    time_part = lax.all_gather(time_sum, "fsdp", axis=0, tiled=False)
    time_own = lax.dynamic_slice(
        time_part, (0, own_group * count, 0), (groups, count, 2 * shard_cols)
    )
    gap = jnp.zeros((groups, count, shard_cols), wide)
    kept = -(-3 * shard_cols // LANES) * LANES
    time_add = jnp.concatenate(
        [
            time_own[:, :, :shard_cols],
            gap,
            time_own[:, :, shard_cols:],
            gap[:, :, : kept - 3 * shard_cols],
        ],
        axis=2,
    )

    attn_full = gather_shards(wire_attn).reshape(groups, width, width)
    up_full = gather_shards(up_weight).reshape(groups, width, width)
    down_full = unpack_down(gather_shards(wire_down))

    bias = position_bias(offset_index, table)

    x_rows = images.reshape(rows, width).astype(wide)
    normed, unit_one, inv_one = normalize(x_rows, gain_one, shift_one)
    normed_low = normed.astype(low)
    qkv, probs, mixed_split = attend(normed_low, attn_full, time_add, bias, count, tokens)
    proj_full = take_proj(attn_full)
    mixed = mixed_split.transpose(1, 0, 2).reshape(rows, width)
    hidden = x_rows + (matmul(mixed, proj_full) + proj_b)
    second, unit_two, inv_two = normalize(hidden, gain_two, shift_two)
    second_low = second.astype(low)
    grad_low = cotangent.reshape(rows, width)
    grad_rows = grad_low.astype(wide)
    result = hidden + down_b
    d_second = jnp.zeros((rows, width), wide)
    activ, d_pre = [], []
    for g in range(groups):
        pre_act = matmul(second_low, up_full[g]) + up_b[g]
        act = jax.nn.gelu(pre_act, approximate=False).astype(low)
        down_g = down_full[g * width : (g + 1) * width]
        result = result + matmul(act, down_g)
        d_g = (times_transposed(grad_low, down_g) * gelu_slope(pre_act)).astype(low)
        d_second = d_second + times_transposed(d_g, up_full[g])
        activ.append(act)
        d_pre.append(d_g)
    layer_out = result.astype(low).reshape(count, tokens, width)

    grad_down = jnp.concatenate([contract_rows(a, grad_low).astype(low) for a in activ], axis=0)
    grad_up = jnp.stack([contract_rows(second_low, d).astype(low) for d in d_pre])
    down_sum = scatter_sum(pack_down(grad_down, groups, parts, shard_rows))
    up_sum = scatter_sum(grad_up.reshape(groups, parts, shard_rows, width))

    d_hidden = grad_rows + norm_back(d_second, unit_two, inv_two, gain_two)
    d_hidden_low = d_hidden.astype(low)
    d_mixed = times_transposed(d_hidden_low, proj_full).astype(low)
    d_mixed_split = d_mixed.reshape(rows, groups, shard_cols).transpose(1, 0, 2)
    d_hidden_split = d_hidden_low.reshape(rows, groups, shard_cols).transpose(1, 0, 2)
    d_packed, pairs = attend_back(d_mixed_split, qkv, probs, d_hidden_split)
    attn_sum = scatter_sum(
        pair_grad(normed_low.T, mixed.T, d_packed).reshape(groups, parts, shard_rows, width)
    )

    d_time = jnp.sum(d_packed.reshape(groups, count, tokens, width).astype(wide), axis=2)
    d_time = jnp.concatenate(
        [d_time[:, :, :shard_cols], d_time[:, :, 2 * shard_cols : 3 * shard_cols]], axis=2
    ).astype(low)
    d_time_all = lax.all_gather(
        d_time.transpose(1, 0, 2).reshape(count, groups * 2 * shard_cols), BOTH, axis=0, tiled=True
    )
    d_time_cols = lax.dynamic_slice(
        d_time_all, (0, own_group * 2 * shard_cols), (all_images, 2 * shard_cols)
    )
    time_grads = contract_rows(time_cols, d_time_cols)
    tquery_grad = time_grads[:, :shard_cols]
    tvalue_grad = time_grads[:, shard_cols:]
    back = times_transposed(d_time_cols, time_weight)
    back = back.reshape(parts, groups, count, shard_rows).transpose(1, 0, 2, 3)
    back = lax.psum_scatter(back, "fsdp", scatter_dimension=0, tiled=False)
    back = lax.all_gather(back, "dp", axis=0, tiled=False)
    back = lax.dynamic_slice(
        back, (0, own_part, 0, 0), (parts, 1, count, shard_rows)
    ).reshape(parts, count, shard_rows)
    time_grad = back.transpose(1, 0, 2).reshape(count, width)

    lane = lax.broadcasted_iota(jnp.int32, (1, width), 1)
    d_normed = jnp.zeros((rows, width), wide)
    for g in range(groups):
        part = jnp.where(lane < 3 * shard_cols, d_packed[g], jnp.zeros((), low))
        d_normed = d_normed + times_transposed(part, attn_full[g])
    d_input = d_hidden + norm_back(d_normed, unit_one, inv_one, gain_one)
    images_grad = d_input.astype(low).reshape(count, tokens, width)

    table_sum = table_gradient(offset_index, pairs).reshape(heads, 8 * LANES)[:, :table_rows]

    def rows_sum(value):
        return jnp.sum(value, axis=0).reshape(groups, -1)

    vectors = [
        rows_sum(d_hidden_low.astype(wide)),
        rows_sum(d_normed * unit_one),
        rows_sum(d_normed),
        rows_sum(d_second * unit_two),
        rows_sum(d_second),
        rows_sum(grad_rows),
        jnp.stack([jnp.sum(d.astype(wide), axis=0) for d in d_pre]),
        table_sum.reshape(groups, group_heads * table_rows),
    ]
    flat = jnp.concatenate(vectors, axis=1)
    flat = jnp.pad(flat, ((0, 0), (0, -flat.shape[1] % 1024)))
    flat = lax.psum(flat, BOTH)
    own = lax.dynamic_slice(flat, (own_group, 0), (1, flat.shape[1]))[0]
    proj_bg, gain1_g, shift1_g, gain2_g, shift2_g, down_bg = (
        own[i * shard_cols : (i + 1) * shard_cols] for i in range(6)
    )
    at = 6 * shard_cols
    up_bg = own[at : at + up_bias.shape[0]]
    at = at + up_bias.shape[0]
    table_grad = own[at : at + group_heads * table_rows].reshape(group_heads, table_rows)

    attn_sum = attn_sum.astype(wide)
    query_grad, key_grad, value_grad, proj_grad = (
        attn_sum[:, i * shard_cols : (i + 1) * shard_cols] for i in range(4)
    )
    down_sum = down_sum.astype(wide)
    down_grad = jnp.concatenate(
        [down_sum[:, g * shard_cols : (g + 1) * shard_cols] for g in range(fold)], axis=0
    )
    return (
        layer_out,
        images_grad,
        time_grad,
        query_grad,
        key_grad,
        value_grad,
        tquery_grad,
        tvalue_grad,
        proj_grad,
        proj_bg,
        gain1_g,
        shift1_g,
        gain2_g,
        shift2_g,
        up_sum.astype(wide),
        down_grad,
        up_bg,
        down_bg,
        table_grad,
    )


def solution(mesh):
    rows = P(BOTH, None, None)
    matrix = P("dp", "fsdp")
    vector = P("fsdp")
    table = P("fsdp", None)
    return jax.shard_map(
        body,
        mesh=mesh,
        in_specs=(
            (rows, P(BOTH, None), P(BOTH), P())
            + (matrix,) * 6
            + (vector,) * 5
            + (matrix,) * 2
            + (vector,) * 2
            + (table, rows)
        ),
        out_specs=(
            (rows, rows, P(BOTH, None))
            + (matrix,) * 6
            + (vector,) * 5
            + (matrix,) * 2
            + (vector,) * 2
            + (table,)
        ),
        check_vma=False,
    )
```

```python
import math

import jax
import jax.numpy as jnp
import numpy as np
from jax import lax
from jax.experimental import pallas as pl
from jax.experimental.pallas import tpu as pltpu
from jax.sharding import PartitionSpec as P

LANES = 128
BOTH = ("dp", "fsdp")
VMEM_LIMIT = 58 * 1024 * 1024


def sinusoid(steps, model_width):
    half_width = model_width // 2
    frequency = jnp.exp(
        -math.log(10000.0) * jnp.arange(half_width).astype(jnp.float32) / half_width
    )
    angles = steps.astype(jnp.float32)[:, None] * frequency[None, :]
    return jnp.concatenate([jnp.sin(angles), jnp.cos(angles)], axis=1)


def matmul(left, right):
    return jnp.dot(left, right, preferred_element_type=jnp.float32)


def contract_rows(left, right):
    return lax.dot_general(
        left, right, (((0,), (0,)), ((), ())), preferred_element_type=jnp.float32
    )


def times_transposed(left, right):
    return lax.dot_general(
        left, right, (((1,), (1,)), ((), ())), preferred_element_type=jnp.float32
    )


def normalize(values, gain, shift):
    row_mean = jnp.mean(values, axis=-1, keepdims=True)
    centered = values - row_mean
    inv_std = lax.rsqrt(jnp.mean(centered * centered, axis=-1, keepdims=True) + 1e-06)
    unit_rows = centered * inv_std
    return (unit_rows * gain + shift, unit_rows, inv_std)


def norm_back(grad_rows, unit_rows, inv_std, gain):
    scaled = grad_rows * gain
    return inv_std * (
        scaled
        - jnp.mean(scaled, axis=-1, keepdims=True)
        - unit_rows * jnp.mean(scaled * unit_rows, axis=-1, keepdims=True)
    )


def gelu_slope(pre_act):
    return 0.5 * (1.0 + lax.erf(pre_act * (1.0 / math.sqrt(2.0)))) + pre_act * jnp.exp(
        -0.5 * pre_act * pre_act
    ) * (1.0 / math.sqrt(2.0 * math.pi))


def params(count=1):
    return pltpu.CompilerParams(
        dimension_semantics=("arbitrary",) * count, vmem_limit_bytes=VMEM_LIMIT
    )


def bias_kernel(index_ref, table_ref, bias_ref):
    heads, rows, tokens = bias_ref.shape
    table = table_ref[...]
    sub = lax.broadcasted_iota(jnp.int32, (8, tokens), 0)
    lane_of = lax.broadcasted_iota(jnp.int32, (LANES, tokens), 0)
    line = lax.broadcasted_iota(jnp.int32, (heads, heads * 8), 0)
    column = lax.broadcasted_iota(jnp.int32, (heads, heads * 8), 1)
    add_up = jnp.where(column >> 3 == line, 1.0, 0.0).astype(jnp.bfloat16)

    def one_row(row):
        index = index_ref[pl.ds(row, 1), :]
        low = jnp.broadcast_to(index & (LANES - 1), (LANES, tokens))
        hit = sub == jnp.broadcast_to(index >> 7, (8, tokens))
        picked = matmul(table, jnp.where(lane_of == low, 1.0, 0.0).astype(jnp.bfloat16))
        only = jnp.concatenate(
            [jnp.where(hit, picked[h * 8 : (h + 1) * 8], 0.0) for h in range(heads)], axis=0
        ).astype(jnp.bfloat16)
        found = matmul(add_up, only)
        for h in range(heads):
            bias_ref[h, pl.ds(row, 1), :] = found[h : h + 1]

    def some_rows(step, carry):
        for part in range(4):
            one_row(step * 4 + part)
        return carry

    lax.fori_loop(0, rows // 4, some_rows, 0)


def position_bias(index, table):
    heads, padded = table.shape
    tokens = index.shape[0]
    block = 64
    return pl.pallas_call(
        bias_kernel,
        grid=(tokens // block,),
        in_specs=[
            pl.BlockSpec((block, tokens), lambda i: (i, 0)),
            pl.BlockSpec((heads * 8, LANES), lambda i: (0, 0)),
        ],
        out_specs=pl.BlockSpec((heads, block, tokens), lambda i: (0, i, 0)),
        out_shape=jax.ShapeDtypeStruct((heads, tokens, tokens), jnp.float32),
        compiler_params=params(),
        name="position_bias",
    )(index, table.reshape(heads * 8, LANES))


def table_kernel(index_ref, pairs_ref, out_ref):
    heads = pairs_ref.shape[0]
    tokens = index_ref.shape[1]
    rows = index_ref.shape[0]

    @pl.when(pl.program_id(0) == 0)
    def _():
        out_ref[...] = jnp.zeros_like(out_ref)

    sub = lax.broadcasted_iota(jnp.int32, (8, tokens), 0)
    lane_of = lax.broadcasted_iota(jnp.int32, (LANES, tokens), 0)

    def one_row(row, total):
        index = index_ref[pl.ds(row, 1), :]
        low = jnp.broadcast_to(index & (LANES - 1), (LANES, tokens))
        high = jnp.broadcast_to(index >> 7, (8, tokens))
        hit = sub == high
        left = jnp.concatenate(
            [
                jnp.where(hit, jnp.broadcast_to(pairs_ref[h, pl.ds(row, 1), :], (8, tokens)), 0.0)
                for h in range(heads)
            ],
            axis=0,
        ).astype(jnp.bfloat16)
        right = jnp.where(lane_of == low, 1.0, 0.0).astype(jnp.bfloat16)
        return total + times_transposed(left, right)

    def two_rows(step, total):
        return one_row(step * 2 + 1, one_row(step * 2, total))

    out_ref[...] += lax.fori_loop(
        0, rows // 2, two_rows, jnp.zeros((heads * 8, LANES), jnp.float32)
    )


def table_gradient(index, pairs):
    heads, tokens, _ = pairs.shape
    block = 64
    return pl.pallas_call(
        table_kernel,
        grid=(tokens // block,),
        in_specs=[
            pl.BlockSpec((block, tokens), lambda i: (i, 0)),
            pl.BlockSpec((heads, block, tokens), lambda i: (0, i, 0)),
        ],
        out_specs=pl.BlockSpec((heads * 8, LANES), lambda i: (0, 0)),
        out_shape=jax.ShapeDtypeStruct((heads * 8, LANES), jnp.float32),
        compiler_params=params(),
        name="table_gradient",
    )(index, pairs)


def attend_kernel(normed_ref, weight_ref, add_ref, bias_ref, qkv_ref, probs_ref, mixed_ref):
    images, heads = probs_ref.shape[1], probs_ref.shape[2]
    tokens = probs_ref.shape[3]
    width = mixed_ref.shape[2]
    size = width // heads
    scale = 1.0 / math.sqrt(size)
    kept = qkv_ref.shape[2]
    for image in range(images):
        rows = slice(image * tokens, (image + 1) * tokens)
        acc = matmul(normed_ref[rows, :], weight_ref[0, :, :kept])
        qkv_ref[0, rows, :] = (acc + add_ref[0, image : image + 1, :]).astype(jnp.bfloat16)
    for image in range(images):
        rows = slice(image * tokens, (image + 1) * tokens)
        both = qkv_ref[0, rows, :]
        outs = []
        for head in range(heads):
            at = head * size
            query = both[:, at : at + size]
            keys = both[:, width + at : width + at + size]
            values = both[:, 2 * width + at : 2 * width + at + size]
            scores = times_transposed(query, keys) * scale + bias_ref[head]
            peak = jnp.max(scores, axis=-1, keepdims=True)
            expo = jnp.exp(scores - peak)
            total = jnp.sum(expo, axis=-1, keepdims=True)
            probs = (expo / total).astype(jnp.bfloat16)
            probs_ref[0, image, head] = probs
            outs.append(matmul(probs, values))
        mixed_ref[0, rows, :] = jnp.concatenate(outs, axis=1).astype(jnp.bfloat16)


def attend(normed, weight, add, bias, images, tokens):
    groups, depth, packed = weight.shape
    heads = bias.shape[0] // groups
    width = packed // groups
    kept = add.shape[2]
    rows = images * tokens
    return pl.pallas_call(
        attend_kernel,
        grid=(groups,),
        in_specs=[
            pl.BlockSpec((rows, depth), lambda f: (0, 0)),
            pl.BlockSpec((1, depth, packed), lambda f: (f, 0, 0)),
            pl.BlockSpec((1, images, kept), lambda f: (f, 0, 0)),
            pl.BlockSpec((heads, tokens, tokens), lambda f: (f, 0, 0)),
        ],
        out_specs=[
            pl.BlockSpec((1, rows, kept), lambda f: (f, 0, 0)),
            pl.BlockSpec((1, images, heads, tokens, tokens), lambda f: (f, 0, 0, 0, 0)),
            pl.BlockSpec((1, rows, width), lambda f: (f, 0, 0)),
        ],
        out_shape=[
            jax.ShapeDtypeStruct((groups, rows, kept), jnp.bfloat16),
            jax.ShapeDtypeStruct((groups, images, heads, tokens, tokens), jnp.bfloat16),
            jax.ShapeDtypeStruct((groups, rows, width), jnp.bfloat16),
        ],
        compiler_params=params(),
        name="attend",
    )(normed, weight, add, bias)


def attend_back_kernel(grad_ref, qkv_ref, probs_ref, hidden_ref, out_ref, pairs_ref):
    images, heads = probs_ref.shape[1], probs_ref.shape[2]
    tokens = probs_ref.shape[3]
    width = grad_ref.shape[2]
    size = width // heads
    scale = 1.0 / math.sqrt(size)
    for image in range(images):
        rows = slice(image * tokens, (image + 1) * tokens)
        both = qkv_ref[0, rows, :]
        grads = grad_ref[0, rows, :]
        d_query, d_keys, d_values = [], [], []
        for head in range(heads):
            at = head * size
            query = both[:, at : at + size]
            keys = both[:, width + at : width + at + size]
            values = both[:, 2 * width + at : 2 * width + at + size]
            grad = grads[:, at : at + size]
            probs_low = probs_ref[0, image, head]
            probs = probs_low.astype(jnp.float32)
            d_values.append(contract_rows(probs_low, grad))
            d_probs = times_transposed(grad, values)
            moved = probs * d_probs
            d_scores = moved - probs * jnp.sum(moved, axis=-1, keepdims=True)
            d_low = d_scores.astype(jnp.bfloat16)
            if image == 0:
                pairs_ref[head] = d_low.astype(jnp.float32)
            else:
                pairs_ref[head] += d_low.astype(jnp.float32)
            d_query.append(matmul(d_low, keys) * scale)
            d_keys.append(contract_rows(d_low, query) * scale)
        out_ref[0, rows, :] = jnp.concatenate(
            d_query + d_keys + d_values + [hidden_ref[0, rows, :].astype(jnp.float32)], axis=1
        ).astype(jnp.bfloat16)


def attend_back(grad, qkv, probs, hidden):
    groups, rows, width = grad.shape
    kept = qkv.shape[2]
    _, images, heads, tokens, _ = probs.shape
    packed = 4 * width
    return pl.pallas_call(
        attend_back_kernel,
        grid=(groups,),
        in_specs=[
            pl.BlockSpec((1, rows, width), lambda f: (f, 0, 0)),
            pl.BlockSpec((1, rows, kept), lambda f: (f, 0, 0)),
            pl.BlockSpec((1, images, heads, tokens, tokens), lambda f: (f, 0, 0, 0, 0)),
            pl.BlockSpec((1, rows, width), lambda f: (f, 0, 0)),
        ],
        out_specs=[
            pl.BlockSpec((1, rows, packed), lambda f: (f, 0, 0)),
            pl.BlockSpec((heads, tokens, tokens), lambda f: (f, 0, 0)),
        ],
        out_shape=[
            jax.ShapeDtypeStruct((groups, rows, packed), jnp.bfloat16),
            jax.ShapeDtypeStruct((groups * heads, tokens, tokens), jnp.float32),
        ],
        compiler_params=params(),
        name="attend_back",
    )(grad, qkv, probs, hidden)


def store_slot(slot, own_ref, send_ref, at, value):
    half = own_ref.shape[0]

    @pl.when(slot < half)
    def _():
        own_ref[(slot,) + at] = value

    @pl.when(slot >= half)
    def _():
        send_ref[(slot - half,) + at] = value


def pair_grad_kernel(slot_ref, one_ref, two_ref, right_ref, own_ref, send_ref):
    cut = 3 * (right_ref.shape[2] // 4)
    below = cut // LANES * LANES
    above = below + LANES
    rows = own_ref.shape[2]
    right = right_ref[0]
    lane = lax.broadcasted_iota(jnp.int32, (rows, LANES), 1)
    first = matmul(one_ref[...], right[:, :above])
    last = matmul(two_ref[...], right[:, below:])
    for part in range(2 * own_ref.shape[0]):
        at = slice(part * rows, (part + 1) * rows)
        value = jnp.concatenate(
            [
                first[at, :below],
                jnp.where(lane < cut - below, first[at, below:], last[at, :LANES]),
                last[at, LANES:],
            ],
            axis=1,
        ).astype(jnp.bfloat16)
        store_slot(slot_ref[part], own_ref, send_ref, (0,), value)


def one_grad_kernel(slot_ref, one_ref, right_ref, own_ref, send_ref):
    rows = own_ref.shape[2]
    first = matmul(one_ref[...], right_ref[0])
    for part in range(2 * own_ref.shape[0]):
        value = first[part * rows : (part + 1) * rows].astype(jnp.bfloat16)
        store_slot(slot_ref[part], own_ref, send_ref, (0,), value)


def slot_grad(kernel, slots, lefts, right, parts, name):
    groups, rows, packed = right.shape
    depth = lefts[0].shape[0]
    half = jax.ShapeDtypeStruct((parts // 2, groups, depth // parts, packed), jnp.bfloat16)
    out = pl.BlockSpec((parts // 2, 1, depth // parts, packed), lambda f, s: (0, f, 0, 0))
    return pl.pallas_call(
        kernel,
        grid_spec=pltpu.PrefetchScalarGridSpec(
            num_scalar_prefetch=1,
            grid=(groups,),
            in_specs=[pl.BlockSpec((depth, rows), lambda f, s: (0, 0)) for _ in lefts]
            + [pl.BlockSpec((1, rows, packed), lambda f, s: (f, 0, 0))],
            out_specs=[out, out],
        ),
        out_shape=[half, half],
        compiler_params=params(),
        name=name,
    )(slots, *lefts, right)


def down_grad_kernel(slot_ref, left_ref, right_ref, own_ref, send_ref):
    half, groups, rows, packed = own_ref.shape
    width = packed // groups
    value = matmul(left_ref[...], right_ref[...]).astype(jnp.bfloat16)
    slot = slot_ref[pl.program_id(0)]
    for f in range(groups):
        block = jnp.concatenate(
            [
                value[g * rows : (g + 1) * rows, f * width : (f + 1) * width]
                for g in range(value.shape[0] // rows)
            ],
            axis=1,
        )
        store_slot(slot, own_ref, send_ref, (f,), block)


def down_slot_grad(slots, left, right, groups, parts, rows):
    hidden, tokens = left.shape
    packed = right.shape[1]
    half = jax.ShapeDtypeStruct((parts // 2, groups, rows, packed), jnp.bfloat16)
    out = pl.BlockSpec((parts // 2, groups, rows, packed), lambda d, s: (0, 0, 0, 0))
    return pl.pallas_call(
        down_grad_kernel,
        grid_spec=pltpu.PrefetchScalarGridSpec(
            num_scalar_prefetch=1,
            grid=(parts,),
            in_specs=[
                pl.BlockSpec((hidden // parts, tokens), lambda d, s: (d, 0)),
                pl.BlockSpec((tokens, packed), lambda d, s: (0, 0)),
            ],
            out_specs=[out, out],
        ),
        out_shape=[half, half],
        compiler_params=params(),
        name="down_grad",
    )(slots, left, right)


def add_kernel(one_ref, two_ref, three_ref, four_ref, came_ref, *outs):
    for k, (mine, out) in enumerate(zip((one_ref, two_ref, three_ref, four_ref), outs)):
        total = mine[0, 0].astype(jnp.float32) + came_ref[k, 0].astype(jnp.float32)
        out[0] = total.astype(jnp.bfloat16)


def add_halves(own, came):
    half, groups, rows, packed = own.shape
    return pl.pallas_call(
        add_kernel,
        grid=(groups,),
        in_specs=[
            pl.BlockSpec((1, 1, rows, packed), lambda f, k=k: (k, f, 0, 0)) for k in range(half)
        ]
        + [pl.BlockSpec((half, 1, rows, packed), lambda f: (0, f, 0, 0))],
        out_specs=[pl.BlockSpec((1, rows, packed), lambda f: (f, 0, 0))] * half,
        out_shape=[jax.ShapeDtypeStruct((groups, rows, packed), jnp.bfloat16)] * half,
        compiler_params=params(),
        name="add_halves",
    )(*([own] * half), came)


def place_kernel(part_ref, *refs):
    *pieces, out_ref, sems = refs
    copies = [
        pltpu.make_async_copy(piece, out_ref.at[:, part_ref[j]], sems.at[j])
        for j, piece in enumerate(pieces)
    ]
    for copy in copies:
        copy.start()
    for copy in copies:
        copy.wait()


def place_pieces(part_of, pieces):
    groups, rows, width = pieces[0].shape
    parts = len(pieces)
    return pl.pallas_call(
        place_kernel,
        grid_spec=pltpu.PrefetchScalarGridSpec(
            num_scalar_prefetch=1,
            grid=(1,),
            in_specs=[pl.BlockSpec(memory_space=pl.ANY)] * parts,
            out_specs=pl.BlockSpec(memory_space=pl.ANY),
            scratch_shapes=[pltpu.SemaphoreType.DMA((parts,))],
        ),
        out_shape=jax.ShapeDtypeStruct((groups, parts, rows, width), pieces[0].dtype),
        compiler_params=params(),
        name="place_pieces",
    )(part_of, *pieces)


def unpack_kernel(part_ref, *refs):
    *pieces, out_ref, held, sems = refs
    step = pl.program_id(0)
    _, groups, rows, packed = held.shape
    width = packed // groups

    @pl.when(step == 0)
    def _():
        for j, piece in enumerate(pieces):
            pltpu.make_async_copy(piece, held.at[j], sems.at[j]).start()

    pltpu.make_async_copy(pieces[0], held.at[step], sems.at[step]).wait()
    for g in range(out_ref.shape[0] // rows):
        out_ref[g * rows : (g + 1) * rows, :] = jnp.concatenate(
            [held[step, f][:, g * width : (g + 1) * width] for f in range(groups)], axis=1
        )


def unpack_pieces(part_of, pieces, fold):
    groups, rows, width = pieces[0].shape
    parts = len(pieces)
    return pl.pallas_call(
        unpack_kernel,
        grid_spec=pltpu.PrefetchScalarGridSpec(
            num_scalar_prefetch=1,
            grid=(parts,),
            in_specs=[pl.BlockSpec(memory_space=pl.ANY)] * parts,
            out_specs=pl.BlockSpec((fold * rows, width), lambda j, p: (p[j], 0)),
            scratch_shapes=[
                pltpu.VMEM((parts, groups, rows, width), pieces[0].dtype),
                pltpu.SemaphoreType.DMA((parts,)),
            ],
        ),
        out_shape=jax.ShapeDtypeStruct((parts * fold * rows, width), pieces[0].dtype),
        compiler_params=params(),
        name="unpack_pieces",
    )(part_of, *pieces)


def take_proj_kernel(in_ref, out_ref):
    groups = in_ref.shape[0]
    width = out_ref.shape[1] // groups
    skip = in_ref.shape[2] - width
    for f in range(groups):
        out_ref[:, f * width : (f + 1) * width] = in_ref[f][:, skip:]


def take_proj(packed):
    groups, depth, width = packed.shape
    block = 288
    tail = width // 3
    return pl.pallas_call(
        take_proj_kernel,
        grid=(depth // block,),
        in_specs=[pl.BlockSpec((groups, block, tail), lambda d: (0, d, 2))],
        out_specs=pl.BlockSpec((block, width), lambda d: (d, 0)),
        out_shape=jax.ShapeDtypeStruct((depth, width), packed.dtype),
        compiler_params=params(),
        name="take_proj",
    )(packed)


NEAR = ((0, 2, 4, 6), (0, 4, 2, 6))


def is_cube():
    return lax.axis_size("dp") == 8 and lax.axis_size("fsdp") == 4


def part_tables():
    part_of = np.zeros((8, 8), np.int32)
    slot_of = np.zeros((8, 8), np.int32)
    for part in range(8):
        core = part & 1
        order = [part ^ m for m in NEAR[core]] + [part ^ 1 ^ m for m in NEAR[1 - core]]
        part_of[part] = order
        for slot, other in enumerate(order):
            slot_of[part, other] = slot
    own = lax.axis_index("dp")
    pick = lambda table: lax.dynamic_slice(jnp.asarray(table), (own, 0), (1, 8))[0]
    return pick(part_of), pick(slot_of)


def swap(value, hop):
    return lax.ppermute(value, "dp", [(i, i ^ NEAR[i & 1][hop]) for i in range(8)])


def swap_core(value):
    return lax.ppermute(value, "dp", [(i, i ^ 1) for i in range(8)])


def after(value, *others):
    return lax.optimization_barrier((value, *others))[0]


class Gather:
    def __init__(self, shard, behind=None, ready=None):
        if behind is not None:
            shard = after(shard, behind.own)
        own = lax.all_gather(shard, "fsdp", axis=0, tiled=False)
        if behind is not None:
            own = after(own, behind.first)
        if ready is not None:
            own = after(own, ready)
        self.own = own
        self.first = swap(own, 1)
        second = swap(own, 2)
        third = swap(self.first, 2)
        near = [own, self.first, second, third]
        self.pieces = near + [swap_core(piece) for piece in near]


class Scatter:
    def __init__(self, own, send):
        self.own = own
        self.came = swap_core(send)

    def near(self):
        self.zero, self.one, two, three = add_halves(self.own, self.came)
        self.far = swap(three, 2)
        self.side = swap(two, 2)
        return three

    def back(self):
        one = self.one.astype(jnp.float32) + self.far.astype(jnp.float32)
        one = one.astype(jnp.bfloat16)
        self.last = swap(one, 1)
        return one

    def total(self):
        total = self.zero.astype(jnp.float32) + self.side.astype(jnp.float32)
        self.sum = (total + self.last.astype(jnp.float32)).astype(jnp.bfloat16)
        return self.sum

    def end(self):
        return lax.psum_scatter(self.sum, "fsdp", scatter_dimension=0, tiled=False)


def swap_bit(value, axis, bit):
    size = lax.axis_size(axis)
    return lax.ppermute(value, axis, [(i, i ^ (1 << bit)) for i in range(size)])


def bit_of(axis, bit):
    return (lax.axis_index(axis) >> bit) & 1 == 1


def small_gather(value, axis):
    if not is_cube():
        return lax.all_gather(value, axis, axis=0, tiled=True)
    for bit in range(lax.axis_size(axis).bit_length() - 1):
        other = swap_bit(value, axis, bit)
        value = jnp.where(
            bit_of(axis, bit),
            jnp.concatenate([other, value], axis=0),
            jnp.concatenate([value, other], axis=0),
        )
    return value


def small_scatter(value, axis):
    if not is_cube():
        return lax.psum_scatter(value, axis, scatter_dimension=0, tiled=True)
    for bit in reversed(range(lax.axis_size(axis).bit_length() - 1)):
        half = value.shape[0] // 2
        high = bit_of(axis, bit)
        keep = jnp.where(high, value[half:], value[:half])
        value = keep + swap_bit(jnp.where(high, value[:half], value[half:]), axis, bit)
    return value


def small_sum(value, axis):
    if not is_cube():
        return lax.psum(value, axis)
    for bit in range(lax.axis_size(axis).bit_length() - 1):
        value = value + swap_bit(value, axis, bit)
    return value


def gather_shards(shard):
    rows, width = shard.shape
    groups, parts = lax.axis_size("fsdp"), lax.axis_size("dp")
    full = lax.all_gather(shard, ("fsdp", "dp"), axis=0, tiled=True)
    return full.reshape(groups, parts, rows, width)


def scatter_sum(terms):
    groups, parts, rows, width = terms.shape
    return lax.psum_scatter(
        terms.reshape(groups * parts * rows, width),
        ("fsdp", "dp"),
        scatter_dimension=0,
        tiled=True,
    )


def pack_down(natural, groups, parts, rows):
    total, width = natural.shape
    split = natural.reshape(parts, total // (parts * rows), rows, groups, width // groups)
    return split.transpose(3, 0, 2, 1, 4).reshape(groups, parts, rows, width)


def unpack_down(packed, fold):
    groups, parts, rows, width = packed.shape
    split = packed.reshape(groups, parts, rows, fold, width // fold)
    return split.transpose(1, 3, 2, 0, 4).reshape(parts * fold * rows, width)


def body(
    images,
    time_vector,
    timesteps,
    offset_index,
    query_weight,
    key_weight,
    value_weight,
    tquery_weight,
    tvalue_weight,
    proj_weight,
    proj_bias,
    first_gain,
    first_shift,
    second_gain,
    second_shift,
    up_weight,
    down_weight,
    up_bias,
    down_bias,
    bias_table,
    cotangent,
):
    low = jnp.bfloat16
    wide = jnp.float32
    count, tokens, width = images.shape
    rows = count * tokens
    groups, parts = lax.axis_size("fsdp"), lax.axis_size("dp")
    shard_rows, shard_cols = query_weight.shape
    group_heads, table_rows = bias_table.shape
    heads = group_heads * groups
    fold = down_weight.shape[0] // shard_rows
    own_part = lax.axis_index("dp")
    own_group = lax.axis_index("fsdp")

    wire_attn = jnp.concatenate([query_weight, key_weight, value_weight, proj_weight], axis=1)
    wire_down = jnp.concatenate(
        [down_weight[g * shard_rows : (g + 1) * shard_rows] for g in range(fold)], axis=1
    )
    small = jnp.concatenate(
        [
            proj_bias,
            first_gain,
            first_shift,
            second_gain,
            second_shift,
            down_bias,
            up_bias,
            bias_table.reshape(-1),
        ]
    )
    small = jnp.pad(small, (0, -small.shape[0] % 1024))
    small_all = small_gather(small.reshape(1, -1, LANES), "fsdp").reshape(groups, -1)

    def vector_of(slot):
        return small_all[:, slot * shard_cols : (slot + 1) * shard_cols].reshape(-1).astype(wide)

    proj_b, gain_one, shift_one, gain_two, shift_two, down_b = (vector_of(i) for i in range(6))
    at = 6 * shard_cols
    up_b = small_all[:, at : at + up_bias.shape[0]].astype(wide)
    at = at + up_bias.shape[0]
    table = small_all[:, at : at + group_heads * table_rows].reshape(heads, table_rows)
    table = jnp.pad(table, ((0, 0), (0, 8 * LANES - table_rows)))
    bias = position_bias(offset_index, table)

    time_low = (time_vector.astype(wide) + sinusoid(timesteps, width)).astype(low)
    time_all = small_gather(small_gather(time_low, "fsdp"), "dp")
    all_images = time_all.shape[0]
    time_cols = lax.dynamic_slice(
        time_all, (0, own_part * shard_rows), (all_images, shard_rows)
    )
    time_weight = jnp.concatenate([tquery_weight, tvalue_weight], axis=1)
    time_sum = small_scatter(matmul(time_cols, time_weight), "dp")
    time_part = small_gather(time_sum[None], "fsdp")
    time_own = lax.dynamic_slice(
        time_part, (0, own_group * count, 0), (groups, count, 2 * shard_cols)
    )
    gap = jnp.zeros((groups, count, shard_cols), wide)
    kept = -(-3 * shard_cols // LANES) * LANES
    time_add = jnp.concatenate(
        [
            time_own[:, :, :shard_cols],
            gap,
            time_own[:, :, shard_cols:],
            gap[:, :, : kept - 3 * shard_cols],
        ],
        axis=2,
    )

    if is_cube():
        part_of, slot_of = part_tables()
        attn_move = Gather(wire_attn, ready=bias)
        up_move = Gather(up_weight, behind=attn_move)
        down_move = Gather(wire_down, behind=up_move)
        attn_full = place_pieces(part_of, attn_move.pieces)
        up_full = place_pieces(part_of, up_move.pieces)
        down_full = unpack_pieces(part_of, down_move.pieces, fold)
    else:
        attn_full = gather_shards(wire_attn)
        up_full = gather_shards(up_weight)
        down_full = unpack_down(gather_shards(wire_down), fold)
    attn_full = attn_full.reshape(groups, width, width)
    up_full = up_full.reshape(groups, width, width)

    x_rows = images.reshape(rows, width).astype(wide)
    normed, unit_one, inv_one = normalize(x_rows, gain_one, shift_one)
    normed_low = normed.astype(low)
    qkv, probs, mixed_split = attend(normed_low, attn_full, time_add, bias, count, tokens)
    proj_full = take_proj(attn_full)
    mixed = mixed_split.transpose(1, 0, 2).reshape(rows, width)
    hidden = x_rows + (matmul(mixed, proj_full) + proj_b)
    second, unit_two, inv_two = normalize(hidden, gain_two, shift_two)
    second_low = second.astype(low)
    grad_low = cotangent.reshape(rows, width)
    grad_rows = grad_low.astype(wide)
    cube = is_cube()
    wire = (groups, parts, shard_rows, width)
    pre = [matmul(second_low, up_full[g]) + up_b[g] for g in range(groups)]
    activ = [jax.nn.gelu(p, approximate=False).astype(low) for p in pre]
    grad_cols = grad_low
    if cube:
        activ_t = jnp.concatenate([a.T for a in activ], axis=0)
        own, send = down_slot_grad(slot_of, activ_t, grad_low, groups, parts, shard_rows)
        down_move = Scatter(own, send)
        grad_cols = after(grad_low, send)
    result = hidden + down_b
    d_second = jnp.zeros((rows, width), wide)
    d_pre = []
    for g in range(groups):
        down_g = down_full[g * width : (g + 1) * width]
        d_g = (times_transposed(grad_cols, down_g) * gelu_slope(pre[g])).astype(low)
        d_second = d_second + times_transposed(d_g, up_full[g])
        d_pre.append(d_g)
    second_t = second_low.T
    if cube:
        second_t = after(second_t, down_move.near())
        own, send = slot_grad(
            one_grad_kernel, slot_of, [second_t], jnp.stack(d_pre), parts, "up_grad"
        )
        up_move = Scatter(own, send)
        d_second = after(d_second, send)
    else:
        grad_down = jnp.concatenate([contract_rows(a, grad_low) for a in activ], axis=0)
        down_sum = scatter_sum(pack_down(grad_down.astype(low), groups, parts, shard_rows))
        grad_up = jnp.stack([contract_rows(second_low, d).astype(low) for d in d_pre])
        up_sum = scatter_sum(grad_up.reshape(wire))
    for g in range(groups):
        down_g = down_full[g * width : (g + 1) * width]
        result = result + matmul(activ[g], down_g)
    layer_out = result.astype(low).reshape(count, tokens, width)

    d_hidden = grad_rows + norm_back(d_second, unit_two, inv_two, gain_two)
    d_hidden_low = d_hidden.astype(low)
    d_hidden_cols = after(d_hidden_low, down_move.back()) if cube else d_hidden_low
    d_mixed = times_transposed(d_hidden_cols, proj_full).astype(low)
    d_mixed_split = d_mixed.reshape(rows, groups, shard_cols).transpose(1, 0, 2)
    d_hidden_split = d_hidden_low.reshape(rows, groups, shard_cols).transpose(1, 0, 2)
    if cube:
        d_mixed_split = after(d_mixed_split, up_move.near())
    d_packed, pairs = attend_back(d_mixed_split, qkv, probs, d_hidden_split)
    attn_back = attn_full
    if cube:
        normed_t = after(normed_low.T, up_move.back())
        own, send = slot_grad(
            pair_grad_kernel, slot_of, [normed_t, mixed.T], d_packed, parts, "pair_grad"
        )
        attn_move = Scatter(own, send)
        attn_back = after(attn_full, send)
        pairs = after(pairs, attn_move.near(), down_move.total())
    else:
        cut = 3 * shard_cols
        grad_attn = jnp.stack(
            [
                jnp.concatenate(
                    [contract_rows(normed_low, d[:, :cut]), contract_rows(mixed, d[:, cut:])],
                    axis=1,
                )
                for d in d_packed
            ]
        )
        attn_sum = scatter_sum(grad_attn.astype(low).reshape(wire))

    d_time = jnp.sum(d_packed.reshape(groups, count, tokens, width).astype(wide), axis=2)
    d_time = jnp.concatenate(
        [d_time[:, :, :shard_cols], d_time[:, :, 2 * shard_cols : 3 * shard_cols]], axis=2
    ).astype(low)
    d_time = d_time.transpose(1, 0, 2).reshape(count, groups * 2 * shard_cols)
    d_time_all = small_gather(small_gather(d_time, "fsdp"), "dp")
    d_time_cols = lax.dynamic_slice(
        d_time_all, (0, own_group * 2 * shard_cols), (all_images, 2 * shard_cols)
    )
    time_grads = contract_rows(time_cols, d_time_cols)
    tquery_grad = time_grads[:, :shard_cols]
    tvalue_grad = time_grads[:, shard_cols:]
    back = times_transposed(d_time_cols, time_weight)
    back = back.reshape(parts, groups, count, shard_rows).transpose(1, 0, 2, 3)
    back = small_gather(small_scatter(back, "fsdp"), "dp")
    back = lax.dynamic_slice(
        back, (0, own_part, 0, 0), (parts, 1, count, shard_rows)
    ).reshape(parts, count, shard_rows)
    time_grad = back.transpose(1, 0, 2).reshape(count, width)

    lane = lax.broadcasted_iota(jnp.int32, (1, width), 1)
    d_normed = jnp.zeros((rows, width), wide)
    for g in range(groups):
        part = jnp.where(lane < 3 * shard_cols, d_packed[g], jnp.zeros((), low))
        d_normed = d_normed + times_transposed(part, attn_back[g])
    d_input = d_hidden + norm_back(d_normed, unit_one, inv_one, gain_one)
    images_grad = d_input.astype(low).reshape(count, tokens, width)

    table_sum = table_gradient(offset_index, pairs).reshape(heads, 8 * LANES)[:, :table_rows]

    def rows_sum(value):
        return jnp.sum(value, axis=0).reshape(groups, -1)

    vectors = [
        rows_sum(d_hidden_low.astype(wide)),
        rows_sum(d_normed * unit_one),
        rows_sum(d_normed),
        rows_sum(d_second * unit_two),
        rows_sum(d_second),
        rows_sum(grad_rows),
        jnp.stack([jnp.sum(d.astype(wide), axis=0) for d in d_pre]),
        table_sum.reshape(groups, group_heads * table_rows),
    ]
    flat = jnp.concatenate(vectors, axis=1)
    flat = jnp.pad(flat, ((0, 0), (0, -flat.shape[1] % 1024)))
    own = small_sum(small_scatter(flat.reshape(groups, -1, LANES), "fsdp"), "dp").reshape(-1)
    proj_bg, gain1_g, shift1_g, gain2_g, shift2_g, down_bg = (
        own[i * shard_cols : (i + 1) * shard_cols] for i in range(6)
    )
    at = 6 * shard_cols
    up_bg = own[at : at + up_bias.shape[0]]
    at = at + up_bias.shape[0]
    table_grad = own[at : at + group_heads * table_rows].reshape(group_heads, table_rows)

    if cube:
        down_sum = down_move.end()
        attn_move.back()
        up_move.total()
        up_sum = up_move.end()
        attn_move.total()
        attn_sum = attn_move.end()
    attn_sum = attn_sum.astype(wide)
    query_grad, key_grad, value_grad, proj_grad = (
        attn_sum[:, i * shard_cols : (i + 1) * shard_cols] for i in range(4)
    )
    down_sum = down_sum.astype(wide)
    down_grad = jnp.concatenate(
        [down_sum[:, g * shard_cols : (g + 1) * shard_cols] for g in range(fold)], axis=0
    )
    return (
        layer_out,
        images_grad,
        time_grad,
        query_grad,
        key_grad,
        value_grad,
        tquery_grad,
        tvalue_grad,
        proj_grad,
        proj_bg,
        gain1_g,
        shift1_g,
        gain2_g,
        shift2_g,
        up_sum.astype(wide),
        down_grad,
        up_bg,
        down_bg,
        table_grad,
    )


def solution(mesh):
    rows = P(BOTH, None, None)
    matrix = P("dp", "fsdp")
    vector = P("fsdp")
    table = P("fsdp", None)
    return jax.shard_map(
        body,
        mesh=mesh,
        in_specs=(
            (rows, P(BOTH, None), P(BOTH), P())
            + (matrix,) * 6
            + (vector,) * 5
            + (matrix,) * 2
            + (vector,) * 2
            + (table, rows)
        ),
        out_specs=(
            (rows, rows, P(BOTH, None))
            + (matrix,) * 6
            + (vector,) * 5
            + (matrix,) * 2
            + (vector,) * 2
            + (table,)
        ),
        check_vma=False,
    )
```

```python
import math

import jax
import jax.numpy as jnp
import numpy as np
from jax import lax
from jax.experimental import pallas as pl
from jax.experimental.pallas import tpu as pltpu
from jax.sharding import PartitionSpec as P

LANES = 128
BOTH = ("dp", "fsdp")
VMEM_LIMIT = 58 * 1024 * 1024
SHORT = pl.CostEstimate(flops=1, transcendentals=0, bytes_accessed=1)


def sinusoid(steps, model_width):
    half_width = model_width // 2
    frequency = jnp.exp(
        -math.log(10000.0) * jnp.arange(half_width).astype(jnp.float32) / half_width
    )
    angles = steps.astype(jnp.float32)[:, None] * frequency[None, :]
    return jnp.concatenate([jnp.sin(angles), jnp.cos(angles)], axis=1)


def matmul(left, right):
    return jnp.dot(left, right, preferred_element_type=jnp.float32)


def contract_rows(left, right):
    return lax.dot_general(
        left, right, (((0,), (0,)), ((), ())), preferred_element_type=jnp.float32
    )


def times_transposed(left, right):
    return lax.dot_general(
        left, right, (((1,), (1,)), ((), ())), preferred_element_type=jnp.float32
    )


def normalize(values, gain, shift):
    row_mean = jnp.mean(values, axis=-1, keepdims=True)
    centered = values - row_mean
    inv_std = lax.rsqrt(jnp.mean(centered * centered, axis=-1, keepdims=True) + 1e-06)
    unit_rows = centered * inv_std
    return (unit_rows * gain + shift, unit_rows, inv_std)


def norm_back(grad_rows, unit_rows, inv_std, gain):
    scaled = grad_rows * gain
    return inv_std * (
        scaled
        - jnp.mean(scaled, axis=-1, keepdims=True)
        - unit_rows * jnp.mean(scaled * unit_rows, axis=-1, keepdims=True)
    )


def gelu_slope(pre_act):
    return 0.5 * (1.0 + lax.erf(pre_act * (1.0 / math.sqrt(2.0)))) + pre_act * jnp.exp(
        -0.5 * pre_act * pre_act
    ) * (1.0 / math.sqrt(2.0 * math.pi))


def params(count=1):
    return pltpu.CompilerParams(
        dimension_semantics=("arbitrary",) * count, vmem_limit_bytes=VMEM_LIMIT
    )


def bias_kernel(index_ref, table_ref, bias_ref):
    heads, rows, tokens = bias_ref.shape
    chunks = table_ref.shape[2] // LANES
    pieces = [
        [
            jnp.broadcast_to(table_ref[h, :, c * LANES : (c + 1) * LANES], (8, LANES))
            for c in range(chunks)
        ]
        for h in range(heads)
    ]

    def some_rows(step, carry):
        at = pl.multiple_of(step * 8, 8)
        for col in range(tokens // LANES):
            lanes = slice(col * LANES, (col + 1) * LANES)
            index = index_ref[pl.ds(at, 8), lanes]
            low = index & (LANES - 1)
            high = index >> 7
            hits = [high == c for c in range(chunks)]
            for h in range(heads):
                found = jnp.take_along_axis(pieces[h][0], low, axis=1)
                for c in range(1, chunks):
                    found = jnp.where(
                        hits[c], jnp.take_along_axis(pieces[h][c], low, axis=1), found
                    )
                bias_ref[h, pl.ds(at, 8), lanes] = found
        return carry

    lax.fori_loop(0, rows // 8, some_rows, 0)


def position_bias(index, table):
    heads, padded = table.shape
    tokens = index.shape[0]
    group = heads // 4
    return pl.pallas_call(
        bias_kernel,
        grid=(4,),
        in_specs=[
            pl.BlockSpec((tokens, tokens), lambda f: (0, 0)),
            pl.BlockSpec((group, 1, padded), lambda f: (f, 0, 0)),
        ],
        out_specs=pl.BlockSpec((group, tokens, tokens), lambda f: (f, 0, 0)),
        out_shape=jax.ShapeDtypeStruct((heads, tokens, tokens), jnp.float32),
        compiler_params=params(),
        cost_estimate=SHORT,
        name="position_bias",
    )(index, table.astype(jnp.float32).reshape(heads, 1, padded))


def table_kernel(index_ref, pairs_ref, out_ref):
    heads = pairs_ref.shape[0]
    tokens = index_ref.shape[1]
    rows = index_ref.shape[0]

    @pl.when(pl.program_id(0) == 0)
    def _():
        out_ref[...] = jnp.zeros_like(out_ref)

    sub = lax.broadcasted_iota(jnp.int32, (8, tokens), 0)
    lane_of = lax.broadcasted_iota(jnp.int32, (LANES, tokens), 0)

    def one_row(row, total):
        index = index_ref[pl.ds(row, 1), :]
        low = jnp.broadcast_to(index & (LANES - 1), (LANES, tokens))
        high = jnp.broadcast_to(index >> 7, (8, tokens))
        hit = sub == high
        left = jnp.concatenate(
            [
                jnp.where(hit, jnp.broadcast_to(pairs_ref[h, pl.ds(row, 1), :], (8, tokens)), 0.0)
                for h in range(heads)
            ],
            axis=0,
        ).astype(jnp.bfloat16)
        right = jnp.where(lane_of == low, 1.0, 0.0).astype(jnp.bfloat16)
        return total + times_transposed(left, right)

    def two_rows(step, total):
        return one_row(step * 2 + 1, one_row(step * 2, total))

    out_ref[...] += lax.fori_loop(
        0, rows // 2, two_rows, jnp.zeros((heads * 8, LANES), jnp.float32)
    )


def table_gradient(index, pairs):
    heads, tokens, _ = pairs.shape
    block = 64
    return pl.pallas_call(
        table_kernel,
        grid=(tokens // block,),
        in_specs=[
            pl.BlockSpec((block, tokens), lambda i: (i, 0)),
            pl.BlockSpec((heads, block, tokens), lambda i: (0, i, 0)),
        ],
        out_specs=pl.BlockSpec((heads * 8, LANES), lambda i: (0, 0)),
        out_shape=jax.ShapeDtypeStruct((heads * 8, LANES), jnp.float32),
        compiler_params=params(),
        cost_estimate=SHORT,
        name="table_gradient",
    )(index, pairs)


def load_group(part_ref, pieces, held, in_sems, full_ref, out_sems):
    step = pl.program_id(0)
    rows = pieces[0].shape[1]

    def copy(group, j):
        at = pl.multiple_of(part_ref[j] * rows, 16)
        return pltpu.make_async_copy(
            pieces[j].at[group], held.at[group, pl.ds(at, rows)], in_sems.at[group, j]
        )

    @pl.when(step == 0)
    def _():
        for group in range(held.shape[0]):
            for j in range(len(pieces)):
                copy(group, j).start()

    for j in range(len(pieces)):
        copy(step, j).wait()
    pltpu.make_async_copy(held.at[step], full_ref.at[step], out_sems.at[step]).start()


def finish_groups(held, full_ref, out_sems):
    @pl.when(pl.program_id(0) == held.shape[0] - 1)
    def _():
        for group in range(held.shape[0]):
            pltpu.make_async_copy(held.at[group], full_ref.at[group], out_sems.at[group]).wait()


def piece_call(kernel, name, part_of, pieces, inputs, in_specs, out_specs, out_shapes):
    groups, rows, packed = pieces[0].shape
    depth = rows * len(pieces)
    full = jax.ShapeDtypeStruct((groups, depth, packed), pieces[0].dtype)
    anywhere = pl.BlockSpec(memory_space=pl.ANY)
    return pl.pallas_call(
        kernel,
        grid_spec=pltpu.PrefetchScalarGridSpec(
            num_scalar_prefetch=1,
            grid=(groups,),
            in_specs=in_specs + [anywhere] * len(pieces),
            out_specs=out_specs + [anywhere],
            scratch_shapes=[
                pltpu.VMEM((groups, depth, packed), pieces[0].dtype),
                pltpu.SemaphoreType.DMA((groups, len(pieces))),
                pltpu.SemaphoreType.DMA((groups,)),
            ],
        ),
        out_shape=out_shapes + [full],
        compiler_params=params(),
        cost_estimate=SHORT,
        name=name,
    )(part_of, *inputs, *pieces)


def attend_kernel(part_ref, normed_ref, add_ref, bias_ref, *refs):
    *pieces, qkv_ref, probs_ref, mixed_ref, proj_ref, full_ref, held, in_sems, out_sems = refs
    images, heads = probs_ref.shape[1], probs_ref.shape[2]
    tokens = probs_ref.shape[3]
    width = mixed_ref.shape[2]
    size = width // heads
    scale = 1.0 / math.sqrt(size)
    kept = qkv_ref.shape[2]
    step = pl.program_id(0)
    load_group(part_ref, pieces, held, in_sems, full_ref, out_sems)
    for image in range(images):
        rows = slice(image * tokens, (image + 1) * tokens)
        acc = matmul(normed_ref[rows, :], held[step, :, :kept])
        qkv_ref[0, rows, :] = (acc + add_ref[0, image : image + 1, :]).astype(jnp.bfloat16)
    for image in range(images):
        rows = slice(image * tokens, (image + 1) * tokens)
        both = qkv_ref[0, rows, :]
        outs = []
        for head in range(heads):
            at = head * size
            query = both[:, at : at + size]
            keys = both[:, width + at : width + at + size]
            values = both[:, 2 * width + at : 2 * width + at + size]
            scores = times_transposed(query, keys) * scale + bias_ref[head]
            peak = jnp.max(scores, axis=-1, keepdims=True)
            expo = jnp.exp(scores - peak)
            total = jnp.sum(expo, axis=-1, keepdims=True)
            probs = (expo / total).astype(jnp.bfloat16)
            probs_ref[0, image, head] = probs
            outs.append(matmul(probs, values))
        mixed_ref[0, rows, :] = jnp.concatenate(outs, axis=1).astype(jnp.bfloat16)
    for group in range(held.shape[0]):

        @pl.when(step == group)
        def _(group=group):
            proj_ref[:, group * width : (group + 1) * width] = held[group, :, 3 * width :]

    finish_groups(held, full_ref, out_sems)


def attend(part_of, pieces, normed, add, bias, images, tokens):
    groups, part_rows, packed = pieces[0].shape
    depth = part_rows * len(pieces)
    heads = bias.shape[0] // groups
    width = packed // groups
    kept = add.shape[2]
    rows = images * tokens
    low = jnp.bfloat16
    return piece_call(
        attend_kernel,
        "attend",
        part_of,
        pieces,
        [normed, add, bias],
        [
            pl.BlockSpec((rows, depth), lambda f, p: (0, 0)),
            pl.BlockSpec((1, images, kept), lambda f, p: (f, 0, 0)),
            pl.BlockSpec((heads, tokens, tokens), lambda f, p: (f, 0, 0)),
        ],
        [
            pl.BlockSpec((1, rows, kept), lambda f, p: (f, 0, 0)),
            pl.BlockSpec((1, images, heads, tokens, tokens), lambda f, p: (f, 0, 0, 0, 0)),
            pl.BlockSpec((1, rows, width), lambda f, p: (f, 0, 0)),
            pl.BlockSpec((depth, packed), lambda f, p: (0, 0)),
        ],
        [
            jax.ShapeDtypeStruct((groups, rows, kept), low),
            jax.ShapeDtypeStruct((groups, images, heads, tokens, tokens), low),
            jax.ShapeDtypeStruct((groups, rows, width), low),
            jax.ShapeDtypeStruct((depth, packed), low),
        ],
    )


def up_kernel(part_ref, second_ref, bias_ref, *refs):
    *pieces, activ_ref, slope_ref, full_ref, held, in_sems, out_sems = refs
    load_group(part_ref, pieces, held, in_sems, full_ref, out_sems)
    weight = held[pl.program_id(0)]
    block = 256
    for start in range(0, second_ref.shape[0], block):
        rows = slice(start, start + block)
        pre = matmul(second_ref[rows, :], weight) + bias_ref[0]
        below = 0.5 * (1.0 + lax.erf(pre * (1.0 / math.sqrt(2.0))))
        density = jnp.exp(-0.5 * pre * pre) * (1.0 / math.sqrt(2.0 * math.pi))
        activ_ref[0, rows, :] = (pre * below).astype(jnp.bfloat16)
        slope_ref[0, rows, :] = (below + pre * density).astype(jnp.bfloat16)
    finish_groups(held, full_ref, out_sems)


def up_forward(part_of, pieces, second, bias):
    groups, part_rows, packed = pieces[0].shape
    rows, depth = second.shape
    wide = pl.BlockSpec((1, rows, packed), lambda f, p: (f, 0, 0))
    shape = jax.ShapeDtypeStruct((groups, rows, packed), jnp.bfloat16)
    return piece_call(
        up_kernel,
        "up_forward",
        part_of,
        pieces,
        [second, bias.reshape(groups, 1, packed)],
        [
            pl.BlockSpec((rows, depth), lambda f, p: (0, 0)),
            pl.BlockSpec((1, 1, packed), lambda f, p: (f, 0, 0)),
        ],
        [wide, wide],
        [shape, shape],
    )


def down_back_kernel(
    grad_ref, hidden_ref, activ_ref, slope_ref, up_ref, down_ref, pre_ref, second_ref, out_ref, total
):
    step = pl.program_id(0)
    weight = down_ref[...]
    d_activ = times_transposed(grad_ref[...], weight)
    d_pre = (d_activ * slope_ref[0].astype(jnp.float32)).astype(jnp.bfloat16)
    pre_ref[0] = d_pre
    part = times_transposed(d_pre, up_ref[0])
    more = matmul(activ_ref[0], weight)

    @pl.when(step == 0)
    def _():
        second_ref[...] = part
        total[...] = hidden_ref[...] + more

    @pl.when(step > 0)
    def _():
        second_ref[...] += part
        total[...] += more

    @pl.when(step == pl.num_programs(0) - 1)
    def _():
        out_ref[...] = total[...].astype(jnp.bfloat16)


def down_back(grad, hidden, activ, slope, up_full, down_full):
    groups, rows, packed = activ.shape
    depth = up_full.shape[1]
    whole = pl.BlockSpec((rows, depth), lambda f: (0, 0))
    mine = pl.BlockSpec((1, rows, packed), lambda f: (f, 0, 0))
    return pl.pallas_call(
        down_back_kernel,
        grid=(groups,),
        in_specs=[
            whole,
            whole,
            mine,
            mine,
            pl.BlockSpec((1, depth, packed), lambda f: (f, 0, 0)),
            pl.BlockSpec((packed, depth), lambda f: (f, 0)),
        ],
        out_specs=[mine, whole, whole],
        out_shape=[
            jax.ShapeDtypeStruct((groups, rows, packed), jnp.bfloat16),
            jax.ShapeDtypeStruct((rows, depth), jnp.float32),
            jax.ShapeDtypeStruct((rows, depth), jnp.bfloat16),
        ],
        scratch_shapes=[pltpu.VMEM((rows, depth), jnp.float32)],
        compiler_params=params(),
        cost_estimate=SHORT,
        name="down_back",
    )(grad, hidden, activ, slope, up_full, down_full)


def attend_back_kernel(grad_ref, qkv_ref, probs_ref, hidden_ref, out_ref, pairs_ref):
    images, heads = probs_ref.shape[1], probs_ref.shape[2]
    tokens = probs_ref.shape[3]
    width = grad_ref.shape[2]
    size = width // heads
    scale = 1.0 / math.sqrt(size)
    for image in range(images):
        rows = slice(image * tokens, (image + 1) * tokens)
        both = qkv_ref[0, rows, :]
        grads = grad_ref[0, rows, :]
        d_query, d_keys, d_values = [], [], []
        for head in range(heads):
            at = head * size
            query = both[:, at : at + size]
            keys = both[:, width + at : width + at + size]
            values = both[:, 2 * width + at : 2 * width + at + size]
            grad = grads[:, at : at + size]
            probs_low = probs_ref[0, image, head]
            probs = probs_low.astype(jnp.float32)
            d_values.append(contract_rows(probs_low, grad))
            d_probs = times_transposed(grad, values)
            moved = probs * d_probs
            d_scores = moved - probs * jnp.sum(moved, axis=-1, keepdims=True)
            d_low = d_scores.astype(jnp.bfloat16)
            if image == 0:
                pairs_ref[head] = d_low.astype(jnp.float32)
            else:
                pairs_ref[head] += d_low.astype(jnp.float32)
            d_query.append(matmul(d_low, keys) * scale)
            d_keys.append(contract_rows(d_low, query) * scale)
        out_ref[0, rows, :] = jnp.concatenate(
            d_query + d_keys + d_values + [hidden_ref[0, rows, :].astype(jnp.float32)], axis=1
        ).astype(jnp.bfloat16)


def attend_back(grad, qkv, probs, hidden):
    groups, rows, width = grad.shape
    kept = qkv.shape[2]
    _, images, heads, tokens, _ = probs.shape
    packed = 4 * width
    return pl.pallas_call(
        attend_back_kernel,
        grid=(groups,),
        in_specs=[
            pl.BlockSpec((1, rows, width), lambda f: (f, 0, 0)),
            pl.BlockSpec((1, rows, kept), lambda f: (f, 0, 0)),
            pl.BlockSpec((1, images, heads, tokens, tokens), lambda f: (f, 0, 0, 0, 0)),
            pl.BlockSpec((1, rows, width), lambda f: (f, 0, 0)),
        ],
        out_specs=[
            pl.BlockSpec((1, rows, packed), lambda f: (f, 0, 0)),
            pl.BlockSpec((heads, tokens, tokens), lambda f: (f, 0, 0)),
        ],
        out_shape=[
            jax.ShapeDtypeStruct((groups, rows, packed), jnp.bfloat16),
            jax.ShapeDtypeStruct((groups * heads, tokens, tokens), jnp.float32),
        ],
        compiler_params=params(),
        cost_estimate=SHORT,
        name="attend_back",
    )(grad, qkv, probs, hidden)


def store_slot(slot, own_ref, send_ref, at, value):
    half = own_ref.shape[0]

    @pl.when(slot < half)
    def _():
        own_ref[(slot,) + at] = value

    @pl.when(slot >= half)
    def _():
        send_ref[(slot - half,) + at] = value


def pair_grad_kernel(slot_ref, one_ref, two_ref, right_ref, own_ref, send_ref):
    cut = 3 * (right_ref.shape[2] // 4)
    below = cut // LANES * LANES
    above = below + LANES
    rows = own_ref.shape[2]
    right = right_ref[0]
    lane = lax.broadcasted_iota(jnp.int32, (rows, LANES), 1)
    first = matmul(one_ref[...], right[:, :above])
    last = matmul(two_ref[...], right[:, below:])
    for part in range(2 * own_ref.shape[0]):
        at = slice(part * rows, (part + 1) * rows)
        value = jnp.concatenate(
            [
                first[at, :below],
                jnp.where(lane < cut - below, first[at, below:], last[at, :LANES]),
                last[at, LANES:],
            ],
            axis=1,
        ).astype(jnp.bfloat16)
        store_slot(slot_ref[part], own_ref, send_ref, (0,), value)


def one_grad_kernel(slot_ref, one_ref, right_ref, own_ref, send_ref):
    rows = own_ref.shape[2]
    first = matmul(one_ref[...], right_ref[0])
    for part in range(2 * own_ref.shape[0]):
        value = first[part * rows : (part + 1) * rows].astype(jnp.bfloat16)
        store_slot(slot_ref[part], own_ref, send_ref, (0,), value)


def slot_grad(kernel, slots, lefts, right, parts, name):
    groups, rows, packed = right.shape
    depth = lefts[0].shape[0]
    half = jax.ShapeDtypeStruct((parts // 2, groups, depth // parts, packed), jnp.bfloat16)
    out = pl.BlockSpec((parts // 2, 1, depth // parts, packed), lambda f, s: (0, f, 0, 0))
    return pl.pallas_call(
        kernel,
        grid_spec=pltpu.PrefetchScalarGridSpec(
            num_scalar_prefetch=1,
            grid=(groups,),
            in_specs=[pl.BlockSpec((depth, rows), lambda f, s: (0, 0)) for _ in lefts]
            + [pl.BlockSpec((1, rows, packed), lambda f, s: (f, 0, 0))],
            out_specs=[out, out],
        ),
        out_shape=[half, half],
        compiler_params=params(),
        cost_estimate=SHORT,
        name=name,
    )(slots, *lefts, right)


def down_grad_kernel(slot_ref, left_ref, right_ref, own_ref, send_ref):
    half, groups, rows, packed = own_ref.shape
    width = packed // groups
    value = contract_rows(left_ref[0], right_ref[...]).astype(jnp.bfloat16)
    each = 2 * half // groups
    fold = value.shape[0] // (each * rows)
    for part in range(each):
        slot = slot_ref[pl.program_id(0) * each + part]
        base = part * fold * rows
        for f in range(groups):
            block = jnp.concatenate(
                [
                    value[base + g * rows : base + (g + 1) * rows, f * width : (f + 1) * width]
                    for g in range(fold)
                ],
                axis=1,
            )
            store_slot(slot, own_ref, send_ref, (f,), block)


def down_slot_grad(slots, left, right, parts, part_rows):
    groups, rows, packed = left.shape
    half = jax.ShapeDtypeStruct((parts // 2, groups, part_rows, packed), jnp.bfloat16)
    out = pl.BlockSpec((parts // 2, groups, part_rows, packed), lambda f, s: (0, 0, 0, 0))
    return pl.pallas_call(
        down_grad_kernel,
        grid_spec=pltpu.PrefetchScalarGridSpec(
            num_scalar_prefetch=1,
            grid=(groups,),
            in_specs=[
                pl.BlockSpec((1, rows, packed), lambda f, s: (f, 0, 0)),
                pl.BlockSpec((rows, packed), lambda f, s: (0, 0)),
            ],
            out_specs=[out, out],
        ),
        out_shape=[half, half],
        compiler_params=params(),
        cost_estimate=SHORT,
        name="down_grad",
    )(slots, left, right)


def add_kernel(one_ref, two_ref, three_ref, four_ref, came_ref, *outs):
    places = ((outs[0], (0,)), (outs[1], (0,)), (outs[2], (1, 0)), (outs[2], (0, 0)))
    for k, (mine, (out, at)) in enumerate(
        zip((one_ref, two_ref, three_ref, four_ref), places)
    ):
        total = mine[0, 0].astype(jnp.float32) + came_ref[k, 0].astype(jnp.float32)
        out[at] = total.astype(jnp.bfloat16)


def add_halves(own, came):
    half, groups, rows, packed = own.shape
    single = pl.BlockSpec((1, rows, packed), lambda f: (f, 0, 0))
    one = jax.ShapeDtypeStruct((groups, rows, packed), jnp.bfloat16)
    return pl.pallas_call(
        add_kernel,
        grid=(groups,),
        in_specs=[
            pl.BlockSpec((1, 1, rows, packed), lambda f, k=k: (k, f, 0, 0)) for k in range(half)
        ]
        + [pl.BlockSpec((half, 1, rows, packed), lambda f: (0, f, 0, 0))],
        out_specs=[single, single, pl.BlockSpec((2, 1, rows, packed), lambda f: (0, f, 0, 0))],
        out_shape=[one, one, jax.ShapeDtypeStruct((2, groups, rows, packed), jnp.bfloat16)],
        compiler_params=params(),
        cost_estimate=SHORT,
        name="add_halves",
    )(*([own] * half), came)


def unpack_kernel(part_ref, *refs):
    *pieces, out_ref, held, sems = refs
    step = pl.program_id(0)
    _, groups, rows, packed = held.shape
    width = packed // groups

    @pl.when(step == 0)
    def _():
        for j, piece in enumerate(pieces):
            pltpu.make_async_copy(piece, held.at[j], sems.at[j]).start()

    pltpu.make_async_copy(pieces[0], held.at[step], sems.at[step]).wait()
    for g in range(out_ref.shape[0] // rows):
        out_ref[g * rows : (g + 1) * rows, :] = jnp.concatenate(
            [held[step, f][:, g * width : (g + 1) * width] for f in range(groups)], axis=1
        )


def unpack_pieces(part_of, pieces, fold):
    groups, rows, width = pieces[0].shape
    parts = len(pieces)
    return pl.pallas_call(
        unpack_kernel,
        grid_spec=pltpu.PrefetchScalarGridSpec(
            num_scalar_prefetch=1,
            grid=(parts,),
            in_specs=[pl.BlockSpec(memory_space=pl.ANY)] * parts,
            out_specs=pl.BlockSpec((fold * rows, width), lambda j, p: (p[j], 0)),
            scratch_shapes=[
                pltpu.VMEM((parts, groups, rows, width), pieces[0].dtype),
                pltpu.SemaphoreType.DMA((parts,)),
            ],
        ),
        out_shape=jax.ShapeDtypeStruct((parts * fold * rows, width), pieces[0].dtype),
        compiler_params=params(),
        cost_estimate=SHORT,
        name="unpack_pieces",
    )(part_of, *pieces)


NEAR = ((0, 2, 4, 6), (0, 4, 2, 6))


def is_cube():
    return lax.axis_size("dp") == 8 and lax.axis_size("fsdp") == 4


def part_tables():
    part_of = np.zeros((8, 8), np.int32)
    slot_of = np.zeros((8, 8), np.int32)
    for part in range(8):
        core = part & 1
        order = [part ^ m for m in NEAR[core]] + [part ^ 1 ^ m for m in NEAR[1 - core]]
        part_of[part] = order
        for slot, other in enumerate(order):
            slot_of[part, other] = slot
    own = lax.axis_index("dp")
    pick = lambda table: lax.dynamic_slice(jnp.asarray(table), (own, 0), (1, 8))[0]
    return pick(part_of), pick(slot_of)


def swap(value, hop):
    return lax.ppermute(value, "dp", [(i, i ^ NEAR[i & 1][hop]) for i in range(8)])


def swap_core(value):
    return lax.ppermute(value, "dp", [(i, i ^ 1) for i in range(8)])


def after(value, *others):
    return lax.optimization_barrier((value, *others))[0]


class Gather:
    def __init__(self, shard, behind=None, ready=None):
        if behind is not None:
            shard = after(shard, behind.own)
        own = lax.all_gather(shard, "fsdp", axis=0, tiled=False)
        if behind is not None:
            own = after(own, behind.first)
        if ready is not None:
            own = after(own, ready)
        self.own = own
        self.first = swap(own, 1)
        second = swap(own, 2)
        third = swap(self.first, 2)
        near = [own, self.first, second, third]
        self.pieces = near + [swap_core(piece) for piece in near]


class Scatter:
    def __init__(self, own, send):
        self.own = own
        self.came = swap_core(send)

    def near(self):
        self.zero, self.one, pair = add_halves(self.own, self.came)
        self.far = swap(pair, 2)
        return pair

    def back(self):
        one = self.one.astype(jnp.float32) + self.far[0].astype(jnp.float32)
        one = one.astype(jnp.bfloat16)
        self.last = swap(one, 1)
        return one

    def total(self):
        total = self.zero.astype(jnp.float32) + self.far[1].astype(jnp.float32)
        self.sum = (total + self.last.astype(jnp.float32)).astype(jnp.bfloat16)
        return self.sum

    def end(self):
        return lax.psum_scatter(self.sum, "fsdp", scatter_dimension=0, tiled=False)


def swap_bit(value, axis, bit):
    size = lax.axis_size(axis)
    return lax.ppermute(value, axis, [(i, i ^ (1 << bit)) for i in range(size)])


def bit_of(axis, bit):
    return (lax.axis_index(axis) >> bit) & 1 == 1


def small_gather(value, axis):
    if not is_cube():
        return lax.all_gather(value, axis, axis=0, tiled=True)
    for bit in range(lax.axis_size(axis).bit_length() - 1):
        other = swap_bit(value, axis, bit)
        value = jnp.where(
            bit_of(axis, bit),
            jnp.concatenate([other, value], axis=0),
            jnp.concatenate([value, other], axis=0),
        )
    return value


def small_scatter(value, axis):
    if not is_cube():
        return lax.psum_scatter(value, axis, scatter_dimension=0, tiled=True)
    for bit in reversed(range(lax.axis_size(axis).bit_length() - 1)):
        half = value.shape[0] // 2
        high = bit_of(axis, bit)
        keep = jnp.where(high, value[half:], value[:half])
        value = keep + swap_bit(jnp.where(high, value[:half], value[half:]), axis, bit)
    return value


def small_sum(value, axis):
    if not is_cube():
        return lax.psum(value, axis)
    for bit in range(lax.axis_size(axis).bit_length() - 1):
        value = value + swap_bit(value, axis, bit)
    return value


def gather_shards(shard):
    rows, width = shard.shape
    groups, parts = lax.axis_size("fsdp"), lax.axis_size("dp")
    full = lax.all_gather(shard, ("fsdp", "dp"), axis=0, tiled=True)
    return full.reshape(groups, parts, rows, width)


def scatter_sum(terms):
    groups, parts, rows, width = terms.shape
    return lax.psum_scatter(
        terms.reshape(groups * parts * rows, width),
        ("fsdp", "dp"),
        scatter_dimension=0,
        tiled=True,
    )


def pack_down(natural, groups, parts, rows):
    total, width = natural.shape
    split = natural.reshape(parts, total // (parts * rows), rows, groups, width // groups)
    return split.transpose(3, 0, 2, 1, 4).reshape(groups, parts, rows, width)


def unpack_down(packed, fold):
    groups, parts, rows, width = packed.shape
    split = packed.reshape(groups, parts, rows, fold, width // fold)
    return split.transpose(1, 3, 2, 0, 4).reshape(parts * fold * rows, width)


def body(
    images,
    time_vector,
    timesteps,
    offset_index,
    query_weight,
    key_weight,
    value_weight,
    tquery_weight,
    tvalue_weight,
    proj_weight,
    proj_bias,
    first_gain,
    first_shift,
    second_gain,
    second_shift,
    up_weight,
    down_weight,
    up_bias,
    down_bias,
    bias_table,
    cotangent,
):
    low = jnp.bfloat16
    wide = jnp.float32
    count, tokens, width = images.shape
    rows = count * tokens
    groups, parts = lax.axis_size("fsdp"), lax.axis_size("dp")
    shard_rows, shard_cols = query_weight.shape
    group_heads, table_rows = bias_table.shape
    heads = group_heads * groups
    fold = down_weight.shape[0] // shard_rows
    own_part = lax.axis_index("dp")
    own_group = lax.axis_index("fsdp")

    wire_attn = jnp.concatenate([query_weight, key_weight, value_weight, proj_weight], axis=1)
    wire_down = jnp.concatenate(
        [down_weight[g * shard_rows : (g + 1) * shard_rows] for g in range(fold)], axis=1
    )
    small = jnp.concatenate(
        [
            proj_bias,
            first_gain,
            first_shift,
            second_gain,
            second_shift,
            down_bias,
            up_bias,
            bias_table.reshape(-1),
        ]
    )
    small = jnp.pad(small, (0, -small.shape[0] % 1024))
    small_all = small_gather(small.reshape(1, -1, LANES), "fsdp").reshape(groups, -1)

    def vector_of(slot):
        return small_all[:, slot * shard_cols : (slot + 1) * shard_cols].reshape(-1).astype(wide)

    proj_b, gain_one, shift_one, gain_two, shift_two, down_b = (vector_of(i) for i in range(6))
    at = 6 * shard_cols
    up_b = small_all[:, at : at + up_bias.shape[0]].astype(wide)
    at = at + up_bias.shape[0]
    table = small_all[:, at : at + group_heads * table_rows].reshape(heads, table_rows)
    table = jnp.pad(table, ((0, 0), (0, 8 * LANES - table_rows)))
    bias = position_bias(offset_index, table)

    time_low = (time_vector.astype(wide) + sinusoid(timesteps, width)).astype(low)
    time_all = small_gather(small_gather(time_low, "fsdp"), "dp")
    all_images = time_all.shape[0]
    time_cols = lax.dynamic_slice(
        time_all, (0, own_part * shard_rows), (all_images, shard_rows)
    )
    time_weight = jnp.concatenate([tquery_weight, tvalue_weight], axis=1)
    time_sum = small_scatter(matmul(time_cols, time_weight), "dp")
    time_part = small_gather(time_sum[None], "fsdp")
    time_own = lax.dynamic_slice(
        time_part, (0, own_group * count, 0), (groups, count, 2 * shard_cols)
    )
    gap = jnp.zeros((groups, count, shard_cols), wide)
    kept = -(-3 * shard_cols // LANES) * LANES
    time_add = jnp.concatenate(
        [
            time_own[:, :, :shard_cols],
            gap,
            time_own[:, :, shard_cols:],
            gap[:, :, : kept - 3 * shard_cols],
        ],
        axis=2,
    )

    cube = is_cube()
    if cube:
        part_of, slot_of = part_tables()
        attn_move = Gather(wire_attn)
        up_move = Gather(up_weight, behind=attn_move)
        down_move = Gather(wire_down, behind=up_move)
        attn_pieces, up_pieces = attn_move.pieces, up_move.pieces
        down_full = unpack_pieces(part_of, down_move.pieces, fold)
    else:
        part_of = jnp.zeros((1,), jnp.int32)
        attn_pieces = [gather_shards(wire_attn).reshape(groups, width, width)]
        up_pieces = [gather_shards(up_weight).reshape(groups, width, width)]
        down_full = unpack_down(gather_shards(wire_down), fold)

    x_rows = images.reshape(rows, width).astype(wide)
    normed, unit_one, inv_one = normalize(x_rows, gain_one, shift_one)
    normed_low = normed.astype(low)
    qkv, probs, mixed_split, proj_full, attn_full = attend(
        part_of, attn_pieces, normed_low, time_add, bias, count, tokens
    )
    mixed = mixed_split.transpose(1, 0, 2).reshape(rows, width)
    hidden = x_rows + (matmul(mixed, proj_full) + proj_b)
    second, unit_two, inv_two = normalize(hidden, gain_two, shift_two)
    second_low = second.astype(low)
    grad_low = cotangent.reshape(rows, width)
    grad_rows = grad_low.astype(wide)
    wire = (groups, parts, shard_rows, width)
    if cube:
        second_low = after(second_low, down_move.first)
    activ, slope, up_full = up_forward(part_of, up_pieces, second_low, up_b)
    grad_cols = grad_low
    if cube:
        own, send = down_slot_grad(slot_of, activ, grad_low, parts, shard_rows)
        down_move = Scatter(own, send)
        grad_cols = after(grad_low, down_move.near())
    d_pre, d_second, layer_out = down_back(
        grad_cols, hidden + down_b, activ, slope, up_full, down_full
    )
    layer_out = layer_out.reshape(count, tokens, width)
    if cube:
        own, send = slot_grad(
            one_grad_kernel, slot_of, [second_low.T], d_pre, parts, "up_grad"
        )
        up_move = Scatter(own, send)
        d_second = after(d_second, send)
    else:
        grad_down = jnp.concatenate([contract_rows(a, grad_low) for a in activ], axis=0)
        down_sum = scatter_sum(pack_down(grad_down.astype(low), groups, parts, shard_rows))
        grad_up = jnp.stack([contract_rows(second_low, d).astype(low) for d in d_pre])
        up_sum = scatter_sum(grad_up.reshape(wire))

    d_hidden = grad_rows + norm_back(d_second, unit_two, inv_two, gain_two)
    d_hidden_low = d_hidden.astype(low)
    d_mixed = times_transposed(d_hidden_low, proj_full).astype(low)
    d_mixed_split = d_mixed.reshape(rows, groups, shard_cols).transpose(1, 0, 2)
    d_hidden_split = d_hidden_low.reshape(rows, groups, shard_cols).transpose(1, 0, 2)
    if cube:
        d_mixed_split = after(d_mixed_split, down_move.back(), up_move.near())
    d_packed, pairs = attend_back(d_mixed_split, qkv, probs, d_hidden_split)
    attn_back = attn_full
    if cube:
        normed_t = after(normed_low.T, down_move.total())
        own, send = slot_grad(
            pair_grad_kernel, slot_of, [normed_t, mixed.T], d_packed, parts, "pair_grad"
        )
        attn_move = Scatter(own, send)
        attn_back = after(attn_full, send, up_move.back())
        pairs = after(pairs, attn_move.near(), up_move.total())
    else:
        cut = 3 * shard_cols
        grad_attn = jnp.stack(
            [
                jnp.concatenate(
                    [contract_rows(normed_low, d[:, :cut]), contract_rows(mixed, d[:, cut:])],
                    axis=1,
                )
                for d in d_packed
            ]
        )
        attn_sum = scatter_sum(grad_attn.astype(low).reshape(wire))

    d_time = after(d_packed, attn_back)
    d_time = jnp.sum(d_time.reshape(groups, count, tokens, width).astype(wide), axis=2)
    d_time = jnp.concatenate(
        [d_time[:, :, :shard_cols], d_time[:, :, 2 * shard_cols : 3 * shard_cols]], axis=2
    ).astype(low)
    d_time = d_time.transpose(1, 0, 2).reshape(count, groups * 2 * shard_cols)
    d_time_all = small_gather(small_gather(d_time, "fsdp"), "dp")
    d_time_cols = lax.dynamic_slice(
        d_time_all, (0, own_group * 2 * shard_cols), (all_images, 2 * shard_cols)
    )
    time_grads = contract_rows(time_cols, d_time_cols)
    tquery_grad = time_grads[:, :shard_cols]
    tvalue_grad = time_grads[:, shard_cols:]
    back = times_transposed(d_time_cols, time_weight)
    back = back.reshape(parts, groups, count, shard_rows).transpose(1, 0, 2, 3)
    back = small_gather(small_scatter(back, "fsdp"), "dp")
    back = lax.dynamic_slice(
        back, (0, own_part, 0, 0), (parts, 1, count, shard_rows)
    ).reshape(parts, count, shard_rows)
    time_grad = back.transpose(1, 0, 2).reshape(count, width)

    lane = lax.broadcasted_iota(jnp.int32, (1, width), 1)
    d_normed = jnp.zeros((rows, width), wide)
    for g in range(groups):
        part = jnp.where(lane < 3 * shard_cols, d_packed[g], jnp.zeros((), low))
        d_normed = d_normed + times_transposed(part, attn_back[g])
    d_input = d_hidden + norm_back(d_normed, unit_one, inv_one, gain_one)
    images_grad = d_input.astype(low).reshape(count, tokens, width)

    table_sum = table_gradient(offset_index, pairs).reshape(heads, 8 * LANES)[:, :table_rows]

    def rows_sum(value):
        return jnp.sum(value, axis=0).reshape(groups, -1)

    vectors = [
        rows_sum(d_hidden_low.astype(wide)),
        rows_sum(d_normed * unit_one),
        rows_sum(d_normed),
        rows_sum(d_second * unit_two),
        rows_sum(d_second),
        rows_sum(grad_rows),
        jnp.sum(d_pre.astype(wide), axis=1),
        table_sum.reshape(groups, group_heads * table_rows),
    ]
    flat = jnp.concatenate(vectors, axis=1)
    flat = jnp.pad(flat, ((0, 0), (0, -flat.shape[1] % 1024)))
    own = small_sum(small_scatter(flat.reshape(groups, -1, LANES), "fsdp"), "dp").reshape(-1)
    proj_bg, gain1_g, shift1_g, gain2_g, shift2_g, down_bg = (
        own[i * shard_cols : (i + 1) * shard_cols] for i in range(6)
    )
    at = 6 * shard_cols
    up_bg = own[at : at + up_bias.shape[0]]
    at = at + up_bias.shape[0]
    table_grad = own[at : at + group_heads * table_rows].reshape(group_heads, table_rows)

    if cube:
        down_sum = down_move.end()
        attn_move.back()
        up_sum = up_move.end()
        attn_move.total()
        attn_sum = attn_move.end()
    attn_sum = attn_sum.astype(wide)
    query_grad, key_grad, value_grad, proj_grad = (
        attn_sum[:, i * shard_cols : (i + 1) * shard_cols] for i in range(4)
    )
    down_sum = down_sum.astype(wide)
    down_grad = jnp.concatenate(
        [down_sum[:, g * shard_cols : (g + 1) * shard_cols] for g in range(fold)], axis=0
    )
    return (
        layer_out,
        images_grad,
        time_grad,
        query_grad,
        key_grad,
        value_grad,
        tquery_grad,
        tvalue_grad,
        proj_grad,
        proj_bg,
        gain1_g,
        shift1_g,
        gain2_g,
        shift2_g,
        up_sum.astype(wide),
        down_grad,
        up_bg,
        down_bg,
        table_grad,
    )


def solution(mesh):
    rows = P(BOTH, None, None)
    matrix = P("dp", "fsdp")
    vector = P("fsdp")
    table = P("fsdp", None)
    return jax.shard_map(
        body,
        mesh=mesh,
        in_specs=(
            (rows, P(BOTH, None), P(BOTH), P())
            + (matrix,) * 6
            + (vector,) * 5
            + (matrix,) * 2
            + (vector,) * 2
            + (table, rows)
        ),
        out_specs=(
            (rows, rows, P(BOTH, None))
            + (matrix,) * 6
            + (vector,) * 5
            + (matrix,) * 2
            + (vector,) * 2
            + (table,)
        ),
        check_vma=False,
    )
```

```python
import math

import jax
import jax.numpy as jnp
import numpy as np
from jax import lax
from jax.experimental import pallas as pl
from jax.experimental.pallas import tpu as pltpu
from jax.sharding import PartitionSpec as P

LANES = 128
BOTH = ("dp", "fsdp")
VMEM_LIMIT = 58 * 1024 * 1024
SHORT = pl.CostEstimate(flops=1, transcendentals=0, bytes_accessed=1)


def sinusoid(steps, model_width):
    half_width = model_width // 2
    frequency = jnp.exp(
        -math.log(10000.0) * jnp.arange(half_width).astype(jnp.float32) / half_width
    )
    angles = steps.astype(jnp.float32)[:, None] * frequency[None, :]
    return jnp.concatenate([jnp.sin(angles), jnp.cos(angles)], axis=1)


def matmul(left, right):
    return jnp.dot(left, right, preferred_element_type=jnp.float32)


def contract_rows(left, right):
    return lax.dot_general(
        left, right, (((0,), (0,)), ((), ())), preferred_element_type=jnp.float32
    )


def times_transposed(left, right):
    return lax.dot_general(
        left, right, (((1,), (1,)), ((), ())), preferred_element_type=jnp.float32
    )


def normalize(values, gain, shift):
    row_mean = jnp.mean(values, axis=-1, keepdims=True)
    centered = values - row_mean
    inv_std = lax.rsqrt(jnp.mean(centered * centered, axis=-1, keepdims=True) + 1e-06)
    unit_rows = centered * inv_std
    return (unit_rows * gain + shift, unit_rows, inv_std)


def norm_back(grad_rows, unit_rows, inv_std, gain):
    scaled = grad_rows * gain
    return inv_std * (
        scaled
        - jnp.mean(scaled, axis=-1, keepdims=True)
        - unit_rows * jnp.mean(scaled * unit_rows, axis=-1, keepdims=True)
    )


def gelu_slope(pre_act):
    return 0.5 * (1.0 + lax.erf(pre_act * (1.0 / math.sqrt(2.0)))) + pre_act * jnp.exp(
        -0.5 * pre_act * pre_act
    ) * (1.0 / math.sqrt(2.0 * math.pi))


def params(count=1):
    return pltpu.CompilerParams(
        dimension_semantics=("arbitrary",) * count, vmem_limit_bytes=VMEM_LIMIT
    )


def bias_kernel(index_ref, table_ref, bias_ref):
    heads, rows, tokens = bias_ref.shape
    chunks = table_ref.shape[2] // LANES
    pieces = [
        [
            jnp.broadcast_to(table_ref[h, :, c * LANES : (c + 1) * LANES], (8, LANES))
            for c in range(chunks)
        ]
        for h in range(heads)
    ]

    def some_rows(step, carry):
        at = pl.multiple_of(step * 8, 8)
        for col in range(tokens // LANES):
            lanes = slice(col * LANES, (col + 1) * LANES)
            index = index_ref[pl.ds(at, 8), lanes]
            low = index & (LANES - 1)
            high = index >> 7
            hits = [high == c for c in range(chunks)]
            for h in range(heads):
                found = jnp.take_along_axis(pieces[h][0], low, axis=1)
                for c in range(1, chunks):
                    found = jnp.where(
                        hits[c], jnp.take_along_axis(pieces[h][c], low, axis=1), found
                    )
                bias_ref[h, pl.ds(at, 8), lanes] = found
        return carry

    lax.fori_loop(0, rows // 8, some_rows, 0)


def position_bias(index, table):
    heads, padded = table.shape
    tokens = index.shape[0]
    group = heads // 4
    return pl.pallas_call(
        bias_kernel,
        grid=(4,),
        in_specs=[
            pl.BlockSpec((tokens, tokens), lambda f: (0, 0)),
            pl.BlockSpec((group, 1, padded), lambda f: (f, 0, 0)),
        ],
        out_specs=pl.BlockSpec((group, tokens, tokens), lambda f: (f, 0, 0)),
        out_shape=jax.ShapeDtypeStruct((heads, tokens, tokens), jnp.float32),
        compiler_params=params(),
        cost_estimate=pl.CostEstimate(flops=1 << 34, transcendentals=0, bytes_accessed=1 << 22),
        name="position_bias",
    )(index, table.astype(jnp.float32).reshape(heads, 1, padded))


def table_kernel(index_ref, pairs_ref, out_ref):
    heads = pairs_ref.shape[0]
    tokens = index_ref.shape[1]
    rows = index_ref.shape[0]

    @pl.when(pl.program_id(0) == 0)
    def _():
        out_ref[...] = jnp.zeros_like(out_ref)

    sub = lax.broadcasted_iota(jnp.int32, (8, tokens), 0)
    lane_of = lax.broadcasted_iota(jnp.int32, (LANES, tokens), 0)

    def row_terms(row):
        index = index_ref[pl.ds(row, 1), :]
        low = jnp.broadcast_to(index & (LANES - 1), (LANES, tokens))
        high = jnp.broadcast_to(index >> 7, (8, tokens))
        hit = sub == high
        left = jnp.concatenate(
            [
                jnp.where(hit, jnp.broadcast_to(pairs_ref[h, pl.ds(row, 1), :], (8, tokens)), 0.0)
                for h in range(heads)
            ],
            axis=0,
        ).astype(jnp.bfloat16)
        right = jnp.where(lane_of == low, 1.0, 0.0).astype(jnp.bfloat16)
        return left, right

    def some_rows(step, total):
        terms = [row_terms(step * 4 + k) for k in range(4)]
        left = jnp.concatenate([t[0] for t in terms], axis=1)
        right = jnp.concatenate([t[1] for t in terms], axis=1)
        return total + times_transposed(left, right)

    out_ref[...] += lax.fori_loop(
        0, rows // 4, some_rows, jnp.zeros((heads * 8, LANES), jnp.float32)
    )


def table_gradient(index, pairs):
    heads, tokens, _ = pairs.shape
    block = 64
    return pl.pallas_call(
        table_kernel,
        grid=(tokens // block,),
        in_specs=[
            pl.BlockSpec((block, tokens), lambda i: (i, 0)),
            pl.BlockSpec((heads, block, tokens), lambda i: (0, i, 0)),
        ],
        out_specs=pl.BlockSpec((heads * 8, LANES), lambda i: (0, 0)),
        out_shape=jax.ShapeDtypeStruct((heads * 8, LANES), jnp.float32),
        compiler_params=params(),
        cost_estimate=SHORT,
        name="table_gradient",
    )(index, pairs)


def load_group(part_ref, pieces, held, in_sems, full_ref, out_sems):
    step = pl.program_id(0)
    rows = pieces[0].shape[1]

    def copy(group, j):
        at = pl.multiple_of(part_ref[j] * rows, 16)
        return pltpu.make_async_copy(
            pieces[j].at[group], held.at[group, pl.ds(at, rows)], in_sems.at[group, j]
        )

    @pl.when(step == 0)
    def _():
        for group in range(held.shape[0]):
            for j in range(len(pieces)):
                copy(group, j).start()

    for j in range(len(pieces)):
        copy(step, j).wait()
    pltpu.make_async_copy(held.at[step], full_ref.at[step], out_sems.at[step]).start()


def finish_groups(held, full_ref, out_sems):
    @pl.when(pl.program_id(0) == held.shape[0] - 1)
    def _():
        for group in range(held.shape[0]):
            pltpu.make_async_copy(held.at[group], full_ref.at[group], out_sems.at[group]).wait()


def piece_call(kernel, name, part_of, pieces, inputs, in_specs, out_specs, out_shapes):
    groups, rows, packed = pieces[0].shape
    depth = rows * len(pieces)
    full = jax.ShapeDtypeStruct((groups, depth, packed), pieces[0].dtype)
    anywhere = pl.BlockSpec(memory_space=pl.ANY)
    return pl.pallas_call(
        kernel,
        grid_spec=pltpu.PrefetchScalarGridSpec(
            num_scalar_prefetch=1,
            grid=(groups,),
            in_specs=in_specs + [anywhere] * len(pieces),
            out_specs=out_specs + [anywhere],
            scratch_shapes=[
                pltpu.VMEM((groups, depth, packed), pieces[0].dtype),
                pltpu.SemaphoreType.DMA((groups, len(pieces))),
                pltpu.SemaphoreType.DMA((groups,)),
            ],
        ),
        out_shape=out_shapes + [full],
        compiler_params=params(),
        cost_estimate=SHORT,
        name=name,
    )(part_of, *inputs, *pieces)


def attend_kernel(part_ref, normed_ref, add_ref, bias_ref, *refs):
    *pieces, qkv_ref, probs_ref, mixed_ref, proj_ref, full_ref, held, in_sems, out_sems = refs
    images, heads = probs_ref.shape[1], probs_ref.shape[2]
    tokens = probs_ref.shape[3]
    width = mixed_ref.shape[2]
    size = width // heads
    scale = 1.0 / math.sqrt(size)
    kept = qkv_ref.shape[2]
    step = pl.program_id(0)
    load_group(part_ref, pieces, held, in_sems, full_ref, out_sems)
    for image in range(images):
        rows = slice(image * tokens, (image + 1) * tokens)
        acc = matmul(normed_ref[rows, :], held[step, :, :kept])
        qkv_ref[0, rows, :] = (acc + add_ref[0, image : image + 1, :]).astype(jnp.bfloat16)
    for image in range(images):
        rows = slice(image * tokens, (image + 1) * tokens)
        both = qkv_ref[0, rows, :]
        outs = []
        for head in range(heads):
            at = head * size
            query = both[:, at : at + size]
            keys = both[:, width + at : width + at + size]
            values = both[:, 2 * width + at : 2 * width + at + size]
            scores = times_transposed(query, keys) * scale + bias_ref[head]
            peak = jnp.max(scores, axis=-1, keepdims=True)
            expo = jnp.exp(scores - peak)
            total = jnp.sum(expo, axis=-1, keepdims=True)
            probs = (expo / total).astype(jnp.bfloat16)
            probs_ref[0, image, head] = probs
            outs.append(matmul(probs, values))
        mixed_ref[0, rows, :] = jnp.concatenate(outs, axis=1).astype(jnp.bfloat16)
    for group in range(held.shape[0]):

        @pl.when(step == group)
        def _(group=group):
            proj_ref[:, group * width : (group + 1) * width] = held[group, :, 3 * width :]

    finish_groups(held, full_ref, out_sems)


def attend(part_of, pieces, normed, add, bias, images, tokens):
    groups, part_rows, packed = pieces[0].shape
    depth = part_rows * len(pieces)
    heads = bias.shape[0] // groups
    width = packed // groups
    kept = add.shape[2]
    rows = images * tokens
    low = jnp.bfloat16
    return piece_call(
        attend_kernel,
        "attend",
        part_of,
        pieces,
        [normed, add, bias],
        [
            pl.BlockSpec((rows, depth), lambda f, p: (0, 0)),
            pl.BlockSpec((1, images, kept), lambda f, p: (f, 0, 0)),
            pl.BlockSpec((heads, tokens, tokens), lambda f, p: (f, 0, 0)),
        ],
        [
            pl.BlockSpec((1, rows, kept), lambda f, p: (f, 0, 0)),
            pl.BlockSpec((1, images, heads, tokens, tokens), lambda f, p: (f, 0, 0, 0, 0)),
            pl.BlockSpec((1, rows, width), lambda f, p: (f, 0, 0)),
            pl.BlockSpec((depth, packed), lambda f, p: (0, 0)),
        ],
        [
            jax.ShapeDtypeStruct((groups, rows, kept), low),
            jax.ShapeDtypeStruct((groups, images, heads, tokens, tokens), low),
            jax.ShapeDtypeStruct((groups, rows, width), low),
            jax.ShapeDtypeStruct((depth, packed), low),
        ],
    )


def up_kernel(part_ref, second_ref, bias_ref, *refs):
    *pieces, activ_ref, slope_ref, full_ref, held, in_sems, out_sems = refs
    load_group(part_ref, pieces, held, in_sems, full_ref, out_sems)
    weight = held[pl.program_id(0)]
    block = 256
    for start in range(0, second_ref.shape[0], block):
        rows = slice(start, start + block)
        pre = matmul(second_ref[rows, :], weight) + bias_ref[0]
        below = 0.5 * (1.0 + lax.erf(pre * (1.0 / math.sqrt(2.0))))
        density = jnp.exp(-0.5 * pre * pre) * (1.0 / math.sqrt(2.0 * math.pi))
        activ_ref[0, rows, :] = (pre * below).astype(jnp.bfloat16)
        slope_ref[0, rows, :] = (below + pre * density).astype(jnp.bfloat16)
    finish_groups(held, full_ref, out_sems)


def up_forward(part_of, pieces, second, bias):
    groups, part_rows, packed = pieces[0].shape
    rows, depth = second.shape
    wide = pl.BlockSpec((1, rows, packed), lambda f, p: (f, 0, 0))
    shape = jax.ShapeDtypeStruct((groups, rows, packed), jnp.bfloat16)
    return piece_call(
        up_kernel,
        "up_forward",
        part_of,
        pieces,
        [second, bias.reshape(groups, 1, packed)],
        [
            pl.BlockSpec((rows, depth), lambda f, p: (0, 0)),
            pl.BlockSpec((1, 1, packed), lambda f, p: (f, 0, 0)),
        ],
        [wide, wide],
        [shape, shape],
    )


def down_back_kernel(
    grad_ref, hidden_ref, activ_ref, slope_ref, up_ref, down_ref, pre_ref, second_ref, out_ref, total
):
    step = pl.program_id(0)
    weight = down_ref[...]
    d_activ = times_transposed(grad_ref[...], weight)
    d_pre = (d_activ * slope_ref[0].astype(jnp.float32)).astype(jnp.bfloat16)
    pre_ref[0] = d_pre
    part = times_transposed(d_pre, up_ref[0])
    more = matmul(activ_ref[0], weight)

    @pl.when(step == 0)
    def _():
        second_ref[...] = part
        total[...] = hidden_ref[...] + more

    @pl.when(step > 0)
    def _():
        second_ref[...] += part
        total[...] += more

    @pl.when(step == pl.num_programs(0) - 1)
    def _():
        out_ref[...] = total[...].astype(jnp.bfloat16)


def down_back(grad, hidden, activ, slope, up_full, down_full):
    groups, rows, packed = activ.shape
    depth = up_full.shape[1]
    whole = pl.BlockSpec((rows, depth), lambda f: (0, 0))
    mine = pl.BlockSpec((1, rows, packed), lambda f: (f, 0, 0))
    return pl.pallas_call(
        down_back_kernel,
        grid=(groups,),
        in_specs=[
            whole,
            whole,
            mine,
            mine,
            pl.BlockSpec((1, depth, packed), lambda f: (f, 0, 0)),
            pl.BlockSpec((packed, depth), lambda f: (f, 0)),
        ],
        out_specs=[mine, whole, whole],
        out_shape=[
            jax.ShapeDtypeStruct((groups, rows, packed), jnp.bfloat16),
            jax.ShapeDtypeStruct((rows, depth), jnp.float32),
            jax.ShapeDtypeStruct((rows, depth), jnp.bfloat16),
        ],
        scratch_shapes=[pltpu.VMEM((rows, depth), jnp.float32)],
        compiler_params=params(),
        cost_estimate=SHORT,
        name="down_back",
    )(grad, hidden, activ, slope, up_full, down_full)


def attend_back_kernel(grad_ref, qkv_ref, probs_ref, hidden_ref, out_ref, pairs_ref):
    images, heads = probs_ref.shape[1], probs_ref.shape[2]
    tokens = probs_ref.shape[3]
    width = grad_ref.shape[2]
    size = width // heads
    scale = 1.0 / math.sqrt(size)
    for image in range(images):
        rows = slice(image * tokens, (image + 1) * tokens)
        both = qkv_ref[0, rows, :]
        grads = grad_ref[0, rows, :]
        d_query, d_keys, d_values = [], [], []
        for head in range(heads):
            at = head * size
            query = both[:, at : at + size]
            keys = both[:, width + at : width + at + size]
            values = both[:, 2 * width + at : 2 * width + at + size]
            grad = grads[:, at : at + size]
            probs_low = probs_ref[0, image, head]
            probs = probs_low.astype(jnp.float32)
            d_values.append(contract_rows(probs_low, grad))
            d_probs = times_transposed(grad, values)
            moved = probs * d_probs
            d_scores = moved - probs * jnp.sum(moved, axis=-1, keepdims=True)
            d_low = d_scores.astype(jnp.bfloat16)
            if image == 0:
                pairs_ref[head] = d_low.astype(jnp.float32)
            else:
                pairs_ref[head] += d_low.astype(jnp.float32)
            d_query.append(matmul(d_low, keys) * scale)
            d_keys.append(contract_rows(d_low, query) * scale)
        out_ref[0, rows, :] = jnp.concatenate(
            d_query + d_keys + d_values + [hidden_ref[0, rows, :].astype(jnp.float32)], axis=1
        ).astype(jnp.bfloat16)


def attend_back(grad, qkv, probs, hidden):
    groups, rows, width = grad.shape
    kept = qkv.shape[2]
    _, images, heads, tokens, _ = probs.shape
    packed = 4 * width
    return pl.pallas_call(
        attend_back_kernel,
        grid=(groups,),
        in_specs=[
            pl.BlockSpec((1, rows, width), lambda f: (f, 0, 0)),
            pl.BlockSpec((1, rows, kept), lambda f: (f, 0, 0)),
            pl.BlockSpec((1, images, heads, tokens, tokens), lambda f: (f, 0, 0, 0, 0)),
            pl.BlockSpec((1, rows, width), lambda f: (f, 0, 0)),
        ],
        out_specs=[
            pl.BlockSpec((1, rows, packed), lambda f: (f, 0, 0)),
            pl.BlockSpec((heads, tokens, tokens), lambda f: (f, 0, 0)),
        ],
        out_shape=[
            jax.ShapeDtypeStruct((groups, rows, packed), jnp.bfloat16),
            jax.ShapeDtypeStruct((groups * heads, tokens, tokens), jnp.float32),
        ],
        compiler_params=params(),
        cost_estimate=SHORT,
        name="attend_back",
    )(grad, qkv, probs, hidden)


def store_slot(slot, own_ref, send_ref, at, value):
    half = own_ref.shape[0]

    @pl.when(slot < half)
    def _():
        own_ref[(slot,) + at] = value

    @pl.when(slot >= half)
    def _():
        send_ref[(slot - half,) + at] = value


def pair_grad_kernel(slot_ref, one_ref, two_ref, right_ref, own_ref, send_ref):
    cut = 3 * (right_ref.shape[2] // 4)
    below = cut // LANES * LANES
    above = below + LANES
    rows = own_ref.shape[2]
    right = right_ref[0]
    lane = lax.broadcasted_iota(jnp.int32, (rows, LANES), 1)
    first = matmul(one_ref[...], right[:, :above])
    last = matmul(two_ref[...], right[:, below:])
    for part in range(2 * own_ref.shape[0]):
        at = slice(part * rows, (part + 1) * rows)
        value = jnp.concatenate(
            [
                first[at, :below],
                jnp.where(lane < cut - below, first[at, below:], last[at, :LANES]),
                last[at, LANES:],
            ],
            axis=1,
        ).astype(jnp.bfloat16)
        store_slot(slot_ref[part], own_ref, send_ref, (0,), value)


def one_grad_kernel(slot_ref, one_ref, right_ref, own_ref, send_ref):
    rows = own_ref.shape[2]
    first = matmul(one_ref[...], right_ref[0])
    for part in range(2 * own_ref.shape[0]):
        value = first[part * rows : (part + 1) * rows].astype(jnp.bfloat16)
        store_slot(slot_ref[part], own_ref, send_ref, (0,), value)


def slot_grad(kernel, slots, lefts, right, parts, name):
    groups, rows, packed = right.shape
    depth = lefts[0].shape[0]
    half = jax.ShapeDtypeStruct((parts // 2, groups, depth // parts, packed), jnp.bfloat16)
    out = pl.BlockSpec((parts // 2, 1, depth // parts, packed), lambda f, s: (0, f, 0, 0))
    return pl.pallas_call(
        kernel,
        grid_spec=pltpu.PrefetchScalarGridSpec(
            num_scalar_prefetch=1,
            grid=(groups,),
            in_specs=[pl.BlockSpec((depth, rows), lambda f, s: (0, 0)) for _ in lefts]
            + [pl.BlockSpec((1, rows, packed), lambda f, s: (f, 0, 0))],
            out_specs=[out, out],
        ),
        out_shape=[half, half],
        compiler_params=params(),
        cost_estimate=SHORT,
        name=name,
    )(slots, *lefts, right)


def down_grad_kernel(slot_ref, left_ref, right_ref, own_ref, send_ref):
    half, groups, rows, packed = own_ref.shape
    width = packed // groups
    value = contract_rows(left_ref[0], right_ref[...]).astype(jnp.bfloat16)
    each = 2 * half // groups
    fold = value.shape[0] // (each * rows)
    for part in range(each):
        slot = slot_ref[pl.program_id(0) * each + part]
        base = part * fold * rows
        for f in range(groups):
            block = jnp.concatenate(
                [
                    value[base + g * rows : base + (g + 1) * rows, f * width : (f + 1) * width]
                    for g in range(fold)
                ],
                axis=1,
            )
            store_slot(slot, own_ref, send_ref, (f,), block)


def down_slot_grad(slots, left, right, parts, part_rows):
    groups, rows, packed = left.shape
    half = jax.ShapeDtypeStruct((parts // 2, groups, part_rows, packed), jnp.bfloat16)
    out = pl.BlockSpec((parts // 2, groups, part_rows, packed), lambda f, s: (0, 0, 0, 0))
    return pl.pallas_call(
        down_grad_kernel,
        grid_spec=pltpu.PrefetchScalarGridSpec(
            num_scalar_prefetch=1,
            grid=(groups,),
            in_specs=[
                pl.BlockSpec((1, rows, packed), lambda f, s: (f, 0, 0)),
                pl.BlockSpec((rows, packed), lambda f, s: (0, 0)),
            ],
            out_specs=[out, out],
        ),
        out_shape=[half, half],
        compiler_params=params(),
        cost_estimate=SHORT,
        name="down_grad",
    )(slots, left, right)


def add_kernel(one_ref, two_ref, three_ref, four_ref, came_ref, *outs):
    places = ((outs[0], (0,)), (outs[1], (0,)), (outs[2], (1, 0)), (outs[2], (0, 0)))
    for k, (mine, (out, at)) in enumerate(
        zip((one_ref, two_ref, three_ref, four_ref), places)
    ):
        total = mine[0, 0].astype(jnp.float32) + came_ref[k, 0].astype(jnp.float32)
        out[at] = total.astype(jnp.bfloat16)


def add_halves(own, came):
    half, groups, rows, packed = own.shape
    single = pl.BlockSpec((1, rows, packed), lambda f: (f, 0, 0))
    one = jax.ShapeDtypeStruct((groups, rows, packed), jnp.bfloat16)
    return pl.pallas_call(
        add_kernel,
        grid=(groups,),
        in_specs=[
            pl.BlockSpec((1, 1, rows, packed), lambda f, k=k: (k, f, 0, 0)) for k in range(half)
        ]
        + [pl.BlockSpec((half, 1, rows, packed), lambda f: (0, f, 0, 0))],
        out_specs=[single, single, pl.BlockSpec((2, 1, rows, packed), lambda f: (0, f, 0, 0))],
        out_shape=[one, one, jax.ShapeDtypeStruct((2, groups, rows, packed), jnp.bfloat16)],
        compiler_params=params(),
        cost_estimate=SHORT,
        name="add_halves",
    )(*([own] * half), came)


def unpack_kernel(part_ref, *refs):
    *pieces, out_ref, held, sems = refs
    step = pl.program_id(0)
    _, groups, rows, packed = held.shape
    width = packed // groups

    @pl.when(step == 0)
    def _():
        for j, piece in enumerate(pieces):
            pltpu.make_async_copy(piece, held.at[j], sems.at[j]).start()

    pltpu.make_async_copy(pieces[0], held.at[step], sems.at[step]).wait()
    for g in range(out_ref.shape[0] // rows):
        out_ref[g * rows : (g + 1) * rows, :] = jnp.concatenate(
            [held[step, f][:, g * width : (g + 1) * width] for f in range(groups)], axis=1
        )


def unpack_pieces(part_of, pieces, fold):
    groups, rows, width = pieces[0].shape
    parts = len(pieces)
    return pl.pallas_call(
        unpack_kernel,
        grid_spec=pltpu.PrefetchScalarGridSpec(
            num_scalar_prefetch=1,
            grid=(parts,),
            in_specs=[pl.BlockSpec(memory_space=pl.ANY)] * parts,
            out_specs=pl.BlockSpec((fold * rows, width), lambda j, p: (p[j], 0)),
            scratch_shapes=[
                pltpu.VMEM((parts, groups, rows, width), pieces[0].dtype),
                pltpu.SemaphoreType.DMA((parts,)),
            ],
        ),
        out_shape=jax.ShapeDtypeStruct((parts * fold * rows, width), pieces[0].dtype),
        compiler_params=params(),
        cost_estimate=SHORT,
        name="unpack_pieces",
    )(part_of, *pieces)


NEAR = ((0, 2, 4, 6), (0, 4, 2, 6))


def is_cube():
    return lax.axis_size("dp") == 8 and lax.axis_size("fsdp") == 4


def part_tables():
    part_of = np.zeros((8, 8), np.int32)
    slot_of = np.zeros((8, 8), np.int32)
    for part in range(8):
        core = part & 1
        order = [part ^ m for m in NEAR[core]] + [part ^ 1 ^ m for m in NEAR[1 - core]]
        part_of[part] = order
        for slot, other in enumerate(order):
            slot_of[part, other] = slot
    own = lax.axis_index("dp")
    pick = lambda table: lax.dynamic_slice(jnp.asarray(table), (own, 0), (1, 8))[0]
    return pick(part_of), pick(slot_of)


def swap(value, hop):
    return lax.ppermute(value, "dp", [(i, i ^ NEAR[i & 1][hop]) for i in range(8)])


def swap_core(value):
    return lax.ppermute(value, "dp", [(i, i ^ 1) for i in range(8)])


def after(value, *others):
    return lax.optimization_barrier((value, *others))[0]


class Gather:
    def __init__(self, shard, queue=None, behind=None, ready=None, between=None):
        if queue is not None:
            shard = after(shard, queue.group)
        self.group = own = lax.all_gather(shard, "fsdp", axis=0, tiled=False)
        if behind is not None:
            own = after(own, behind.first)
        if ready is not None:
            own = after(own, ready)
        self.first = swap(own, 1)
        self.second = swap(own, 2)
        third = self.first if between is None else after(self.first, between)
        self.third = swap(third, 2)
        near = [own, self.first, self.second, self.third]
        self.pieces = near + [swap_core(piece) for piece in near]


class Scatter:
    def __init__(self, own, send):
        self.own = own
        self.came = swap_core(send)

    def near(self, *gates):
        self.zero, self.one, pair = add_halves(after(self.own, *gates), self.came)
        self.far = swap(pair, 2)
        return pair

    def back(self):
        one = self.one.astype(jnp.float32) + self.far[0].astype(jnp.float32)
        one = one.astype(jnp.bfloat16)
        self.last = swap(one, 1)
        return one

    def total(self, *gates):
        zero = after(self.zero, *gates)
        total = zero.astype(jnp.float32) + self.far[1].astype(jnp.float32)
        self.sum = (total + self.last.astype(jnp.float32)).astype(jnp.bfloat16)
        return self.sum

    def end(self):
        return lax.psum_scatter(self.sum, "fsdp", scatter_dimension=0, tiled=False)


def swap_bit(value, axis, bit):
    size = lax.axis_size(axis)
    return lax.ppermute(value, axis, [(i, i ^ (1 << bit)) for i in range(size)])


def bit_of(axis, bit):
    return (lax.axis_index(axis) >> bit) & 1 == 1


def small_gather(value, axis):
    if not is_cube():
        return lax.all_gather(value, axis, axis=0, tiled=True)
    for bit in range(lax.axis_size(axis).bit_length() - 1):
        other = swap_bit(value, axis, bit)
        value = jnp.where(
            bit_of(axis, bit),
            jnp.concatenate([other, value], axis=0),
            jnp.concatenate([value, other], axis=0),
        )
    return value


def small_scatter(value, axis):
    if not is_cube():
        return lax.psum_scatter(value, axis, scatter_dimension=0, tiled=True)
    for bit in reversed(range(lax.axis_size(axis).bit_length() - 1)):
        half = value.shape[0] // 2
        high = bit_of(axis, bit)
        keep = jnp.where(high, value[half:], value[:half])
        value = keep + swap_bit(jnp.where(high, value[:half], value[half:]), axis, bit)
    return value


def small_sum(value, axis):
    if not is_cube():
        return lax.psum(value, axis)
    for bit in range(lax.axis_size(axis).bit_length() - 1):
        value = value + swap_bit(value, axis, bit)
    return value


def gather_shards(shard):
    rows, width = shard.shape
    groups, parts = lax.axis_size("fsdp"), lax.axis_size("dp")
    full = lax.all_gather(shard, ("fsdp", "dp"), axis=0, tiled=True)
    return full.reshape(groups, parts, rows, width)


def scatter_sum(terms):
    groups, parts, rows, width = terms.shape
    return lax.psum_scatter(
        terms.reshape(groups * parts * rows, width),
        ("fsdp", "dp"),
        scatter_dimension=0,
        tiled=True,
    )


def pack_down(natural, groups, parts, rows):
    total, width = natural.shape
    split = natural.reshape(parts, total // (parts * rows), rows, groups, width // groups)
    return split.transpose(3, 0, 2, 1, 4).reshape(groups, parts, rows, width)


def unpack_down(packed, fold):
    groups, parts, rows, width = packed.shape
    split = packed.reshape(groups, parts, rows, fold, width // fold)
    return split.transpose(1, 3, 2, 0, 4).reshape(parts * fold * rows, width)


def body(
    images,
    time_vector,
    timesteps,
    offset_index,
    query_weight,
    key_weight,
    value_weight,
    tquery_weight,
    tvalue_weight,
    proj_weight,
    proj_bias,
    first_gain,
    first_shift,
    second_gain,
    second_shift,
    up_weight,
    down_weight,
    up_bias,
    down_bias,
    bias_table,
    cotangent,
):
    low = jnp.bfloat16
    wide = jnp.float32
    count, tokens, width = images.shape
    rows = count * tokens
    groups, parts = lax.axis_size("fsdp"), lax.axis_size("dp")
    shard_rows, shard_cols = query_weight.shape
    group_heads, table_rows = bias_table.shape
    heads = group_heads * groups
    fold = down_weight.shape[0] // shard_rows
    own_part = lax.axis_index("dp")
    own_group = lax.axis_index("fsdp")

    wire_attn = jnp.concatenate([query_weight, key_weight, value_weight, proj_weight], axis=1)
    wire_down = jnp.concatenate(
        [down_weight[g * shard_rows : (g + 1) * shard_rows] for g in range(fold)], axis=1
    )
    small = jnp.concatenate(
        [
            proj_bias,
            first_gain,
            first_shift,
            second_gain,
            second_shift,
            down_bias,
            up_bias,
            bias_table.reshape(-1),
        ]
    )
    small = jnp.pad(small, (0, -small.shape[0] % 1024)).reshape(-1, LANES)
    time_low = (time_vector.astype(wide) + sinusoid(timesteps, width)).astype(low)
    both = jnp.concatenate([small, time_low.reshape(-1, LANES)], axis=0)
    both = small_gather(both[None], "fsdp")
    small_all = both[:, : small.shape[0]].reshape(groups, -1)
    time_all = small_gather(both[:, small.shape[0] :].reshape(groups * count, width), "dp")

    def vector_of(slot):
        return small_all[:, slot * shard_cols : (slot + 1) * shard_cols].reshape(-1).astype(wide)

    proj_b, gain_one, shift_one, gain_two, shift_two, down_b = (vector_of(i) for i in range(6))
    at = 6 * shard_cols
    up_b = small_all[:, at : at + up_bias.shape[0]].astype(wide)
    at = at + up_bias.shape[0]
    table = small_all[:, at : at + group_heads * table_rows].reshape(heads, table_rows)
    table = jnp.pad(table, ((0, 0), (0, 8 * LANES - table_rows)))
    bias = position_bias(offset_index, table)

    all_images = time_all.shape[0]
    time_cols = lax.dynamic_slice(
        time_all, (0, own_part * shard_rows), (all_images, shard_rows)
    )
    time_weight = jnp.concatenate([tquery_weight, tvalue_weight], axis=1)
    time_sum = small_scatter(matmul(time_cols, time_weight), "dp")
    time_part = small_gather(time_sum[None], "fsdp")
    time_own = lax.dynamic_slice(
        time_part, (0, own_group * count, 0), (groups, count, 2 * shard_cols)
    )
    gap = jnp.zeros((groups, count, shard_cols), wide)
    kept = -(-3 * shard_cols // LANES) * LANES
    time_add = jnp.concatenate(
        [
            time_own[:, :, :shard_cols],
            gap,
            time_own[:, :, shard_cols:],
            gap[:, :, : kept - 3 * shard_cols],
        ],
        axis=2,
    )

    cube = is_cube()
    if cube:
        part_of, slot_of = part_tables()
        attn_move = Gather(wire_attn, ready=time_own, between=bias)
        up_move = Gather(up_weight, queue=attn_move, behind=attn_move)
        down_move = Gather(wire_down, queue=attn_move, behind=up_move)
        attn_pieces, up_pieces = attn_move.pieces, up_move.pieces
        down_full = unpack_pieces(part_of, down_move.pieces, fold)
    else:
        part_of = jnp.zeros((1,), jnp.int32)
        attn_pieces = [gather_shards(wire_attn).reshape(groups, width, width)]
        up_pieces = [gather_shards(up_weight).reshape(groups, width, width)]
        down_full = unpack_down(gather_shards(wire_down), fold)

    x_rows = images.reshape(rows, width).astype(wide)
    normed, unit_one, inv_one = normalize(x_rows, gain_one, shift_one)
    normed_low = normed.astype(low)
    qkv, probs, mixed_split, proj_full, attn_full = attend(
        part_of, attn_pieces, normed_low, time_add, bias, count, tokens
    )
    if cube:
        mixed_split = after(mixed_split, down_move.first)
    mixed = mixed_split.transpose(1, 0, 2).reshape(rows, width)
    hidden = x_rows + (matmul(mixed, proj_full) + proj_b)
    second, unit_two, inv_two = normalize(hidden, gain_two, shift_two)
    second_low = second.astype(low)
    grad_low = cotangent.reshape(rows, width)
    grad_rows = grad_low.astype(wide)
    wire = (groups, parts, shard_rows, width)
    activ, slope, up_full = up_forward(part_of, up_pieces, second_low, up_b)
    grad_cols = grad_low
    if cube:
        own, send = down_slot_grad(
            slot_of,
            after(activ, down_move.third, *down_move.pieces[4:7]),
            grad_low,
            parts,
            shard_rows,
        )
        down_move = Scatter(own, send)
        grad_cols = after(grad_low, down_move.near(down_full))
    d_pre, d_second, layer_out = down_back(
        grad_cols, hidden + down_b, activ, slope, up_full, down_full
    )
    layer_out = layer_out.reshape(count, tokens, width)
    if cube:
        own, send = slot_grad(
            one_grad_kernel,
            slot_of,
            [after(second_low.T, down_move.back())],
            d_pre,
            parts,
            "up_grad",
        )
        up_move = Scatter(own, send)
        d_second = after(d_second, send, down_move.total())
    else:
        grad_down = jnp.concatenate([contract_rows(a, grad_low) for a in activ], axis=0)
        down_sum = scatter_sum(pack_down(grad_down.astype(low), groups, parts, shard_rows))
        grad_up = jnp.stack([contract_rows(second_low, d).astype(low) for d in d_pre])
        up_sum = scatter_sum(grad_up.reshape(wire))

    d_hidden = grad_rows + norm_back(d_second, unit_two, inv_two, gain_two)
    d_hidden_low = d_hidden.astype(low)
    d_mixed = times_transposed(d_hidden_low, proj_full).astype(low)
    d_mixed_split = d_mixed.reshape(rows, groups, shard_cols).transpose(1, 0, 2)
    d_hidden_split = d_hidden_low.reshape(rows, groups, shard_cols).transpose(1, 0, 2)
    if cube:
        d_mixed_split = after(d_mixed_split, up_move.near())
    d_packed, pairs = attend_back(d_mixed_split, qkv, probs, d_hidden_split)
    attn_back = attn_full
    if cube:
        normed_t = normed_low.T
        own, send = slot_grad(
            pair_grad_kernel, slot_of, [normed_t, mixed.T], d_packed, parts, "pair_grad"
        )
        down_sum = down_move.end()
        attn_move = Scatter(own, after(send, up_move.back(), down_sum))
        attn_pair = attn_move.near()
        attn_back = after(attn_full, attn_pair)
        pairs = after(pairs, attn_pair, up_move.total(attn_pair))
    else:
        cut = 3 * shard_cols
        grad_attn = jnp.stack(
            [
                jnp.concatenate(
                    [contract_rows(normed_low, d[:, :cut]), contract_rows(mixed, d[:, cut:])],
                    axis=1,
                )
                for d in d_packed
            ]
        )
        attn_sum = scatter_sum(grad_attn.astype(low).reshape(wire))

    d_time = after(d_packed, attn_back)
    d_time = jnp.sum(d_time.reshape(groups, count, tokens, width).astype(wide), axis=2)
    d_time = jnp.concatenate(
        [d_time[:, :, :shard_cols], d_time[:, :, 2 * shard_cols : 3 * shard_cols]], axis=2
    ).astype(low)
    d_time = d_time.transpose(1, 0, 2).reshape(count, groups * 2 * shard_cols)
    d_time_all = small_gather(small_gather(d_time, "fsdp"), "dp")
    d_time_cols = lax.dynamic_slice(
        d_time_all, (0, own_group * 2 * shard_cols), (all_images, 2 * shard_cols)
    )
    time_grads = contract_rows(time_cols, d_time_cols)
    tquery_grad = time_grads[:, :shard_cols]
    tvalue_grad = time_grads[:, shard_cols:]
    back = times_transposed(d_time_cols, time_weight)
    back = back.reshape(parts, groups, count, shard_rows).transpose(1, 0, 2, 3)
    back = back.reshape(groups, -1, LANES)

    lane = lax.broadcasted_iota(jnp.int32, (1, width), 1)
    d_normed = jnp.zeros((rows, width), wide)
    for g in range(groups):
        part = jnp.where(lane < 3 * shard_cols, d_packed[g], jnp.zeros((), low))
        d_normed = d_normed + times_transposed(part, attn_back[g])
    d_input = d_hidden + norm_back(d_normed, unit_one, inv_one, gain_one)
    images_grad = d_input.astype(low).reshape(count, tokens, width)

    table_sum = table_gradient(offset_index, pairs).reshape(heads, 8 * LANES)[:, :table_rows]

    def rows_sum(value):
        return jnp.sum(value, axis=0).reshape(groups, -1)

    vectors = [
        rows_sum(d_hidden_low.astype(wide)),
        rows_sum(d_normed * unit_one),
        rows_sum(d_normed),
        rows_sum(d_second * unit_two),
        rows_sum(d_second),
        rows_sum(grad_rows),
        jnp.sum(d_pre.astype(wide), axis=1),
        table_sum.reshape(groups, group_heads * table_rows),
    ]
    flat = jnp.concatenate(vectors, axis=1)
    flat = jnp.pad(flat, ((0, 0), (0, -flat.shape[1] % 1024))).reshape(groups, -1, LANES)
    lines = flat.shape[1]
    own = small_scatter(jnp.concatenate([flat, back], axis=1), "fsdp")[0]
    slots = jnp.where(
        lax.broadcasted_iota(jnp.int32, (parts, 1, 1), 0) == own_part, own[None, lines:], 0.0
    )
    own = small_sum(
        jnp.concatenate([own[:lines], slots.reshape(-1, LANES)], axis=0), "dp"
    )
    back = own[lines:].reshape(parts, parts, count, shard_rows)
    back = lax.dynamic_slice(back, (0, own_part, 0, 0), (parts, 1, count, shard_rows))
    time_grad = back.reshape(parts, count, shard_rows).transpose(1, 0, 2).reshape(count, width)
    own = own[:lines].reshape(-1)
    proj_bg, gain1_g, shift1_g, gain2_g, shift2_g, down_bg = (
        own[i * shard_cols : (i + 1) * shard_cols] for i in range(6)
    )
    at = 6 * shard_cols
    up_bg = own[at : at + up_bias.shape[0]]
    at = at + up_bias.shape[0]
    table_grad = own[at : at + group_heads * table_rows].reshape(group_heads, table_rows)

    if cube:
        attn_move.back()
        attn_total = attn_move.total()
        down_sum = after(down_sum, attn_total)
        up_sum = after(up_move.end(), attn_total)
        attn_sum = attn_move.end()
    attn_sum = attn_sum.astype(wide)
    query_grad, key_grad, value_grad, proj_grad = (
        attn_sum[:, i * shard_cols : (i + 1) * shard_cols] for i in range(4)
    )
    down_sum = down_sum.astype(wide)
    down_grad = jnp.concatenate(
        [down_sum[:, g * shard_cols : (g + 1) * shard_cols] for g in range(fold)], axis=0
    )
    return (
        layer_out,
        images_grad,
        time_grad,
        query_grad,
        key_grad,
        value_grad,
        tquery_grad,
        tvalue_grad,
        proj_grad,
        proj_bg,
        gain1_g,
        shift1_g,
        gain2_g,
        shift2_g,
        up_sum.astype(wide),
        down_grad,
        up_bg,
        down_bg,
        table_grad,
    )


def solution(mesh):
    rows = P(BOTH, None, None)
    matrix = P("dp", "fsdp")
    vector = P("fsdp")
    table = P("fsdp", None)
    return jax.shard_map(
        body,
        mesh=mesh,
        in_specs=(
            (rows, P(BOTH, None), P(BOTH), P())
            + (matrix,) * 6
            + (vector,) * 5
            + (matrix,) * 2
            + (vector,) * 2
            + (table, rows)
        ),
        out_specs=(
            (rows, rows, P(BOTH, None))
            + (matrix,) * 6
            + (vector,) * 5
            + (matrix,) * 2
            + (vector,) * 2
            + (table,)
        ),
        check_vma=False,
    )
```

```python
import math

import jax
import jax.numpy as jnp
import numpy as np
from jax import lax
from jax.experimental import pallas as pl
from jax.experimental.pallas import tpu as pltpu
from jax.sharding import PartitionSpec as P

LANES = 128
BOTH = ("dp", "fsdp")
VMEM_LIMIT = 58 * 1024 * 1024


def lasting(microseconds):
    return pl.CostEstimate(
        flops=int(microseconds * 1e9), transcendentals=0, bytes_accessed=1
    )


def sinusoid(steps, model_width):
    half_width = model_width // 2
    frequency = jnp.exp(
        -math.log(10000.0) * jnp.arange(half_width).astype(jnp.float32) / half_width
    )
    angles = steps.astype(jnp.float32)[:, None] * frequency[None, :]
    return jnp.concatenate([jnp.sin(angles), jnp.cos(angles)], axis=1)


def matmul(left, right):
    return jnp.dot(left, right, preferred_element_type=jnp.float32)


def contract_rows(left, right):
    return lax.dot_general(
        left, right, (((0,), (0,)), ((), ())), preferred_element_type=jnp.float32
    )


def times_transposed(left, right):
    return lax.dot_general(
        left, right, (((1,), (1,)), ((), ())), preferred_element_type=jnp.float32
    )


def normalize(values, gain, shift):
    row_mean = jnp.mean(values, axis=-1, keepdims=True)
    centered = values - row_mean
    inv_std = lax.rsqrt(jnp.mean(centered * centered, axis=-1, keepdims=True) + 1e-06)
    unit_rows = centered * inv_std
    return (unit_rows * gain + shift, unit_rows, inv_std)


def norm_back(grad_rows, unit_rows, inv_std, gain):
    scaled = grad_rows * gain
    return inv_std * (
        scaled
        - jnp.mean(scaled, axis=-1, keepdims=True)
        - unit_rows * jnp.mean(scaled * unit_rows, axis=-1, keepdims=True)
    )


def gelu_slope(pre_act):
    return 0.5 * (1.0 + lax.erf(pre_act * (1.0 / math.sqrt(2.0)))) + pre_act * jnp.exp(
        -0.5 * pre_act * pre_act
    ) * (1.0 / math.sqrt(2.0 * math.pi))


def params(count=1):
    return pltpu.CompilerParams(
        dimension_semantics=("arbitrary",) * count, vmem_limit_bytes=VMEM_LIMIT
    )


def bias_kernel(index_ref, table_ref, bias_ref):
    heads, rows, tokens = bias_ref.shape
    chunks = table_ref.shape[2] // LANES
    pieces = [
        [
            jnp.broadcast_to(table_ref[h, :, c * LANES : (c + 1) * LANES], (8, LANES))
            for c in range(chunks)
        ]
        for h in range(heads)
    ]

    def some_rows(step, carry):
        at = pl.multiple_of(step * 8, 8)
        for col in range(tokens // LANES):
            lanes = slice(col * LANES, (col + 1) * LANES)
            index = index_ref[pl.ds(at, 8), lanes]
            low = index & (LANES - 1)
            high = index >> 7
            hits = [high == c for c in range(chunks)]
            for h in range(heads):
                found = jnp.take_along_axis(pieces[h][0], low, axis=1)
                for c in range(1, chunks):
                    found = jnp.where(
                        hits[c], jnp.take_along_axis(pieces[h][c], low, axis=1), found
                    )
                bias_ref[h, pl.ds(at, 8), lanes] = found
        return carry

    lax.fori_loop(0, rows // 8, some_rows, 0)


def position_bias(index, table):
    heads, padded = table.shape
    tokens = index.shape[0]
    group = heads // 4
    return pl.pallas_call(
        bias_kernel,
        grid=(4,),
        in_specs=[
            pl.BlockSpec((tokens, tokens), lambda f: (0, 0)),
            pl.BlockSpec((group, 1, padded), lambda f: (f, 0, 0)),
        ],
        out_specs=pl.BlockSpec((group, tokens, tokens), lambda f: (f, 0, 0)),
        out_shape=jax.ShapeDtypeStruct((heads, tokens, tokens), jnp.float32),
        compiler_params=params(),
        cost_estimate=lasting(20),
        name="position_bias",
    )(index, table.astype(jnp.float32).reshape(heads, 1, padded))


def table_kernel(index_ref, pairs_ref, out_ref):
    heads = pairs_ref.shape[0]
    tokens = index_ref.shape[1]
    rows = index_ref.shape[0]

    @pl.when(pl.program_id(0) == 0)
    def _():
        out_ref[...] = jnp.zeros_like(out_ref)

    sub = lax.broadcasted_iota(jnp.int32, (8, tokens), 0)
    lane_of = lax.broadcasted_iota(jnp.int32, (LANES, tokens), 0)

    def row_terms(row):
        index = index_ref[pl.ds(row, 1), :]
        low = jnp.broadcast_to(index & (LANES - 1), (LANES, tokens))
        high = jnp.broadcast_to(index >> 7, (8, tokens))
        hit = sub == high
        left = jnp.concatenate(
            [
                jnp.where(hit, jnp.broadcast_to(pairs_ref[h, pl.ds(row, 1), :], (8, tokens)), 0.0)
                for h in range(heads)
            ],
            axis=0,
        ).astype(jnp.bfloat16)
        right = jnp.where(lane_of == low, 1.0, 0.0).astype(jnp.bfloat16)
        return left, right

    def some_rows(step, total):
        terms = [row_terms(step * 4 + k) for k in range(4)]
        left = jnp.concatenate([t[0] for t in terms], axis=1)
        right = jnp.concatenate([t[1] for t in terms], axis=1)
        return total + times_transposed(left, right)

    out_ref[...] += lax.fori_loop(
        0, rows // 4, some_rows, jnp.zeros((heads * 8, LANES), jnp.float32)
    )


def table_gradient(index, pairs):
    heads, tokens, _ = pairs.shape
    block = 64
    return pl.pallas_call(
        table_kernel,
        grid=(tokens // block,),
        in_specs=[
            pl.BlockSpec((block, tokens), lambda i: (i, 0)),
            pl.BlockSpec((heads, block, tokens), lambda i: (0, i, 0)),
        ],
        out_specs=pl.BlockSpec((heads * 8, LANES), lambda i: (0, 0)),
        out_shape=jax.ShapeDtypeStruct((heads * 8, LANES), jnp.float32),
        compiler_params=params(),
        cost_estimate=lasting(18),
        name="table_gradient",
    )(index, pairs)


def piece_list(refs):
    out = []
    for ref in refs:
        out.extend([ref] if len(ref.shape) == 3 else [ref.at[k] for k in range(ref.shape[0])])
    return out


def piece_shape(refs):
    count = sum(1 if len(ref.shape) == 3 else ref.shape[0] for ref in refs)
    return (count, *refs[0].shape)


def load_group(part_ref, refs, held, in_sems, full_ref, out_sems):
    step = pl.program_id(0)
    pieces = piece_list(refs)
    rows = pieces[0].shape[1]

    def copy(group, j):
        at = pl.multiple_of(part_ref[j] * rows, 16)
        return pltpu.make_async_copy(
            pieces[j].at[group], held.at[group, pl.ds(at, rows)], in_sems.at[group, j]
        )

    @pl.when(step == 0)
    def _():
        for group in range(held.shape[0]):
            for j in range(len(pieces)):
                copy(group, j).start()

    for j in range(len(pieces)):
        copy(step, j).wait()
    pltpu.make_async_copy(held.at[step], full_ref.at[step], out_sems.at[step]).start()


def finish_groups(held, full_ref, out_sems):
    @pl.when(pl.program_id(0) == held.shape[0] - 1)
    def _():
        for group in range(held.shape[0]):
            pltpu.make_async_copy(held.at[group], full_ref.at[group], out_sems.at[group]).wait()


def piece_call(kernel, name, part_of, pieces, inputs, in_specs, out_specs, out_shapes):
    parts, groups, rows, packed = piece_shape(pieces)
    depth = rows * parts
    full = jax.ShapeDtypeStruct((groups, depth, packed), pieces[0].dtype)
    anywhere = pl.BlockSpec(memory_space=pl.ANY)
    return pl.pallas_call(
        kernel,
        grid_spec=pltpu.PrefetchScalarGridSpec(
            num_scalar_prefetch=1,
            grid=(groups,),
            in_specs=in_specs + [anywhere] * len(pieces),
            out_specs=out_specs + [anywhere],
            scratch_shapes=[
                pltpu.VMEM((groups, depth, packed), pieces[0].dtype),
                pltpu.SemaphoreType.DMA((groups, parts)),
                pltpu.SemaphoreType.DMA((groups,)),
            ],
        ),
        out_shape=out_shapes + [full],
        compiler_params=params(),
        cost_estimate=lasting(13),
        name=name,
    )(part_of, *inputs, *pieces)


def attend_kernel(part_ref, normed_ref, add_ref, bias_ref, *refs):
    *pieces, qkv_ref, probs_ref, mixed_ref, proj_ref, full_ref, held, in_sems, out_sems = refs
    images, heads = probs_ref.shape[1], probs_ref.shape[2]
    tokens = probs_ref.shape[3]
    width = mixed_ref.shape[2]
    size = width // heads
    scale = 1.0 / math.sqrt(size)
    kept = qkv_ref.shape[2]
    step = pl.program_id(0)
    load_group(part_ref, pieces, held, in_sems, full_ref, out_sems)
    for image in range(images):
        rows = slice(image * tokens, (image + 1) * tokens)
        acc = matmul(normed_ref[rows, :], held[step, :, :kept])
        qkv_ref[0, rows, :] = (acc + add_ref[0, image : image + 1, :]).astype(jnp.bfloat16)
    for image in range(images):
        rows = slice(image * tokens, (image + 1) * tokens)
        both = qkv_ref[0, rows, :]
        outs = []
        for head in range(heads):
            at = head * size
            query = both[:, at : at + size]
            keys = both[:, width + at : width + at + size]
            values = both[:, 2 * width + at : 2 * width + at + size]
            scores = times_transposed(query, keys) * scale + bias_ref[head]
            peak = jnp.max(scores, axis=-1, keepdims=True)
            expo = jnp.exp(scores - peak)
            total = jnp.sum(expo, axis=-1, keepdims=True)
            probs = (expo / total).astype(jnp.bfloat16)
            probs_ref[0, image, head] = probs
            outs.append(matmul(probs, values))
        mixed_ref[0, rows, :] = jnp.concatenate(outs, axis=1).astype(jnp.bfloat16)
    for group in range(held.shape[0]):

        @pl.when(step == group)
        def _(group=group):
            proj_ref[:, group * width : (group + 1) * width] = held[group, :, 3 * width :]

    finish_groups(held, full_ref, out_sems)


def attend(part_of, pieces, normed, add, bias, images, tokens):
    parts, groups, part_rows, packed = piece_shape(pieces)
    depth = part_rows * parts
    heads = bias.shape[0] // groups
    width = packed // groups
    kept = add.shape[2]
    rows = images * tokens
    low = jnp.bfloat16
    return piece_call(
        attend_kernel,
        "attend",
        part_of,
        pieces,
        [normed, add, bias],
        [
            pl.BlockSpec((rows, depth), lambda f, p: (0, 0)),
            pl.BlockSpec((1, images, kept), lambda f, p: (f, 0, 0)),
            pl.BlockSpec((heads, tokens, tokens), lambda f, p: (f, 0, 0)),
        ],
        [
            pl.BlockSpec((1, rows, kept), lambda f, p: (f, 0, 0)),
            pl.BlockSpec((1, images, heads, tokens, tokens), lambda f, p: (f, 0, 0, 0, 0)),
            pl.BlockSpec((1, rows, width), lambda f, p: (f, 0, 0)),
            pl.BlockSpec((depth, packed), lambda f, p: (0, 0)),
        ],
        [
            jax.ShapeDtypeStruct((groups, rows, kept), low),
            jax.ShapeDtypeStruct((groups, images, heads, tokens, tokens), low),
            jax.ShapeDtypeStruct((groups, rows, width), low),
            jax.ShapeDtypeStruct((depth, packed), low),
        ],
    )


def up_kernel(part_ref, second_ref, bias_ref, *refs):
    *pieces, activ_ref, slope_ref, full_ref, held, in_sems, out_sems = refs
    load_group(part_ref, pieces, held, in_sems, full_ref, out_sems)
    weight = held[pl.program_id(0)]
    block = 256
    for start in range(0, second_ref.shape[0], block):
        rows = slice(start, start + block)
        pre = matmul(second_ref[rows, :], weight) + bias_ref[0]
        below = 0.5 * (1.0 + lax.erf(pre * (1.0 / math.sqrt(2.0))))
        density = jnp.exp(-0.5 * pre * pre) * (1.0 / math.sqrt(2.0 * math.pi))
        activ_ref[0, rows, :] = (pre * below).astype(jnp.bfloat16)
        slope_ref[0, rows, :] = (below + pre * density).astype(jnp.bfloat16)
    finish_groups(held, full_ref, out_sems)


def up_forward(part_of, pieces, second, bias):
    _, groups, _, packed = piece_shape(pieces)
    rows, depth = second.shape
    wide = pl.BlockSpec((1, rows, packed), lambda f, p: (f, 0, 0))
    shape = jax.ShapeDtypeStruct((groups, rows, packed), jnp.bfloat16)
    return piece_call(
        up_kernel,
        "up_forward",
        part_of,
        pieces,
        [second, bias.reshape(groups, 1, packed)],
        [
            pl.BlockSpec((rows, depth), lambda f, p: (0, 0)),
            pl.BlockSpec((1, 1, packed), lambda f, p: (f, 0, 0)),
        ],
        [wide, wide],
        [shape, shape],
    )


def column_sum(value):
    return jnp.sum(value, axis=0, keepdims=True)


def down_back_kernel(
    grad_ref,
    hidden_ref,
    row_ref,
    activ_ref,
    slope_ref,
    up_ref,
    down_ref,
    pre_ref,
    out_ref,
    d_hidden_ref,
    d_low_ref,
    sum_ref,
    up_sum_ref,
    total,
    second,
):
    step = pl.program_id(0)
    weight = down_ref[...]
    d_activ = times_transposed(grad_ref[...], weight)
    d_pre = (d_activ * slope_ref[0].astype(jnp.float32)).astype(jnp.bfloat16)
    pre_ref[0] = d_pre
    up_sum_ref[0] = column_sum(d_pre.astype(jnp.float32))
    part = times_transposed(d_pre, up_ref[0])
    more = matmul(activ_ref[0], weight)

    @pl.when(step == 0)
    def _():
        second[...] = part
        total[...] = more

    @pl.when(step > 0)
    def _():
        second[...] += part
        total[...] += more

    @pl.when(step == pl.num_programs(0) - 1)
    def _():
        block = 64
        gain, shift = row_ref[0:1, :], row_ref[1:2, :]
        sum_ref[...] = jnp.zeros_like(sum_ref)

        def some_rows(at, carry):
            rows = pl.ds(pl.multiple_of(at * block, block), block)
            hidden = hidden_ref[rows, :]
            out_ref[rows, :] = (hidden + shift + total[rows, :]).astype(jnp.bfloat16)
            _, unit, inv = normalize(hidden, gain, 0.0)
            d_second = second[rows, :]
            grad = grad_ref[rows, :].astype(jnp.float32)
            d_hidden = grad + norm_back(d_second, unit, inv, gain)
            d_low = d_hidden.astype(jnp.bfloat16)
            d_hidden_ref[rows, :] = d_hidden
            d_low_ref[rows, :] = d_low
            sum_ref[0:1, :] += column_sum(d_low.astype(jnp.float32))
            sum_ref[1:2, :] += column_sum(d_second * unit)
            sum_ref[2:3, :] += column_sum(d_second)
            sum_ref[3:4, :] += column_sum(grad)
            return carry

        lax.fori_loop(0, hidden_ref.shape[0] // block, some_rows, 0)


def down_back(grad, hidden, lines, activ, slope, up_full, down_full):
    groups, rows, packed = activ.shape
    depth = up_full.shape[1]
    whole = pl.BlockSpec((rows, depth), lambda f: (0, 0))
    mine = pl.BlockSpec((1, rows, packed), lambda f: (f, 0, 0))
    few = pl.BlockSpec((8, depth), lambda f: (0, 0))
    return pl.pallas_call(
        down_back_kernel,
        grid=(groups,),
        in_specs=[
            whole,
            whole,
            few,
            mine,
            mine,
            pl.BlockSpec((1, depth, packed), lambda f: (f, 0, 0)),
            pl.BlockSpec((packed, depth), lambda f: (f, 0)),
        ],
        out_specs=[
            mine,
            whole,
            whole,
            whole,
            few,
            pl.BlockSpec((1, 1, packed), lambda f: (f, 0, 0)),
        ],
        out_shape=[
            jax.ShapeDtypeStruct((groups, rows, packed), jnp.bfloat16),
            jax.ShapeDtypeStruct((rows, depth), jnp.bfloat16),
            jax.ShapeDtypeStruct((rows, depth), jnp.float32),
            jax.ShapeDtypeStruct((rows, depth), jnp.bfloat16),
            jax.ShapeDtypeStruct((8, depth), jnp.float32),
            jax.ShapeDtypeStruct((groups, 1, packed), jnp.float32),
        ],
        scratch_shapes=[
            pltpu.VMEM((rows, depth), jnp.float32),
            pltpu.VMEM((rows, depth), jnp.float32),
        ],
        compiler_params=params(),
        cost_estimate=lasting(33),
        name="down_back",
    )(grad, hidden, lines, activ, slope, up_full, down_full)


def attend_back_kernel(
    hidden_ref, proj_ref, qkv_ref, probs_ref, out_ref, pairs_ref, time_ref
):
    images, heads = probs_ref.shape[1], probs_ref.shape[2]
    tokens = probs_ref.shape[3]
    width = proj_ref.shape[0]
    size = width // heads
    scale = 1.0 / math.sqrt(size)
    for image in range(images):
        rows = slice(image * tokens, (image + 1) * tokens)
        both = qkv_ref[0, rows, :]
        grads = times_transposed(hidden_ref[rows, :], proj_ref[...]).astype(jnp.bfloat16)
        d_query, d_keys, d_values = [], [], []
        for head in range(heads):
            at = head * size
            query = both[:, at : at + size]
            keys = both[:, width + at : width + at + size]
            values = both[:, 2 * width + at : 2 * width + at + size]
            grad = grads[:, at : at + size]
            probs_low = probs_ref[0, image, head]
            probs = probs_low.astype(jnp.float32)
            d_values.append(contract_rows(probs_low, grad))
            d_probs = times_transposed(grad, values)
            moved = probs * d_probs
            d_scores = moved - probs * jnp.sum(moved, axis=-1, keepdims=True)
            d_low = d_scores.astype(jnp.bfloat16)
            if image == 0:
                pairs_ref[head] = d_low.astype(jnp.float32)
            else:
                pairs_ref[head] += d_low.astype(jnp.float32)
            d_query.append(matmul(d_low, keys) * scale)
            d_keys.append(contract_rows(d_low, query) * scale)
        packed = jnp.concatenate(d_query + d_keys + d_values, axis=1).astype(jnp.bfloat16)
        out_ref[0, rows, : 3 * width] = packed
        time_ref[0, image : image + 1, :] = column_sum(packed.astype(jnp.float32))
    for group in range(hidden_ref.shape[1] // width):

        @pl.when(pl.program_id(0) == group)
        def _(group=group):
            out_ref[0, :, 3 * width :] = hidden_ref[:, group * width : (group + 1) * width]


def attend_back(hidden, proj, qkv, probs):
    rows, packed = hidden.shape
    groups, images, heads, tokens, _ = probs.shape
    kept = qkv.shape[2]
    width = packed // groups
    return pl.pallas_call(
        attend_back_kernel,
        grid=(groups,),
        in_specs=[
            pl.BlockSpec((rows, packed), lambda f: (0, 0)),
            pl.BlockSpec((width, packed), lambda f: (f, 0)),
            pl.BlockSpec((1, rows, kept), lambda f: (f, 0, 0)),
            pl.BlockSpec((1, images, heads, tokens, tokens), lambda f: (f, 0, 0, 0, 0)),
        ],
        out_specs=[
            pl.BlockSpec((1, rows, packed), lambda f: (f, 0, 0)),
            pl.BlockSpec((heads, tokens, tokens), lambda f: (f, 0, 0)),
            pl.BlockSpec((1, images, 3 * width), lambda f: (f, 0, 0)),
        ],
        out_shape=[
            jax.ShapeDtypeStruct((groups, rows, packed), jnp.bfloat16),
            jax.ShapeDtypeStruct((groups * heads, tokens, tokens), jnp.float32),
            jax.ShapeDtypeStruct((groups, images, 3 * width), jnp.float32),
        ],
        compiler_params=params(),
        cost_estimate=lasting(19),
        name="attend_back",
    )(hidden, proj, qkv, probs)


def input_grad_kernel(
    right_ref, weight_ref, image_ref, d_hidden_ref, row_ref, out_ref, sum_ref, total
):
    step = pl.program_id(0)
    cut = 3 * (right_ref.shape[2] // 4)
    kept = -(-cut // LANES) * LANES
    lane = lax.broadcasted_iota(jnp.int32, (1, kept), 1)
    right = right_ref[0, :, :kept]
    right = jnp.where(lane < cut, right.astype(jnp.float32), 0.0).astype(jnp.bfloat16)
    part = times_transposed(right, weight_ref[0, :, :kept])

    @pl.when(step == 0)
    def _():
        total[...] = part

    @pl.when(step > 0)
    def _():
        total[...] += part

    @pl.when(step == pl.num_programs(0) - 1)
    def _():
        block = 64
        gain = row_ref[0:1, :]
        sum_ref[...] = jnp.zeros_like(sum_ref)

        def some_rows(at, carry):
            rows = pl.ds(pl.multiple_of(at * block, block), block)
            _, unit, inv = normalize(image_ref[rows, :].astype(jnp.float32), gain, 0.0)
            d_normed = total[rows, :]
            d_input = d_hidden_ref[rows, :] + norm_back(d_normed, unit, inv, gain)
            out_ref[rows, :] = d_input.astype(jnp.bfloat16)
            sum_ref[0:1, :] += column_sum(d_normed * unit)
            sum_ref[1:2, :] += column_sum(d_normed)
            return carry

        lax.fori_loop(0, image_ref.shape[0] // block, some_rows, 0)


def input_grad(right, weight, images, d_hidden, lines):
    groups, rows, packed = right.shape
    whole = pl.BlockSpec((rows, packed), lambda f: (0, 0))
    few = pl.BlockSpec((8, packed), lambda f: (0, 0))
    return pl.pallas_call(
        input_grad_kernel,
        grid=(groups,),
        in_specs=[
            pl.BlockSpec((1, rows, packed), lambda f: (f, 0, 0)),
            pl.BlockSpec((1, packed, packed), lambda f: (f, 0, 0)),
            whole,
            whole,
            few,
        ],
        out_specs=[whole, few],
        out_shape=[
            jax.ShapeDtypeStruct((rows, packed), jnp.bfloat16),
            jax.ShapeDtypeStruct((8, packed), jnp.float32),
        ],
        scratch_shapes=[pltpu.VMEM((rows, packed), jnp.float32)],
        compiler_params=params(),
        cost_estimate=lasting(13),
        name="input_grad",
    )(right, weight, images, d_hidden, lines)


def store_slot(slot, own_ref, send_ref, at, value):
    half = own_ref.shape[0]

    @pl.when(slot < half)
    def _():
        own_ref[(slot,) + at] = value

    @pl.when(slot >= half)
    def _():
        send_ref[(slot - half,) + at] = value


def pair_grad_kernel(slot_ref, one_ref, two_ref, right_ref, own_ref, send_ref):
    cut = 3 * (right_ref.shape[2] // 4)
    below = cut // LANES * LANES
    above = below + LANES
    rows = own_ref.shape[2]
    right = right_ref[0]
    lane = lax.broadcasted_iota(jnp.int32, (rows, LANES), 1)
    first = matmul(one_ref[...], right[:, :above])
    last = matmul(two_ref[...], right[:, below:])
    for part in range(2 * own_ref.shape[0]):
        at = slice(part * rows, (part + 1) * rows)
        value = jnp.concatenate(
            [
                first[at, :below],
                jnp.where(lane < cut - below, first[at, below:], last[at, :LANES]),
                last[at, LANES:],
            ],
            axis=1,
        ).astype(jnp.bfloat16)
        store_slot(slot_ref[part], own_ref, send_ref, (0,), value)


def one_grad_kernel(slot_ref, one_ref, right_ref, own_ref, send_ref):
    rows = own_ref.shape[2]
    first = matmul(one_ref[...], right_ref[0])
    for part in range(2 * own_ref.shape[0]):
        value = first[part * rows : (part + 1) * rows].astype(jnp.bfloat16)
        store_slot(slot_ref[part], own_ref, send_ref, (0,), value)


def slot_grad(kernel, slots, lefts, right, parts, name):
    groups, rows, packed = right.shape
    depth = lefts[0].shape[0]
    half = jax.ShapeDtypeStruct((parts // 2, groups, depth // parts, packed), jnp.bfloat16)
    out = pl.BlockSpec((parts // 2, 1, depth // parts, packed), lambda f, s: (0, f, 0, 0))
    return pl.pallas_call(
        kernel,
        grid_spec=pltpu.PrefetchScalarGridSpec(
            num_scalar_prefetch=1,
            grid=(groups,),
            in_specs=[pl.BlockSpec((depth, rows), lambda f, s: (0, 0)) for _ in lefts]
            + [pl.BlockSpec((1, rows, packed), lambda f, s: (f, 0, 0))],
            out_specs=[out, out],
        ),
        out_shape=[half, half],
        compiler_params=params(),
        cost_estimate=lasting(18),
        name=name,
    )(slots, *lefts, right)


def down_grad_kernel(slot_ref, left_ref, right_ref, own_ref, send_ref):
    half, groups, rows, packed = own_ref.shape
    width = packed // groups
    value = contract_rows(left_ref[0], right_ref[...]).astype(jnp.bfloat16)
    each = 2 * half // groups
    fold = value.shape[0] // (each * rows)
    for part in range(each):
        slot = slot_ref[pl.program_id(0) * each + part]
        base = part * fold * rows
        for f in range(groups):
            block = jnp.concatenate(
                [
                    value[base + g * rows : base + (g + 1) * rows, f * width : (f + 1) * width]
                    for g in range(fold)
                ],
                axis=1,
            )
            store_slot(slot, own_ref, send_ref, (f,), block)


def down_slot_grad(slots, left, right, parts, part_rows):
    groups, rows, packed = left.shape
    half = jax.ShapeDtypeStruct((parts // 2, groups, part_rows, packed), jnp.bfloat16)
    out = pl.BlockSpec((parts // 2, groups, part_rows, packed), lambda f, s: (0, 0, 0, 0))
    return pl.pallas_call(
        down_grad_kernel,
        grid_spec=pltpu.PrefetchScalarGridSpec(
            num_scalar_prefetch=1,
            grid=(groups,),
            in_specs=[
                pl.BlockSpec((1, rows, packed), lambda f, s: (f, 0, 0)),
                pl.BlockSpec((rows, packed), lambda f, s: (0, 0)),
            ],
            out_specs=[out, out],
        ),
        out_shape=[half, half],
        compiler_params=params(),
        cost_estimate=lasting(18),
        name="down_grad",
    )(slots, left, right)


def add_kernel(one_ref, two_ref, three_ref, four_ref, came_ref, *outs):
    places = ((outs[0], (0,)), (outs[1], (0,)), (outs[2], (1, 0)), (outs[2], (0, 0)))
    for k, (mine, (out, at)) in enumerate(
        zip((one_ref, two_ref, three_ref, four_ref), places)
    ):
        total = mine[0, 0].astype(jnp.float32) + came_ref[k, 0].astype(jnp.float32)
        out[at] = total.astype(jnp.bfloat16)


def add_halves(own, came):
    half, groups, rows, packed = own.shape
    single = pl.BlockSpec((1, rows, packed), lambda f: (f, 0, 0))
    one = jax.ShapeDtypeStruct((groups, rows, packed), jnp.bfloat16)
    return pl.pallas_call(
        add_kernel,
        grid=(groups,),
        in_specs=[
            pl.BlockSpec((1, 1, rows, packed), lambda f, k=k: (k, f, 0, 0)) for k in range(half)
        ]
        + [pl.BlockSpec((half, 1, rows, packed), lambda f: (0, f, 0, 0))],
        out_specs=[single, single, pl.BlockSpec((2, 1, rows, packed), lambda f: (0, f, 0, 0))],
        out_shape=[one, one, jax.ShapeDtypeStruct((2, groups, rows, packed), jnp.bfloat16)],
        compiler_params=params(),
        cost_estimate=lasting(7),
        name="add_halves",
    )(*([own] * half), came)


def unpack_kernel(part_ref, *refs):
    *pieces, out_ref, held, sems = refs
    pieces = piece_list(pieces)
    step = pl.program_id(0)
    _, groups, rows, packed = held.shape
    width = packed // groups

    @pl.when(step == 0)
    def _():
        for j, piece in enumerate(pieces):
            pltpu.make_async_copy(piece, held.at[j], sems.at[j]).start()

    pltpu.make_async_copy(pieces[0], held.at[step], sems.at[step]).wait()
    for g in range(out_ref.shape[0] // rows):
        out_ref[g * rows : (g + 1) * rows, :] = jnp.concatenate(
            [held[step, f][:, g * width : (g + 1) * width] for f in range(groups)], axis=1
        )


def unpack_pieces(part_of, pieces, fold):
    parts, groups, rows, width = piece_shape(pieces)
    return pl.pallas_call(
        unpack_kernel,
        grid_spec=pltpu.PrefetchScalarGridSpec(
            num_scalar_prefetch=1,
            grid=(parts,),
            in_specs=[pl.BlockSpec(memory_space=pl.ANY)] * len(pieces),
            out_specs=pl.BlockSpec((fold * rows, width), lambda j, p: (p[j], 0)),
            scratch_shapes=[
                pltpu.VMEM((parts, groups, rows, width), pieces[0].dtype),
                pltpu.SemaphoreType.DMA((parts,)),
            ],
        ),
        out_shape=jax.ShapeDtypeStruct((parts * fold * rows, width), pieces[0].dtype),
        compiler_params=params(),
        cost_estimate=lasting(9),
        name="unpack_pieces",
    )(part_of, *pieces)


NEAR = ((0, 2, 4, 6), (0, 4, 2, 6))


def is_cube():
    return lax.axis_size("dp") == 8 and lax.axis_size("fsdp") == 4


def part_tables():
    part_of = np.zeros((8, 8), np.int32)
    slot_of = np.zeros((8, 8), np.int32)
    for part in range(8):
        core = part & 1
        order = [part ^ m for m in NEAR[core]] + [part ^ 1 ^ m for m in NEAR[1 - core]]
        part_of[part] = order
        for slot, other in enumerate(order):
            slot_of[part, other] = slot
    own = lax.axis_index("dp")
    pick = lambda table: lax.dynamic_slice(jnp.asarray(table), (own, 0), (1, 8))[0]
    return pick(part_of), pick(slot_of)


def swap(value, hop):
    return lax.ppermute(value, "dp", [(i, i ^ NEAR[i & 1][hop]) for i in range(8)])


def swap_core(value):
    return lax.ppermute(value, "dp", [(i, i ^ 1) for i in range(8)])


def after(value, *others):
    return lax.optimization_barrier((value, *others))[0]


class Gather:
    def __init__(self, group, ahead=None, *gates):
        own, again = group, group
        if ahead is not None:
            own = after(own, ahead.second)
            again = after(again, ahead.third, *gates)
        self.first = swap(own, 1)
        self.second = swap(again, 2)
        self.third = swap(self.first, 2)
        self.near = [group, self.first, self.second, self.third]

    def pieces(self, *gates):
        late = [after(piece, *gates) if gates else piece for piece in self.near[2:]]
        return self.near + [swap_core(piece) for piece in self.near[:2] + late]


class Scatter:
    def __init__(self, own, send):
        self.own = own
        self.came = swap_core(send)

    def near(self, *gates):
        self.zero, self.one, pair = add_halves(after(self.own, *gates), self.came)
        self.far = swap(pair, 2)
        return pair

    def back(self):
        one = self.one.astype(jnp.float32) + self.far[0].astype(jnp.float32)
        one = one.astype(jnp.bfloat16)
        self.last = swap(one, 1)
        return one

    def total(self, *gates):
        zero = after(self.zero, *gates)
        total = zero.astype(jnp.float32) + self.far[1].astype(jnp.float32)
        self.sum = (total + self.last.astype(jnp.float32)).astype(jnp.bfloat16)
        return self.sum

    def end(self):
        return lax.psum_scatter(self.sum, "fsdp", scatter_dimension=0, tiled=False)


def swap_bit(value, axis, bit):
    size = lax.axis_size(axis)
    return lax.ppermute(value, axis, [(i, i ^ (1 << bit)) for i in range(size)])


def bit_of(axis, bit):
    return (lax.axis_index(axis) >> bit) & 1 == 1


def small_gather(value, axis):
    if not is_cube():
        return lax.all_gather(value, axis, axis=0, tiled=True)
    for bit in range(lax.axis_size(axis).bit_length() - 1):
        other = swap_bit(value, axis, bit)
        value = jnp.where(
            bit_of(axis, bit),
            jnp.concatenate([other, value], axis=0),
            jnp.concatenate([value, other], axis=0),
        )
    return value


def small_scatter(value, axis):
    if not is_cube():
        return lax.psum_scatter(value, axis, scatter_dimension=0, tiled=True)
    for bit in reversed(range(lax.axis_size(axis).bit_length() - 1)):
        half = value.shape[0] // 2
        high = bit_of(axis, bit)
        keep = jnp.where(high, value[half:], value[:half])
        value = keep + swap_bit(jnp.where(high, value[:half], value[half:]), axis, bit)
    return value


def small_sum(value, axis):
    if not is_cube():
        return lax.psum(value, axis)
    for bit in range(lax.axis_size(axis).bit_length() - 1):
        value = value + swap_bit(value, axis, bit)
    return value


def gather_shards(shard):
    rows, width = shard.shape
    groups, parts = lax.axis_size("fsdp"), lax.axis_size("dp")
    full = lax.all_gather(shard, ("fsdp", "dp"), axis=0, tiled=True)
    return full.reshape(groups, parts, rows, width)


def scatter_sum(terms):
    groups, parts, rows, width = terms.shape
    return lax.psum_scatter(
        terms.reshape(groups * parts * rows, width),
        ("fsdp", "dp"),
        scatter_dimension=0,
        tiled=True,
    )


def pack_down(natural, groups, parts, rows):
    total, width = natural.shape
    split = natural.reshape(parts, total // (parts * rows), rows, groups, width // groups)
    return split.transpose(3, 0, 2, 1, 4).reshape(groups, parts, rows, width)


def unpack_down(packed, fold):
    groups, parts, rows, width = packed.shape
    split = packed.reshape(groups, parts, rows, fold, width // fold)
    return split.transpose(1, 3, 2, 0, 4).reshape(parts * fold * rows, width)


def body(
    images,
    time_vector,
    timesteps,
    offset_index,
    query_weight,
    key_weight,
    value_weight,
    tquery_weight,
    tvalue_weight,
    proj_weight,
    proj_bias,
    first_gain,
    first_shift,
    second_gain,
    second_shift,
    up_weight,
    down_weight,
    up_bias,
    down_bias,
    bias_table,
    cotangent,
):
    low = jnp.bfloat16
    wide = jnp.float32
    count, tokens, width = images.shape
    rows = count * tokens
    groups, parts = lax.axis_size("fsdp"), lax.axis_size("dp")
    shard_rows, shard_cols = query_weight.shape
    group_heads, table_rows = bias_table.shape
    heads = group_heads * groups
    fold = down_weight.shape[0] // shard_rows
    own_part = lax.axis_index("dp")
    own_group = lax.axis_index("fsdp")

    wire_attn = jnp.concatenate([query_weight, key_weight, value_weight, proj_weight], axis=1)
    wire_down = jnp.concatenate(
        [down_weight[g * shard_rows : (g + 1) * shard_rows] for g in range(fold)], axis=1
    )
    small = jnp.concatenate(
        [
            proj_bias,
            first_gain,
            first_shift,
            second_gain,
            second_shift,
            down_bias,
            up_bias,
            bias_table.reshape(-1),
        ]
    )
    small = jnp.pad(small, (0, -small.shape[0] % 1024)).reshape(-1, LANES)
    time_low = (time_vector.astype(wide) + sinusoid(timesteps, width)).astype(low)
    both = jnp.concatenate([small, time_low.reshape(-1, LANES)], axis=0)
    both = small_gather(both[None], "fsdp")
    small_all = both[:, : small.shape[0]].reshape(groups, -1)

    def vector_of(slot):
        return small_all[:, slot * shard_cols : (slot + 1) * shard_cols].reshape(-1).astype(wide)

    proj_b, gain_one, shift_one, gain_two, shift_two, down_b = (vector_of(i) for i in range(6))
    at = 6 * shard_cols
    up_b = small_all[:, at : at + up_bias.shape[0]].astype(wide)
    at = at + up_bias.shape[0]
    table = small_all[:, at : at + group_heads * table_rows].reshape(heads, table_rows)
    table = jnp.pad(table, ((0, 0), (0, 8 * LANES - table_rows)))
    bias = position_bias(offset_index, table)

    time_rows = both[:, small.shape[0] :].reshape(groups * count, width)
    time_weight = small_gather(jnp.concatenate([tquery_weight, tvalue_weight], axis=1), "dp")
    time_part = small_gather(matmul(time_rows, time_weight)[None], "fsdp")
    time_own = lax.dynamic_slice(
        time_part, (0, own_group * count, 0), (groups, count, 2 * shard_cols)
    )
    gap = jnp.zeros((groups, count, shard_cols), wide)
    kept = -(-3 * shard_cols // LANES) * LANES
    time_add = jnp.concatenate(
        [
            time_own[:, :, :shard_cols],
            gap,
            time_own[:, :, shard_cols:],
            gap[:, :, : kept - 3 * shard_cols],
        ],
        axis=2,
    )

    cube = is_cube()
    if cube:
        part_of, slot_of = part_tables()
        attn_group = lax.all_gather(wire_attn, "fsdp", axis=0, tiled=False)
        wire_rest = after(jnp.stack([up_weight, wire_down]), both)
        rest = lax.all_gather(wire_rest, "fsdp", axis=1, tiled=False)
        attn_move = Gather(after(attn_group, time_weight))
        up_move = Gather(after(rest[0], bias), attn_move)
        attn_pieces = attn_move.pieces()
    else:
        part_of = jnp.zeros((1,), jnp.int32)
        attn_pieces = [gather_shards(wire_attn).reshape(groups, width, width)]
        up_pieces = [gather_shards(up_weight).reshape(groups, width, width)]
        down_full = unpack_down(gather_shards(wire_down), fold)

    x_rows = images.reshape(rows, width).astype(wide)
    normed, _, _ = normalize(x_rows, gain_one, shift_one)
    normed_low = normed.astype(low)
    qkv, probs, mixed_split, proj_full, attn_full = attend(
        part_of, attn_pieces, normed_low, time_add, bias, count, tokens
    )
    if cube:
        up_pieces = up_move.pieces(mixed_split)
        down_move = Gather(rest[1], up_move, mixed_split)
        mixed_split = after(mixed_split, down_move.first)
    mixed = mixed_split.transpose(1, 0, 2).reshape(rows, width)
    hidden = x_rows + (matmul(mixed, proj_full) + proj_b)
    second, _, _ = normalize(hidden, gain_two, shift_two)
    second_low = second.astype(low)
    grad_low = cotangent.reshape(rows, width)
    wire = (groups, parts, shard_rows, width)
    activ, slope, up_full = up_forward(part_of, up_pieces, second_low, up_b)
    grad_cols = grad_low
    if cube:
        down_pieces = down_move.pieces(activ)
        down_full = unpack_pieces(part_of, down_pieces, fold)
        own, send = down_slot_grad(
            slot_of,
            after(activ, *down_pieces),
            grad_low,
            parts,
            shard_rows,
        )
        down_move = Scatter(own, send)
        grad_cols = after(grad_low, down_move.near(down_full))
    def lines_of(*values):
        return jnp.concatenate([jnp.stack(values), jnp.zeros((8 - len(values), width), wide)])

    d_pre, layer_out, d_hidden, d_hidden_low, down_sums, up_sums = down_back(
        grad_cols, hidden, lines_of(gain_two, down_b), activ, slope, up_full, down_full
    )
    layer_out = layer_out.reshape(count, tokens, width)
    d_hidden_cols = d_hidden_low
    if cube:
        own, send = slot_grad(
            one_grad_kernel,
            slot_of,
            [after(second_low.T, down_move.back())],
            d_pre,
            parts,
            "up_grad",
        )
        up_move = Scatter(own, after(send, down_move.last))
        d_hidden_cols = after(d_hidden_low, send, down_move.total())
    else:
        grad_down = jnp.concatenate([contract_rows(a, grad_low) for a in activ], axis=0)
        down_sum = scatter_sum(pack_down(grad_down.astype(low), groups, parts, shard_rows))
        grad_up = jnp.stack([contract_rows(second_low, d).astype(low) for d in d_pre])
        up_sum = scatter_sum(grad_up.reshape(wire))

    if cube:
        d_hidden_cols = after(d_hidden_cols, up_move.near())
    d_packed, pairs, d_time = attend_back(d_hidden_cols, proj_full, qkv, probs)
    attn_back = attn_full
    if cube:
        normed_t = after(normed_low.T, up_move.back())
        own, send = slot_grad(
            pair_grad_kernel, slot_of, [normed_t, mixed.T], d_packed, parts, "pair_grad"
        )
        down_sum = down_move.end()
        attn_move = Scatter(own, after(send, up_move.last))
        up_total = up_move.total()
        attn_pair = attn_move.near(up_total)
        attn_back = after(attn_full, attn_pair)
        pairs = after(pairs, attn_move.back())
        attn_total = attn_move.total()
    else:
        cut = 3 * shard_cols
        grad_attn = jnp.stack(
            [
                jnp.concatenate(
                    [contract_rows(normed_low, d[:, :cut]), contract_rows(mixed, d[:, cut:])],
                    axis=1,
                )
                for d in d_packed
            ]
        )
        attn_sum = scatter_sum(grad_attn.astype(low).reshape(wire))

    images_grad, input_sums = input_grad(
        d_packed, attn_back, images.reshape(rows, width), d_hidden, lines_of(gain_one)
    )
    images_grad = images_grad.reshape(count, tokens, width)

    d_time = after(d_time, images_grad)
    d_time = jnp.concatenate(
        [d_time[:, :, :shard_cols], d_time[:, :, 2 * shard_cols : 3 * shard_cols]], axis=2
    ).astype(low)
    d_time = d_time.transpose(1, 0, 2).reshape(count, groups * 2 * shard_cols)
    d_time_rows = small_gather(d_time, "fsdp")
    d_time_cols = lax.dynamic_slice(
        d_time_rows, (0, own_group * 2 * shard_cols), (groups * count, 2 * shard_cols)
    )
    time_grads = small_scatter(contract_rows(time_rows, d_time_cols).astype(low), "dp")
    back = times_transposed(d_time_cols, time_weight).reshape(-1, LANES)

    table_sum = table_gradient(offset_index, pairs)
    vectors = jnp.concatenate(
        [down_sums[:4], input_sums[:2], up_sums.reshape(groups, width)]
    ).reshape(-1, LANES)
    flat = jnp.concatenate([vectors, table_sum, back], axis=0)
    ends = (vectors.shape[0], vectors.shape[0] + table_sum.shape[0])
    flat = small_sum(flat, "fsdp")
    time_grad = lax.dynamic_slice(
        flat[ends[1] :].reshape(groups * count, width), (own_group * count, 0), (count, width)
    )
    flat = small_sum(flat[: ends[1]], "dp")
    vectors = flat[: ends[0]].reshape(-1, width)
    own = lax.dynamic_slice(vectors, (0, own_group * shard_cols), (6, shard_cols))
    proj_bg, gain2_g, shift2_g, down_bg, gain1_g, shift1_g = (own[i] for i in range(6))
    up_bg = lax.dynamic_slice(vectors, (6 + own_group, 0), (1, width))[0]
    table_grad = lax.dynamic_slice(
        flat[ends[0] : ends[1]], (own_group * group_heads * 8, 0), (group_heads * 8, LANES)
    )
    table_grad = table_grad.reshape(group_heads, 8 * LANES)[:, :table_rows]

    if cube:
        down_sum = after(down_sum, attn_total)
        up_sum = after(up_move.end(), attn_total)
        attn_sum = attn_move.end()
    time_grads = time_grads.astype(wide)
    tquery_grad, tvalue_grad = time_grads[:, :shard_cols], time_grads[:, shard_cols:]
    attn_sum = attn_sum.astype(wide)
    query_grad, key_grad, value_grad, proj_grad = (
        attn_sum[:, i * shard_cols : (i + 1) * shard_cols] for i in range(4)
    )
    down_sum = down_sum.astype(wide)
    down_grad = jnp.concatenate(
        [down_sum[:, g * shard_cols : (g + 1) * shard_cols] for g in range(fold)], axis=0
    )
    return (
        layer_out,
        images_grad,
        time_grad,
        query_grad,
        key_grad,
        value_grad,
        tquery_grad,
        tvalue_grad,
        proj_grad,
        proj_bg,
        gain1_g,
        shift1_g,
        gain2_g,
        shift2_g,
        up_sum.astype(wide),
        down_grad,
        up_bg,
        down_bg,
        table_grad,
    )


def solution(mesh):
    rows = P(BOTH, None, None)
    matrix = P("dp", "fsdp")
    vector = P("fsdp")
    table = P("fsdp", None)
    return jax.shard_map(
        body,
        mesh=mesh,
        in_specs=(
            (rows, P(BOTH, None), P(BOTH), P())
            + (matrix,) * 6
            + (vector,) * 5
            + (matrix,) * 2
            + (vector,) * 2
            + (table, rows)
        ),
        out_specs=(
            (rows, rows, P(BOTH, None))
            + (matrix,) * 6
            + (vector,) * 5
            + (matrix,) * 2
            + (vector,) * 2
            + (table,)
        ),
        check_vma=False,
    )
```

```python
import math

import jax
import jax.numpy as jnp
import numpy as np
from jax import lax
from jax.experimental import pallas as pl
from jax.experimental.pallas import tpu as pltpu
from jax.sharding import PartitionSpec as P

LANES = 128
BOTH = ("dp", "fsdp")
VMEM_LIMIT = 58 * 1024 * 1024


def lasting(microseconds):
    return pl.CostEstimate(
        flops=int(microseconds * 1e9), transcendentals=0, bytes_accessed=1
    )


def sinusoid(steps, model_width):
    half_width = model_width // 2
    frequency = jnp.exp(
        -math.log(10000.0) * jnp.arange(half_width).astype(jnp.float32) / half_width
    )
    angles = steps.astype(jnp.float32)[:, None] * frequency[None, :]
    return jnp.concatenate([jnp.sin(angles), jnp.cos(angles)], axis=1)


def matmul(left, right):
    return jnp.dot(left, right, preferred_element_type=jnp.float32)


def contract_rows(left, right):
    return lax.dot_general(
        left, right, (((0,), (0,)), ((), ())), preferred_element_type=jnp.float32
    )


def times_transposed(left, right):
    return lax.dot_general(
        left, right, (((1,), (1,)), ((), ())), preferred_element_type=jnp.float32
    )


def normalize(values, gain, shift):
    row_mean = jnp.mean(values, axis=-1, keepdims=True)
    centered = values - row_mean
    inv_std = lax.rsqrt(jnp.mean(centered * centered, axis=-1, keepdims=True) + 1e-06)
    unit_rows = centered * inv_std
    return (unit_rows * gain + shift, unit_rows, inv_std)


def norm_back(grad_rows, unit_rows, inv_std, gain):
    scaled = grad_rows * gain
    return inv_std * (
        scaled
        - jnp.mean(scaled, axis=-1, keepdims=True)
        - unit_rows * jnp.mean(scaled * unit_rows, axis=-1, keepdims=True)
    )


def gelu_slope(pre_act):
    return 0.5 * (1.0 + lax.erf(pre_act * (1.0 / math.sqrt(2.0)))) + pre_act * jnp.exp(
        -0.5 * pre_act * pre_act
    ) * (1.0 / math.sqrt(2.0 * math.pi))


def params(count=1):
    return pltpu.CompilerParams(
        dimension_semantics=("arbitrary",) * count, vmem_limit_bytes=VMEM_LIMIT
    )


def bias_kernel(index_ref, table_ref, bias_ref):
    heads, rows, tokens = bias_ref.shape
    chunks = table_ref.shape[2] // LANES
    pieces = [
        [
            jnp.broadcast_to(table_ref[h, :, c * LANES : (c + 1) * LANES], (8, LANES))
            for c in range(chunks)
        ]
        for h in range(heads)
    ]

    def some_rows(step, carry):
        at = pl.multiple_of(step * 8, 8)
        for col in range(tokens // LANES):
            lanes = slice(col * LANES, (col + 1) * LANES)
            index = index_ref[pl.ds(at, 8), lanes]
            low = index & (LANES - 1)
            high = index >> 7
            hits = [high == c for c in range(chunks)]
            for h in range(heads):
                found = jnp.take_along_axis(pieces[h][0], low, axis=1)
                for c in range(1, chunks):
                    found = jnp.where(
                        hits[c], jnp.take_along_axis(pieces[h][c], low, axis=1), found
                    )
                bias_ref[h, pl.ds(at, 8), lanes] = found
        return carry

    lax.fori_loop(0, rows // 8, some_rows, 0)


def position_bias(index, table):
    heads, padded = table.shape
    tokens = index.shape[0]
    group = heads // 4
    return pl.pallas_call(
        bias_kernel,
        grid=(4,),
        in_specs=[
            pl.BlockSpec((tokens, tokens), lambda f: (0, 0)),
            pl.BlockSpec((group, 1, padded), lambda f: (f, 0, 0)),
        ],
        out_specs=pl.BlockSpec((group, tokens, tokens), lambda f: (f, 0, 0)),
        out_shape=jax.ShapeDtypeStruct((heads, tokens, tokens), jnp.float32),
        compiler_params=params(),
        cost_estimate=lasting(20),
        name="position_bias",
    )(index, table.astype(jnp.float32).reshape(heads, 1, padded))


def table_kernel(index_ref, pairs_ref, out_ref):
    heads = pairs_ref.shape[0]
    tokens = index_ref.shape[1]
    rows = index_ref.shape[0]

    @pl.when(pl.program_id(0) == 0)
    def _():
        out_ref[...] = jnp.zeros_like(out_ref)

    sub = lax.broadcasted_iota(jnp.int32, (8, tokens), 0)
    lane_of = lax.broadcasted_iota(jnp.int32, (LANES, tokens), 0)

    def row_terms(row):
        index = index_ref[pl.ds(row, 1), :]
        low = jnp.broadcast_to(index & (LANES - 1), (LANES, tokens))
        high = jnp.broadcast_to(index >> 7, (8, tokens))
        hit = sub == high
        left = jnp.concatenate(
            [
                jnp.where(hit, jnp.broadcast_to(pairs_ref[h, pl.ds(row, 1), :], (8, tokens)), 0.0)
                for h in range(heads)
            ],
            axis=0,
        ).astype(jnp.bfloat16)
        right = jnp.where(lane_of == low, 1.0, 0.0).astype(jnp.bfloat16)
        return left, right

    def some_rows(step, total):
        terms = [row_terms(step * 4 + k) for k in range(4)]
        left = jnp.concatenate([t[0] for t in terms], axis=1)
        right = jnp.concatenate([t[1] for t in terms], axis=1)
        return total + times_transposed(left, right)

    out_ref[...] += lax.fori_loop(
        0, rows // 4, some_rows, jnp.zeros((heads * 8, LANES), jnp.float32)
    )


def table_gradient(index, pairs):
    heads, tokens, _ = pairs.shape
    block = 64
    return pl.pallas_call(
        table_kernel,
        grid=(tokens // block,),
        in_specs=[
            pl.BlockSpec((block, tokens), lambda i: (i, 0)),
            pl.BlockSpec((heads, block, tokens), lambda i: (0, i, 0)),
        ],
        out_specs=pl.BlockSpec((heads * 8, LANES), lambda i: (0, 0)),
        out_shape=jax.ShapeDtypeStruct((heads * 8, LANES), jnp.float32),
        compiler_params=params(),
        cost_estimate=lasting(18),
        name="table_gradient",
    )(index, pairs)


def piece_list(refs):
    out = []
    for ref in refs:
        out.extend([ref] if len(ref.shape) == 3 else [ref.at[k] for k in range(ref.shape[0])])
    return out


def piece_shape(refs):
    count = sum(1 if len(ref.shape) == 3 else ref.shape[0] for ref in refs)
    return (count, *refs[0].shape)


def load_group(part_ref, refs, held, in_sems, full_ref, out_sems):
    step = pl.program_id(0)
    pieces = piece_list(refs)
    rows = pieces[0].shape[1]

    def copy(group, j):
        at = pl.multiple_of(part_ref[j] * rows, 16)
        return pltpu.make_async_copy(
            pieces[j].at[group], held.at[group, pl.ds(at, rows)], in_sems.at[group, j]
        )

    @pl.when(step == 0)
    def _():
        for group in range(held.shape[0]):
            for j in range(len(pieces)):
                copy(group, j).start()

    for j in range(len(pieces)):
        copy(step, j).wait()
    pltpu.make_async_copy(held.at[step], full_ref.at[step], out_sems.at[step]).start()


def finish_groups(held, full_ref, out_sems):
    @pl.when(pl.program_id(0) == held.shape[0] - 1)
    def _():
        for group in range(held.shape[0]):
            pltpu.make_async_copy(held.at[group], full_ref.at[group], out_sems.at[group]).wait()


def piece_call(kernel, name, part_of, pieces, inputs, in_specs, out_specs, out_shapes):
    parts, groups, rows, packed = piece_shape(pieces)
    depth = rows * parts
    full = jax.ShapeDtypeStruct((groups, depth, packed), pieces[0].dtype)
    anywhere = pl.BlockSpec(memory_space=pl.ANY)
    return pl.pallas_call(
        kernel,
        grid_spec=pltpu.PrefetchScalarGridSpec(
            num_scalar_prefetch=1,
            grid=(groups,),
            in_specs=in_specs + [anywhere] * len(pieces),
            out_specs=out_specs + [anywhere],
            scratch_shapes=[
                pltpu.VMEM((groups, depth, packed), pieces[0].dtype),
                pltpu.SemaphoreType.DMA((groups, parts)),
                pltpu.SemaphoreType.DMA((groups,)),
            ],
        ),
        out_shape=out_shapes + [full],
        compiler_params=params(),
        cost_estimate=lasting(13),
        name=name,
    )(part_of, *inputs, *pieces)


def attend_kernel(part_ref, normed_ref, add_ref, bias_ref, *refs):
    *pieces, qkv_ref, probs_ref, mixed_ref, proj_ref, full_ref, held, in_sems, out_sems = refs
    images, heads = probs_ref.shape[1], probs_ref.shape[2]
    tokens = probs_ref.shape[3]
    width = mixed_ref.shape[2]
    size = width // heads
    scale = 1.0 / math.sqrt(size)
    kept = qkv_ref.shape[2]
    step = pl.program_id(0)
    load_group(part_ref, pieces, held, in_sems, full_ref, out_sems)
    for image in range(images):
        rows = slice(image * tokens, (image + 1) * tokens)
        acc = matmul(normed_ref[rows, :], held[step, :, :kept])
        qkv_ref[0, rows, :] = (acc + add_ref[0, image : image + 1, :]).astype(jnp.bfloat16)
    for image in range(images):
        rows = slice(image * tokens, (image + 1) * tokens)
        both = qkv_ref[0, rows, :]
        outs = []
        for head in range(heads):
            at = head * size
            query = both[:, at : at + size]
            keys = both[:, width + at : width + at + size]
            values = both[:, 2 * width + at : 2 * width + at + size]
            scores = times_transposed(query, keys) * scale + bias_ref[head]
            peak = jnp.max(scores, axis=-1, keepdims=True)
            expo = jnp.exp(scores - peak)
            total = jnp.sum(expo, axis=-1, keepdims=True)
            probs = (expo / total).astype(jnp.bfloat16)
            probs_ref[0, image, head] = probs
            outs.append(matmul(probs, values))
        mixed_ref[0, rows, :] = jnp.concatenate(outs, axis=1).astype(jnp.bfloat16)
    for group in range(held.shape[0]):

        @pl.when(step == group)
        def _(group=group):
            proj_ref[:, group * width : (group + 1) * width] = held[group, :, 3 * width :]

    finish_groups(held, full_ref, out_sems)


def attend(part_of, pieces, normed, add, bias, images, tokens):
    parts, groups, part_rows, packed = piece_shape(pieces)
    depth = part_rows * parts
    heads = bias.shape[0] // groups
    width = packed // groups
    kept = add.shape[2]
    rows = images * tokens
    low = jnp.bfloat16
    return piece_call(
        attend_kernel,
        "attend",
        part_of,
        pieces,
        [normed, add, bias],
        [
            pl.BlockSpec((rows, depth), lambda f, p: (0, 0)),
            pl.BlockSpec((1, images, kept), lambda f, p: (f, 0, 0)),
            pl.BlockSpec((heads, tokens, tokens), lambda f, p: (f, 0, 0)),
        ],
        [
            pl.BlockSpec((1, rows, kept), lambda f, p: (f, 0, 0)),
            pl.BlockSpec((1, images, heads, tokens, tokens), lambda f, p: (f, 0, 0, 0, 0)),
            pl.BlockSpec((1, rows, width), lambda f, p: (f, 0, 0)),
            pl.BlockSpec((depth, packed), lambda f, p: (0, 0)),
        ],
        [
            jax.ShapeDtypeStruct((groups, rows, kept), low),
            jax.ShapeDtypeStruct((groups, images, heads, tokens, tokens), low),
            jax.ShapeDtypeStruct((groups, rows, width), low),
            jax.ShapeDtypeStruct((depth, packed), low),
        ],
    )


def up_kernel(part_ref, second_ref, bias_ref, *refs):
    *pieces, activ_ref, slope_ref, full_ref, held, in_sems, out_sems = refs
    load_group(part_ref, pieces, held, in_sems, full_ref, out_sems)
    weight = held[pl.program_id(0)]
    block = 256
    for start in range(0, second_ref.shape[0], block):
        rows = slice(start, start + block)
        pre = matmul(second_ref[rows, :], weight) + bias_ref[0]
        below = 0.5 * (1.0 + lax.erf(pre * (1.0 / math.sqrt(2.0))))
        density = jnp.exp(-0.5 * pre * pre) * (1.0 / math.sqrt(2.0 * math.pi))
        activ_ref[0, rows, :] = (pre * below).astype(jnp.bfloat16)
        slope_ref[0, rows, :] = (below + pre * density).astype(jnp.bfloat16)
    finish_groups(held, full_ref, out_sems)


def up_forward(part_of, pieces, second, bias):
    _, groups, _, packed = piece_shape(pieces)
    rows, depth = second.shape
    wide = pl.BlockSpec((1, rows, packed), lambda f, p: (f, 0, 0))
    shape = jax.ShapeDtypeStruct((groups, rows, packed), jnp.bfloat16)
    return piece_call(
        up_kernel,
        "up_forward",
        part_of,
        pieces,
        [second, bias.reshape(groups, 1, packed)],
        [
            pl.BlockSpec((rows, depth), lambda f, p: (0, 0)),
            pl.BlockSpec((1, 1, packed), lambda f, p: (f, 0, 0)),
        ],
        [wide, wide],
        [shape, shape],
    )


def column_sum(value):
    return jnp.sum(value, axis=0, keepdims=True)


def down_back_kernel(
    grad_ref,
    hidden_ref,
    row_ref,
    activ_ref,
    slope_ref,
    up_ref,
    down_ref,
    pre_ref,
    out_ref,
    d_hidden_ref,
    d_low_ref,
    sum_ref,
    up_sum_ref,
    total,
    second,
):
    step = pl.program_id(0)
    weight = down_ref[...]
    d_activ = times_transposed(grad_ref[...], weight)
    d_pre = (d_activ * slope_ref[0].astype(jnp.float32)).astype(jnp.bfloat16)
    pre_ref[0] = d_pre
    up_sum_ref[0] = column_sum(d_pre.astype(jnp.float32))
    part = times_transposed(d_pre, up_ref[0])
    more = matmul(activ_ref[0], weight)

    @pl.when(step == 0)
    def _():
        second[...] = part
        total[...] = more

    @pl.when(step > 0)
    def _():
        second[...] += part
        total[...] += more

    @pl.when(step == pl.num_programs(0) - 1)
    def _():
        block = 64
        gain, shift = row_ref[0:1, :], row_ref[1:2, :]
        sum_ref[...] = jnp.zeros_like(sum_ref)

        def some_rows(at, carry):
            rows = pl.ds(pl.multiple_of(at * block, block), block)
            hidden = hidden_ref[rows, :]
            out_ref[rows, :] = (hidden + shift + total[rows, :]).astype(jnp.bfloat16)
            _, unit, inv = normalize(hidden, gain, 0.0)
            d_second = second[rows, :]
            grad = grad_ref[rows, :].astype(jnp.float32)
            d_hidden = grad + norm_back(d_second, unit, inv, gain)
            d_low = d_hidden.astype(jnp.bfloat16)
            d_hidden_ref[rows, :] = d_hidden
            d_low_ref[rows, :] = d_low
            sum_ref[0:1, :] += column_sum(d_low.astype(jnp.float32))
            sum_ref[1:2, :] += column_sum(d_second * unit)
            sum_ref[2:3, :] += column_sum(d_second)
            sum_ref[3:4, :] += column_sum(grad)
            return carry

        lax.fori_loop(0, hidden_ref.shape[0] // block, some_rows, 0)


def down_back(grad, hidden, lines, activ, slope, up_full, down_full):
    groups, rows, packed = activ.shape
    depth = up_full.shape[1]
    whole = pl.BlockSpec((rows, depth), lambda f: (0, 0))
    mine = pl.BlockSpec((1, rows, packed), lambda f: (f, 0, 0))
    few = pl.BlockSpec((8, depth), lambda f: (0, 0))
    return pl.pallas_call(
        down_back_kernel,
        grid=(groups,),
        in_specs=[
            whole,
            whole,
            few,
            mine,
            mine,
            pl.BlockSpec((1, depth, packed), lambda f: (f, 0, 0)),
            pl.BlockSpec((packed, depth), lambda f: (f, 0)),
        ],
        out_specs=[
            mine,
            whole,
            whole,
            whole,
            few,
            pl.BlockSpec((1, 1, packed), lambda f: (f, 0, 0)),
        ],
        out_shape=[
            jax.ShapeDtypeStruct((groups, rows, packed), jnp.bfloat16),
            jax.ShapeDtypeStruct((rows, depth), jnp.bfloat16),
            jax.ShapeDtypeStruct((rows, depth), jnp.float32),
            jax.ShapeDtypeStruct((rows, depth), jnp.bfloat16),
            jax.ShapeDtypeStruct((8, depth), jnp.float32),
            jax.ShapeDtypeStruct((groups, 1, packed), jnp.float32),
        ],
        scratch_shapes=[
            pltpu.VMEM((rows, depth), jnp.float32),
            pltpu.VMEM((rows, depth), jnp.float32),
        ],
        compiler_params=params(),
        cost_estimate=lasting(33),
        name="down_back",
    )(grad, hidden, lines, activ, slope, up_full, down_full)


def attend_back_kernel(
    hidden_ref, proj_ref, qkv_ref, probs_ref, out_ref, pairs_ref, time_ref
):
    images, heads = probs_ref.shape[1], probs_ref.shape[2]
    tokens = probs_ref.shape[3]
    width = proj_ref.shape[0]
    size = width // heads
    scale = 1.0 / math.sqrt(size)
    for image in range(images):
        rows = slice(image * tokens, (image + 1) * tokens)
        both = qkv_ref[0, rows, :]
        grads = times_transposed(hidden_ref[rows, :], proj_ref[...]).astype(jnp.bfloat16)
        d_query, d_keys, d_values = [], [], []
        for head in range(heads):
            at = head * size
            query = both[:, at : at + size]
            keys = both[:, width + at : width + at + size]
            values = both[:, 2 * width + at : 2 * width + at + size]
            grad = grads[:, at : at + size]
            probs_low = probs_ref[0, image, head]
            probs = probs_low.astype(jnp.float32)
            d_values.append(contract_rows(probs_low, grad))
            d_probs = times_transposed(grad, values)
            moved = probs * d_probs
            d_scores = moved - probs * jnp.sum(moved, axis=-1, keepdims=True)
            d_low = d_scores.astype(jnp.bfloat16)
            if image == 0:
                pairs_ref[head] = d_low.astype(jnp.float32)
            else:
                pairs_ref[head] += d_low.astype(jnp.float32)
            d_query.append(matmul(d_low, keys) * scale)
            d_keys.append(contract_rows(d_low, query) * scale)
        packed = jnp.concatenate(d_query + d_keys + d_values, axis=1).astype(jnp.bfloat16)
        out_ref[0, rows, : 3 * width] = packed
        time_ref[0, image : image + 1, :] = column_sum(packed.astype(jnp.float32))
    for group in range(hidden_ref.shape[1] // width):

        @pl.when(pl.program_id(0) == group)
        def _(group=group):
            out_ref[0, :, 3 * width :] = hidden_ref[:, group * width : (group + 1) * width]


def attend_back(hidden, proj, qkv, probs):
    rows, packed = hidden.shape
    groups, images, heads, tokens, _ = probs.shape
    kept = qkv.shape[2]
    width = packed // groups
    return pl.pallas_call(
        attend_back_kernel,
        grid=(groups,),
        in_specs=[
            pl.BlockSpec((rows, packed), lambda f: (0, 0)),
            pl.BlockSpec((width, packed), lambda f: (f, 0)),
            pl.BlockSpec((1, rows, kept), lambda f: (f, 0, 0)),
            pl.BlockSpec((1, images, heads, tokens, tokens), lambda f: (f, 0, 0, 0, 0)),
        ],
        out_specs=[
            pl.BlockSpec((1, rows, packed), lambda f: (f, 0, 0)),
            pl.BlockSpec((heads, tokens, tokens), lambda f: (f, 0, 0)),
            pl.BlockSpec((1, images, 3 * width), lambda f: (f, 0, 0)),
        ],
        out_shape=[
            jax.ShapeDtypeStruct((groups, rows, packed), jnp.bfloat16),
            jax.ShapeDtypeStruct((groups * heads, tokens, tokens), jnp.float32),
            jax.ShapeDtypeStruct((groups, images, 3 * width), jnp.float32),
        ],
        compiler_params=params(),
        cost_estimate=lasting(19),
        name="attend_back",
    )(hidden, proj, qkv, probs)


def input_grad_kernel(
    right_ref, weight_ref, image_ref, d_hidden_ref, row_ref, out_ref, sum_ref, total
):
    step = pl.program_id(0)
    cut = 3 * (right_ref.shape[2] // 4)
    kept = -(-cut // LANES) * LANES
    lane = lax.broadcasted_iota(jnp.int32, (1, kept), 1)
    right = right_ref[0, :, :kept]
    right = jnp.where(lane < cut, right.astype(jnp.float32), 0.0).astype(jnp.bfloat16)
    part = times_transposed(right, weight_ref[0, :, :kept])

    @pl.when(step == 0)
    def _():
        total[...] = part

    @pl.when(step > 0)
    def _():
        total[...] += part

    @pl.when(step == pl.num_programs(0) - 1)
    def _():
        block = 64
        gain = row_ref[0:1, :]
        sum_ref[...] = jnp.zeros_like(sum_ref)

        def some_rows(at, carry):
            rows = pl.ds(pl.multiple_of(at * block, block), block)
            _, unit, inv = normalize(image_ref[rows, :].astype(jnp.float32), gain, 0.0)
            d_normed = total[rows, :]
            d_input = d_hidden_ref[rows, :] + norm_back(d_normed, unit, inv, gain)
            out_ref[rows, :] = d_input.astype(jnp.bfloat16)
            sum_ref[0:1, :] += column_sum(d_normed * unit)
            sum_ref[1:2, :] += column_sum(d_normed)
            return carry

        lax.fori_loop(0, image_ref.shape[0] // block, some_rows, 0)


def input_grad(right, weight, images, d_hidden, lines):
    groups, rows, packed = right.shape
    whole = pl.BlockSpec((rows, packed), lambda f: (0, 0))
    few = pl.BlockSpec((8, packed), lambda f: (0, 0))
    return pl.pallas_call(
        input_grad_kernel,
        grid=(groups,),
        in_specs=[
            pl.BlockSpec((1, rows, packed), lambda f: (f, 0, 0)),
            pl.BlockSpec((1, packed, packed), lambda f: (f, 0, 0)),
            whole,
            whole,
            few,
        ],
        out_specs=[whole, few],
        out_shape=[
            jax.ShapeDtypeStruct((rows, packed), jnp.bfloat16),
            jax.ShapeDtypeStruct((8, packed), jnp.float32),
        ],
        scratch_shapes=[pltpu.VMEM((rows, packed), jnp.float32)],
        compiler_params=params(),
        cost_estimate=lasting(13),
        name="input_grad",
    )(right, weight, images, d_hidden, lines)


def store_slot(slot, own_ref, send_ref, at, value):
    half = own_ref.shape[0]

    @pl.when(slot < half)
    def _():
        own_ref[(slot,) + at] = value

    @pl.when(slot >= half)
    def _():
        send_ref[(slot - half,) + at] = value


def pair_grad_kernel(slot_ref, one_ref, two_ref, right_ref, own_ref, send_ref):
    cut = 3 * (right_ref.shape[2] // 4)
    below = cut // LANES * LANES
    above = below + LANES
    rows = own_ref.shape[2]
    right = right_ref[0]
    lane = lax.broadcasted_iota(jnp.int32, (rows, LANES), 1)
    first = matmul(one_ref[...], right[:, :above])
    last = matmul(two_ref[...], right[:, below:])
    for part in range(2 * own_ref.shape[0]):
        at = slice(part * rows, (part + 1) * rows)
        value = jnp.concatenate(
            [
                first[at, :below],
                jnp.where(lane < cut - below, first[at, below:], last[at, :LANES]),
                last[at, LANES:],
            ],
            axis=1,
        ).astype(jnp.bfloat16)
        store_slot(slot_ref[part], own_ref, send_ref, (0,), value)


def one_grad_kernel(slot_ref, one_ref, right_ref, own_ref, send_ref):
    rows = own_ref.shape[2]
    first = matmul(one_ref[...], right_ref[0])
    for part in range(2 * own_ref.shape[0]):
        value = first[part * rows : (part + 1) * rows].astype(jnp.bfloat16)
        store_slot(slot_ref[part], own_ref, send_ref, (0,), value)


def slot_grad(kernel, slots, lefts, right, parts, name):
    groups, rows, packed = right.shape
    depth = lefts[0].shape[0]
    half = jax.ShapeDtypeStruct((parts // 2, groups, depth // parts, packed), jnp.bfloat16)
    out = pl.BlockSpec((parts // 2, 1, depth // parts, packed), lambda f, s: (0, f, 0, 0))
    return pl.pallas_call(
        kernel,
        grid_spec=pltpu.PrefetchScalarGridSpec(
            num_scalar_prefetch=1,
            grid=(groups,),
            in_specs=[pl.BlockSpec((depth, rows), lambda f, s: (0, 0)) for _ in lefts]
            + [pl.BlockSpec((1, rows, packed), lambda f, s: (f, 0, 0))],
            out_specs=[out, out],
        ),
        out_shape=[half, half],
        compiler_params=params(),
        cost_estimate=lasting(18),
        name=name,
    )(slots, *lefts, right)


def down_grad_kernel(slot_ref, left_ref, right_ref, own_ref, send_ref):
    half, groups, rows, packed = own_ref.shape
    width = packed // groups
    value = contract_rows(left_ref[0], right_ref[...]).astype(jnp.bfloat16)
    each = 2 * half // groups
    fold = value.shape[0] // (each * rows)
    for part in range(each):
        slot = slot_ref[pl.program_id(0) * each + part]
        base = part * fold * rows
        for f in range(groups):
            block = jnp.concatenate(
                [
                    value[base + g * rows : base + (g + 1) * rows, f * width : (f + 1) * width]
                    for g in range(fold)
                ],
                axis=1,
            )
            store_slot(slot, own_ref, send_ref, (f,), block)


def down_slot_grad(slots, left, right, parts, part_rows):
    groups, rows, packed = left.shape
    half = jax.ShapeDtypeStruct((parts // 2, groups, part_rows, packed), jnp.bfloat16)
    out = pl.BlockSpec((parts // 2, groups, part_rows, packed), lambda f, s: (0, 0, 0, 0))
    return pl.pallas_call(
        down_grad_kernel,
        grid_spec=pltpu.PrefetchScalarGridSpec(
            num_scalar_prefetch=1,
            grid=(groups,),
            in_specs=[
                pl.BlockSpec((1, rows, packed), lambda f, s: (f, 0, 0)),
                pl.BlockSpec((rows, packed), lambda f, s: (0, 0)),
            ],
            out_specs=[out, out],
        ),
        out_shape=[half, half],
        compiler_params=params(),
        cost_estimate=lasting(18),
        name="down_grad",
    )(slots, left, right)


def add_kernel(one_ref, two_ref, three_ref, four_ref, came_ref, *outs):
    places = ((outs[0], (0,)), (outs[1], (0,)), (outs[2], (1, 0)), (outs[2], (0, 0)))
    for k, (mine, (out, at)) in enumerate(
        zip((one_ref, two_ref, three_ref, four_ref), places)
    ):
        total = mine[0, 0].astype(jnp.float32) + came_ref[k, 0].astype(jnp.float32)
        out[at] = total.astype(jnp.bfloat16)


def add_halves(own, came):
    half, groups, rows, packed = own.shape
    single = pl.BlockSpec((1, rows, packed), lambda f: (f, 0, 0))
    one = jax.ShapeDtypeStruct((groups, rows, packed), jnp.bfloat16)
    return pl.pallas_call(
        add_kernel,
        grid=(groups,),
        in_specs=[
            pl.BlockSpec((1, 1, rows, packed), lambda f, k=k: (k, f, 0, 0)) for k in range(half)
        ]
        + [pl.BlockSpec((half, 1, rows, packed), lambda f: (0, f, 0, 0))],
        out_specs=[single, single, pl.BlockSpec((2, 1, rows, packed), lambda f: (0, f, 0, 0))],
        out_shape=[one, one, jax.ShapeDtypeStruct((2, groups, rows, packed), jnp.bfloat16)],
        compiler_params=params(),
        cost_estimate=lasting(7),
        name="add_halves",
    )(*([own] * half), came)


def unpack_kernel(part_ref, *refs):
    *pieces, out_ref, held, sems = refs
    pieces = piece_list(pieces)
    step = pl.program_id(0)
    _, groups, rows, packed = held.shape
    width = packed // groups

    @pl.when(step == 0)
    def _():
        for j, piece in enumerate(pieces):
            pltpu.make_async_copy(piece, held.at[j], sems.at[j]).start()

    pltpu.make_async_copy(pieces[0], held.at[step], sems.at[step]).wait()
    for g in range(out_ref.shape[0] // rows):
        out_ref[g * rows : (g + 1) * rows, :] = jnp.concatenate(
            [held[step, f][:, g * width : (g + 1) * width] for f in range(groups)], axis=1
        )


def unpack_pieces(part_of, pieces, fold):
    parts, groups, rows, width = piece_shape(pieces)
    return pl.pallas_call(
        unpack_kernel,
        grid_spec=pltpu.PrefetchScalarGridSpec(
            num_scalar_prefetch=1,
            grid=(parts,),
            in_specs=[pl.BlockSpec(memory_space=pl.ANY)] * len(pieces),
            out_specs=pl.BlockSpec((fold * rows, width), lambda j, p: (p[j], 0)),
            scratch_shapes=[
                pltpu.VMEM((parts, groups, rows, width), pieces[0].dtype),
                pltpu.SemaphoreType.DMA((parts,)),
            ],
        ),
        out_shape=jax.ShapeDtypeStruct((parts * fold * rows, width), pieces[0].dtype),
        compiler_params=params(),
        cost_estimate=lasting(9),
        name="unpack_pieces",
    )(part_of, *pieces)


NEAR = ((0, 2, 4, 6), (0, 4, 2, 6))


def is_cube():
    return lax.axis_size("dp") == 8 and lax.axis_size("fsdp") == 4


def part_tables():
    part_of = np.zeros((8, 8), np.int32)
    slot_of = np.zeros((8, 8), np.int32)
    for part in range(8):
        core = part & 1
        order = [part ^ m for m in NEAR[core]] + [part ^ 1 ^ m for m in NEAR[1 - core]]
        part_of[part] = order
        for slot, other in enumerate(order):
            slot_of[part, other] = slot
    own = lax.axis_index("dp")
    pick = lambda table: lax.dynamic_slice(jnp.asarray(table), (own, 0), (1, 8))[0]
    return pick(part_of), pick(slot_of)


def swap(value, hop):
    return lax.ppermute(value, "dp", [(i, i ^ NEAR[i & 1][hop]) for i in range(8)])


def swap_core(value):
    return lax.ppermute(value, "dp", [(i, i ^ 1) for i in range(8)])


def after(value, *others):
    return lax.optimization_barrier((value, *others))[0]


class Gather:
    def __init__(self, group, ahead=None, *gates):
        own, again = group, group
        if ahead is not None:
            own = after(own, ahead.second)
            again = after(again, ahead.third, *gates)
        self.first = swap(own, 1)
        self.second = swap(again, 2)
        self.third = swap(self.first, 2)
        self.near = [group, self.first, self.second, self.third]

    def pieces(self, *gates):
        late = [after(piece, *gates) if gates else piece for piece in self.near[2:]]
        return self.near + [swap_core(piece) for piece in self.near[:2] + late]


class Scatter:
    def __init__(self, own, send):
        self.own = own
        self.came = swap_core(send)

    def near(self, *gates):
        self.zero, self.one, self.sent = add_halves(after(self.own, *gates), self.came)
        return self.sent

    def send(self, *gates):
        self.far = swap(after(self.sent, *gates), 2)

    def back(self, *gates):
        one = after(self.one, *gates) if gates else self.one
        one = one.astype(jnp.float32) + self.far[0].astype(jnp.float32)
        one = one.astype(jnp.bfloat16)
        self.last = swap(one, 1)
        return one

    def total(self, *gates):
        zero = after(self.zero, *gates)
        total = zero.astype(jnp.float32) + self.far[1].astype(jnp.float32)
        self.sum = (total + self.last.astype(jnp.float32)).astype(jnp.bfloat16)
        return self.sum

    def end(self):
        return lax.psum_scatter(self.sum, "fsdp", scatter_dimension=0, tiled=False)


def swap_bit(value, axis, bit):
    size = lax.axis_size(axis)
    return lax.ppermute(value, axis, [(i, i ^ (1 << bit)) for i in range(size)])


def bit_of(axis, bit):
    return (lax.axis_index(axis) >> bit) & 1 == 1


def small_gather(value, axis):
    if not is_cube():
        return lax.all_gather(value, axis, axis=0, tiled=True)
    for bit in range(lax.axis_size(axis).bit_length() - 1):
        other = swap_bit(value, axis, bit)
        value = jnp.where(
            bit_of(axis, bit),
            jnp.concatenate([other, value], axis=0),
            jnp.concatenate([value, other], axis=0),
        )
    return value


def gather_links_first(value, axis):
    if not is_cube():
        return lax.all_gather(value, axis, axis=0, tiled=True)
    bits = lax.axis_size(axis).bit_length() - 1
    rest = value.shape
    for done, bit in enumerate(reversed(range(bits))):
        other = swap_bit(value, axis, bit)
        value = jnp.where(
            bit_of(axis, bit),
            jnp.stack([other, value], axis=done),
            jnp.stack([value, other], axis=done),
        )
    return value.reshape(-1, *rest[1:])


def small_scatter(value, axis):
    if not is_cube():
        return lax.psum_scatter(value, axis, scatter_dimension=0, tiled=True)
    for bit in reversed(range(lax.axis_size(axis).bit_length() - 1)):
        half = value.shape[0] // 2
        high = bit_of(axis, bit)
        keep = jnp.where(high, value[half:], value[:half])
        value = keep + swap_bit(jnp.where(high, value[:half], value[half:]), axis, bit)
    return value


def small_sum(value, axis):
    if not is_cube():
        return lax.psum(value, axis)
    for bit in range(lax.axis_size(axis).bit_length() - 1):
        value = value + swap_bit(value, axis, bit)
    return value


def gather_shards(shard):
    rows, width = shard.shape
    groups, parts = lax.axis_size("fsdp"), lax.axis_size("dp")
    full = lax.all_gather(shard, ("fsdp", "dp"), axis=0, tiled=True)
    return full.reshape(groups, parts, rows, width)


def scatter_sum(terms):
    groups, parts, rows, width = terms.shape
    return lax.psum_scatter(
        terms.reshape(groups * parts * rows, width),
        ("fsdp", "dp"),
        scatter_dimension=0,
        tiled=True,
    )


def pack_down(natural, groups, parts, rows):
    total, width = natural.shape
    split = natural.reshape(parts, total // (parts * rows), rows, groups, width // groups)
    return split.transpose(3, 0, 2, 1, 4).reshape(groups, parts, rows, width)


def unpack_down(packed, fold):
    groups, parts, rows, width = packed.shape
    split = packed.reshape(groups, parts, rows, fold, width // fold)
    return split.transpose(1, 3, 2, 0, 4).reshape(parts * fold * rows, width)


def body(
    images,
    time_vector,
    timesteps,
    offset_index,
    query_weight,
    key_weight,
    value_weight,
    tquery_weight,
    tvalue_weight,
    proj_weight,
    proj_bias,
    first_gain,
    first_shift,
    second_gain,
    second_shift,
    up_weight,
    down_weight,
    up_bias,
    down_bias,
    bias_table,
    cotangent,
):
    low = jnp.bfloat16
    wide = jnp.float32
    count, tokens, width = images.shape
    rows = count * tokens
    groups, parts = lax.axis_size("fsdp"), lax.axis_size("dp")
    shard_rows, shard_cols = query_weight.shape
    group_heads, table_rows = bias_table.shape
    heads = group_heads * groups
    fold = down_weight.shape[0] // shard_rows
    own_part = lax.axis_index("dp")
    own_group = lax.axis_index("fsdp")

    wire_attn = jnp.concatenate([query_weight, key_weight, value_weight, proj_weight], axis=1)
    wire_down = jnp.concatenate(
        [down_weight[g * shard_rows : (g + 1) * shard_rows] for g in range(fold)], axis=1
    )
    small = jnp.concatenate(
        [
            proj_bias,
            first_gain,
            first_shift,
            second_gain,
            second_shift,
            down_bias,
            up_bias,
            bias_table.reshape(-1),
        ]
    )
    small = jnp.pad(small, (0, -small.shape[0] % 1024)).reshape(-1, LANES)
    time_low = (time_vector.astype(wide) + sinusoid(timesteps, width)).astype(low)
    both = jnp.concatenate([small, time_low.reshape(-1, LANES)], axis=0)
    both = small_gather(both[None], "fsdp")
    small_all = both[:, : small.shape[0]].reshape(groups, -1)

    def vector_of(slot):
        return small_all[:, slot * shard_cols : (slot + 1) * shard_cols].reshape(-1).astype(wide)

    proj_b, gain_one, shift_one, gain_two, shift_two, down_b = (vector_of(i) for i in range(6))
    at = 6 * shard_cols
    up_b = small_all[:, at : at + up_bias.shape[0]].astype(wide)
    at = at + up_bias.shape[0]
    table = small_all[:, at : at + group_heads * table_rows].reshape(heads, table_rows)
    table = jnp.pad(table, ((0, 0), (0, 8 * LANES - table_rows)))
    bias = position_bias(offset_index, table)

    time_rows = both[:, small.shape[0] :].reshape(groups * count, width)
    time_weight = gather_links_first(
        jnp.concatenate([tquery_weight, tvalue_weight], axis=1), "dp"
    )
    time_part = small_gather(matmul(time_rows, time_weight)[None], "fsdp")
    time_own = lax.dynamic_slice(
        time_part, (0, own_group * count, 0), (groups, count, 2 * shard_cols)
    )
    gap = jnp.zeros((groups, count, shard_cols), wide)
    kept = -(-3 * shard_cols // LANES) * LANES
    time_add = jnp.concatenate(
        [
            time_own[:, :, :shard_cols],
            gap,
            time_own[:, :, shard_cols:],
            gap[:, :, : kept - 3 * shard_cols],
        ],
        axis=2,
    )

    cube = is_cube()
    if cube:
        part_of, slot_of = part_tables()
        attn_group = lax.all_gather(wire_attn, "fsdp", axis=0, tiled=False)
        up_group = lax.all_gather(after(up_weight, both), "fsdp", axis=0, tiled=False)
        down_group = lax.all_gather(after(wire_down, both), "fsdp", axis=0, tiled=False)
        attn_move = Gather(after(attn_group, time_weight))
        up_move = Gather(after(up_group, bias), attn_move)
        attn_pieces = attn_move.pieces()
    else:
        part_of = jnp.zeros((1,), jnp.int32)
        attn_pieces = [gather_shards(wire_attn).reshape(groups, width, width)]
        up_pieces = [gather_shards(up_weight).reshape(groups, width, width)]
        down_full = unpack_down(gather_shards(wire_down), fold)

    x_rows = images.reshape(rows, width).astype(wide)
    normed, _, _ = normalize(x_rows, gain_one, shift_one)
    normed_low = normed.astype(low)
    qkv, probs, mixed_split, proj_full, attn_full = attend(
        part_of, attn_pieces, normed_low, time_add, bias, count, tokens
    )
    if cube:
        up_pieces = up_move.pieces(mixed_split)
        down_move = Gather(down_group, up_move, mixed_split)
        mixed_split = after(mixed_split, down_move.first)
    mixed = mixed_split.transpose(1, 0, 2).reshape(rows, width)
    hidden = x_rows + (matmul(mixed, proj_full) + proj_b)
    second, _, _ = normalize(hidden, gain_two, shift_two)
    second_low = second.astype(low)
    grad_low = cotangent.reshape(rows, width)
    wire = (groups, parts, shard_rows, width)
    activ, slope, up_full = up_forward(part_of, up_pieces, second_low, up_b)
    grad_cols = grad_low
    if cube:
        down_pieces = down_move.pieces(activ)
        down_full = unpack_pieces(part_of, down_pieces, fold)
        own, send = down_slot_grad(
            slot_of,
            after(activ, *down_pieces),
            grad_low,
            parts,
            shard_rows,
        )
        down_move = Scatter(own, send)
        grad_cols = after(grad_low, down_move.near(down_full))
        down_move.send()
    def lines_of(*values):
        return jnp.concatenate([jnp.stack(values), jnp.zeros((8 - len(values), width), wide)])

    d_pre, layer_out, d_hidden, d_hidden_low, down_sums, up_sums = down_back(
        grad_cols, hidden, lines_of(gain_two, down_b), activ, slope, up_full, down_full
    )
    layer_out = layer_out.reshape(count, tokens, width)
    d_hidden_cols = d_hidden_low
    if cube:
        d_hidden_cols = after(d_hidden_low, down_move.back())
    d_packed, pairs, d_time = attend_back(d_hidden_cols, proj_full, qkv, probs)
    attn_back = attn_full
    if cube:
        normed_t = after(normed_low.T, down_move.last)
        own, send = slot_grad(
            pair_grad_kernel, slot_of, [normed_t, mixed.T], d_packed, parts, "pair_grad"
        )
        attn_move = Scatter(own, after(send, down_move.total()))
        down_sum = down_move.end()
        second_t = after(second_low.T, send)
        own, send = slot_grad(one_grad_kernel, slot_of, [second_t], d_pre, parts, "up_grad")
        up_move = Scatter(own, send)
        attn_pair = attn_move.near(send)
        attn_move.send()
        attn_back = after(attn_full, up_move.near(attn_pair))
    else:
        grad_down = jnp.concatenate([contract_rows(a, grad_low) for a in activ], axis=0)
        down_sum = scatter_sum(pack_down(grad_down.astype(low), groups, parts, shard_rows))
        grad_up = jnp.stack([contract_rows(second_low, d).astype(low) for d in d_pre])
        up_sum = scatter_sum(grad_up.reshape(wire))
        cut = 3 * shard_cols
        grad_attn = jnp.stack(
            [
                jnp.concatenate(
                    [contract_rows(normed_low, d[:, :cut]), contract_rows(mixed, d[:, cut:])],
                    axis=1,
                )
                for d in d_packed
            ]
        )
        attn_sum = scatter_sum(grad_attn.astype(low).reshape(wire))

    images_grad, input_sums = input_grad(
        d_packed, attn_back, images.reshape(rows, width), d_hidden, lines_of(gain_one)
    )
    images_grad = images_grad.reshape(count, tokens, width)

    if cube:
        attn_one = attn_move.back(images_grad)
        up_move.send(attn_one)
        pairs = after(pairs, attn_one)
    table_sum = table_gradient(offset_index, pairs)
    if cube:
        d_time = after(d_time, table_sum)
        attn_total = attn_move.total(table_sum)
        up_one = up_move.back()
        up_total = up_move.total()
    d_time = jnp.concatenate(
        [d_time[:, :, :shard_cols], d_time[:, :, 2 * shard_cols : 3 * shard_cols]], axis=2
    ).astype(low)
    d_time = d_time.transpose(1, 0, 2).reshape(count, groups * 2 * shard_cols)
    d_time_rows = small_gather(d_time, "fsdp")
    d_time_cols = lax.dynamic_slice(
        d_time_rows, (0, own_group * 2 * shard_cols), (groups * count, 2 * shard_cols)
    )
    time_grads = contract_rows(time_rows, d_time_cols).astype(low)
    if cube:
        time_grads = after(time_grads, up_total)
    time_grads = small_scatter(time_grads, "dp")
    back = times_transposed(d_time_cols, time_weight).reshape(-1, LANES)

    vectors = jnp.concatenate(
        [down_sums[:4], input_sums[:2], up_sums.reshape(groups, width)]
    ).reshape(-1, LANES)
    flat = jnp.concatenate([vectors, table_sum, back], axis=0)
    ends = (vectors.shape[0], vectors.shape[0] + table_sum.shape[0])
    flat = small_sum(flat, "fsdp")
    time_grad = lax.dynamic_slice(
        flat[ends[1] :].reshape(groups * count, width), (own_group * count, 0), (count, width)
    )
    flat = flat[: ends[1]]
    if cube:
        flat = after(flat, attn_total, up_one)
    flat = small_sum(flat, "dp")
    vectors = flat[: ends[0]].reshape(-1, width)
    own = lax.dynamic_slice(vectors, (0, own_group * shard_cols), (6, shard_cols))
    proj_bg, gain2_g, shift2_g, down_bg, gain1_g, shift1_g = (own[i] for i in range(6))
    up_bg = lax.dynamic_slice(vectors, (6 + own_group, 0), (1, width))[0]
    table_grad = lax.dynamic_slice(
        flat[ends[0] : ends[1]], (own_group * group_heads * 8, 0), (group_heads * 8, LANES)
    )
    table_grad = table_grad.reshape(group_heads, 8 * LANES)[:, :table_rows]

    if cube:
        down_sum = after(down_sum, up_total)
        attn_sum = after(attn_move.end(), up_total)
        up_sum = up_move.end()
    time_grads = time_grads.astype(wide)
    tquery_grad, tvalue_grad = time_grads[:, :shard_cols], time_grads[:, shard_cols:]
    attn_sum = attn_sum.astype(wide)
    query_grad, key_grad, value_grad, proj_grad = (
        attn_sum[:, i * shard_cols : (i + 1) * shard_cols] for i in range(4)
    )
    down_sum = down_sum.astype(wide)
    down_grad = jnp.concatenate(
        [down_sum[:, g * shard_cols : (g + 1) * shard_cols] for g in range(fold)], axis=0
    )
    return (
        layer_out,
        images_grad,
        time_grad,
        query_grad,
        key_grad,
        value_grad,
        tquery_grad,
        tvalue_grad,
        proj_grad,
        proj_bg,
        gain1_g,
        shift1_g,
        gain2_g,
        shift2_g,
        up_sum.astype(wide),
        down_grad,
        up_bg,
        down_bg,
        table_grad,
    )


def solution(mesh):
    rows = P(BOTH, None, None)
    matrix = P("dp", "fsdp")
    vector = P("fsdp")
    table = P("fsdp", None)
    return jax.shard_map(
        body,
        mesh=mesh,
        in_specs=(
            (rows, P(BOTH, None), P(BOTH), P())
            + (matrix,) * 6
            + (vector,) * 5
            + (matrix,) * 2
            + (vector,) * 2
            + (table, rows)
        ),
        out_specs=(
            (rows, rows, P(BOTH, None))
            + (matrix,) * 6
            + (vector,) * 5
            + (matrix,) * 2
            + (vector,) * 2
            + (table,)
        ),
        check_vma=False,
    )
```

```python
import math

import jax
import jax.numpy as jnp
import numpy as np
from jax import lax
from jax.experimental import pallas as pl
from jax.experimental.pallas import tpu as pltpu
from jax.sharding import PartitionSpec as P

LANES = 128
BOTH = ("dp", "fsdp")
VMEM_LIMIT = 58 * 1024 * 1024


def lasting(microseconds):
    return pl.CostEstimate(
        flops=int(microseconds * 1e9), transcendentals=0, bytes_accessed=1
    )


def sinusoid(steps, model_width):
    half_width = model_width // 2
    frequency = jnp.exp(
        -math.log(10000.0) * jnp.arange(half_width).astype(jnp.float32) / half_width
    )
    angles = steps.astype(jnp.float32)[:, None] * frequency[None, :]
    return jnp.concatenate([jnp.sin(angles), jnp.cos(angles)], axis=1)


def matmul(left, right):
    return jnp.dot(left, right, preferred_element_type=jnp.float32)


def contract_rows(left, right):
    return lax.dot_general(
        left, right, (((0,), (0,)), ((), ())), preferred_element_type=jnp.float32
    )


def times_transposed(left, right):
    return lax.dot_general(
        left, right, (((1,), (1,)), ((), ())), preferred_element_type=jnp.float32
    )


def normalize(values, gain, shift):
    row_mean = jnp.mean(values, axis=-1, keepdims=True)
    centered = values - row_mean
    inv_std = lax.rsqrt(jnp.mean(centered * centered, axis=-1, keepdims=True) + 1e-06)
    unit_rows = centered * inv_std
    return (unit_rows * gain + shift, unit_rows, inv_std)


def norm_back(grad_rows, unit_rows, inv_std, gain):
    scaled = grad_rows * gain
    return inv_std * (
        scaled
        - jnp.mean(scaled, axis=-1, keepdims=True)
        - unit_rows * jnp.mean(scaled * unit_rows, axis=-1, keepdims=True)
    )


def gelu_slope(pre_act):
    return 0.5 * (1.0 + lax.erf(pre_act * (1.0 / math.sqrt(2.0)))) + pre_act * jnp.exp(
        -0.5 * pre_act * pre_act
    ) * (1.0 / math.sqrt(2.0 * math.pi))


def params(count=1):
    return pltpu.CompilerParams(
        dimension_semantics=("arbitrary",) * count, vmem_limit_bytes=VMEM_LIMIT
    )


def bias_kernel(index_ref, table_ref, bias_ref):
    heads, rows, tokens = bias_ref.shape
    chunks = table_ref.shape[2] // LANES
    pieces = [
        [
            jnp.broadcast_to(table_ref[h, :, c * LANES : (c + 1) * LANES], (8, LANES))
            for c in range(chunks)
        ]
        for h in range(heads)
    ]

    def some_rows(step, carry):
        at = pl.multiple_of(step * 8, 8)
        for col in range(tokens // LANES):
            lanes = slice(col * LANES, (col + 1) * LANES)
            index = index_ref[pl.ds(at, 8), lanes]
            low = index & (LANES - 1)
            high = index >> 7
            hits = [high == c for c in range(chunks)]
            for h in range(heads):
                found = jnp.take_along_axis(pieces[h][0], low, axis=1)
                for c in range(1, chunks):
                    found = jnp.where(
                        hits[c], jnp.take_along_axis(pieces[h][c], low, axis=1), found
                    )
                bias_ref[h, pl.ds(at, 8), lanes] = found
        return carry

    lax.fori_loop(0, rows // 8, some_rows, 0)


def position_bias(index, table):
    heads, padded = table.shape
    tokens = index.shape[0]
    group = heads // 4
    return pl.pallas_call(
        bias_kernel,
        grid=(4,),
        in_specs=[
            pl.BlockSpec((tokens, tokens), lambda f: (0, 0)),
            pl.BlockSpec((group, 1, padded), lambda f: (f, 0, 0)),
        ],
        out_specs=pl.BlockSpec((group, tokens, tokens), lambda f: (f, 0, 0)),
        out_shape=jax.ShapeDtypeStruct((heads, tokens, tokens), jnp.float32),
        compiler_params=params(),
        cost_estimate=lasting(20),
        name="position_bias",
    )(index, table.astype(jnp.float32).reshape(heads, 1, padded))


def table_kernel(index_ref, pairs_ref, out_ref):
    heads = pairs_ref.shape[0]
    tokens = index_ref.shape[1]
    rows = index_ref.shape[0]

    @pl.when(pl.program_id(0) == 0)
    def _():
        out_ref[...] = jnp.zeros_like(out_ref)

    sub = lax.broadcasted_iota(jnp.int32, (8, tokens), 0)
    lane_of = lax.broadcasted_iota(jnp.int32, (LANES, tokens), 0)

    def row_terms(row):
        index = index_ref[pl.ds(row, 1), :]
        low = jnp.broadcast_to(index & (LANES - 1), (LANES, tokens))
        high = jnp.broadcast_to(index >> 7, (8, tokens))
        hit = sub == high
        left = jnp.concatenate(
            [
                jnp.where(hit, jnp.broadcast_to(pairs_ref[h, pl.ds(row, 1), :], (8, tokens)), 0.0)
                for h in range(heads)
            ],
            axis=0,
        ).astype(jnp.bfloat16)
        right = jnp.where(lane_of == low, 1.0, 0.0).astype(jnp.bfloat16)
        return left, right

    def some_rows(step, total):
        terms = [row_terms(step * 4 + k) for k in range(4)]
        left = jnp.concatenate([t[0] for t in terms], axis=1)
        right = jnp.concatenate([t[1] for t in terms], axis=1)
        return total + times_transposed(left, right)

    out_ref[...] += lax.fori_loop(
        0, rows // 4, some_rows, jnp.zeros((heads * 8, LANES), jnp.float32)
    )


def table_gradient(index, pairs):
    heads, tokens, _ = pairs.shape
    block = 64
    return pl.pallas_call(
        table_kernel,
        grid=(tokens // block,),
        in_specs=[
            pl.BlockSpec((block, tokens), lambda i: (i, 0)),
            pl.BlockSpec((heads, block, tokens), lambda i: (0, i, 0)),
        ],
        out_specs=pl.BlockSpec((heads * 8, LANES), lambda i: (0, 0)),
        out_shape=jax.ShapeDtypeStruct((heads * 8, LANES), jnp.float32),
        compiler_params=params(),
        cost_estimate=lasting(18),
        name="table_gradient",
    )(index, pairs)


def piece_list(refs):
    out = []
    for ref in refs:
        out.extend([ref] if len(ref.shape) == 3 else [ref.at[k] for k in range(ref.shape[0])])
    return out


def piece_shape(refs):
    count = sum(1 if len(ref.shape) == 3 else ref.shape[0] for ref in refs)
    return (count, *refs[0].shape)


def load_group(part_ref, refs, held, in_sems, full_ref, out_sems):
    step = pl.program_id(0)
    pieces = piece_list(refs)
    rows = pieces[0].shape[1]

    def copy(group, j):
        at = pl.multiple_of(part_ref[j] * rows, 16)
        return pltpu.make_async_copy(
            pieces[j].at[group], held.at[group, pl.ds(at, rows)], in_sems.at[group, j]
        )

    @pl.when(step == 0)
    def _():
        for group in range(held.shape[0]):
            for j in range(len(pieces)):
                copy(group, j).start()

    for j in range(len(pieces)):
        copy(step, j).wait()
    pltpu.make_async_copy(held.at[step], full_ref.at[step], out_sems.at[step]).start()


def finish_groups(held, full_ref, out_sems):
    @pl.when(pl.program_id(0) == held.shape[0] - 1)
    def _():
        for group in range(held.shape[0]):
            pltpu.make_async_copy(held.at[group], full_ref.at[group], out_sems.at[group]).wait()


def piece_call(kernel, name, part_of, pieces, inputs, in_specs, out_specs, out_shapes):
    parts, groups, rows, packed = piece_shape(pieces)
    depth = rows * parts
    full = jax.ShapeDtypeStruct((groups, depth, packed), pieces[0].dtype)
    anywhere = pl.BlockSpec(memory_space=pl.ANY)
    return pl.pallas_call(
        kernel,
        grid_spec=pltpu.PrefetchScalarGridSpec(
            num_scalar_prefetch=1,
            grid=(groups,),
            in_specs=in_specs + [anywhere] * len(pieces),
            out_specs=out_specs + [anywhere],
            scratch_shapes=[
                pltpu.VMEM((groups, depth, packed), pieces[0].dtype),
                pltpu.SemaphoreType.DMA((groups, parts)),
                pltpu.SemaphoreType.DMA((groups,)),
            ],
        ),
        out_shape=out_shapes + [full],
        compiler_params=params(),
        cost_estimate=lasting(13),
        name=name,
    )(part_of, *inputs, *pieces)


def attend_kernel(part_ref, normed_ref, add_ref, bias_ref, *refs):
    *pieces, qkv_ref, probs_ref, mixed_ref, proj_ref, full_ref, held, in_sems, out_sems = refs
    images, heads = probs_ref.shape[1], probs_ref.shape[2]
    tokens = probs_ref.shape[3]
    width = mixed_ref.shape[2]
    size = width // heads
    scale = 1.0 / math.sqrt(size)
    kept = qkv_ref.shape[2]
    step = pl.program_id(0)
    load_group(part_ref, pieces, held, in_sems, full_ref, out_sems)
    for image in range(images):
        rows = slice(image * tokens, (image + 1) * tokens)
        acc = matmul(normed_ref[rows, :], held[step, :, :kept])
        qkv_ref[0, rows, :] = (acc + add_ref[0, image : image + 1, :]).astype(jnp.bfloat16)
    for image in range(images):
        rows = slice(image * tokens, (image + 1) * tokens)
        both = qkv_ref[0, rows, :]
        outs = []
        for head in range(heads):
            at = head * size
            query = both[:, at : at + size]
            keys = both[:, width + at : width + at + size]
            values = both[:, 2 * width + at : 2 * width + at + size]
            scores = times_transposed(query, keys) * scale + bias_ref[head]
            peak = jnp.max(scores, axis=-1, keepdims=True)
            expo = jnp.exp(scores - peak)
            total = jnp.sum(expo, axis=-1, keepdims=True)
            probs = (expo / total).astype(jnp.bfloat16)
            probs_ref[0, image, head] = probs
            outs.append(matmul(probs, values))
        mixed_ref[0, rows, :] = jnp.concatenate(outs, axis=1).astype(jnp.bfloat16)
    for group in range(held.shape[0]):

        @pl.when(step == group)
        def _(group=group):
            proj_ref[:, group * width : (group + 1) * width] = held[group, :, 3 * width :]

    finish_groups(held, full_ref, out_sems)


def attend(part_of, pieces, normed, add, bias, images, tokens):
    parts, groups, part_rows, packed = piece_shape(pieces)
    depth = part_rows * parts
    heads = bias.shape[0] // groups
    width = packed // groups
    kept = add.shape[2]
    rows = images * tokens
    low = jnp.bfloat16
    return piece_call(
        attend_kernel,
        "attend",
        part_of,
        pieces,
        [normed, add, bias],
        [
            pl.BlockSpec((rows, depth), lambda f, p: (0, 0)),
            pl.BlockSpec((1, images, kept), lambda f, p: (f, 0, 0)),
            pl.BlockSpec((heads, tokens, tokens), lambda f, p: (f, 0, 0)),
        ],
        [
            pl.BlockSpec((1, rows, kept), lambda f, p: (f, 0, 0)),
            pl.BlockSpec((1, images, heads, tokens, tokens), lambda f, p: (f, 0, 0, 0, 0)),
            pl.BlockSpec((1, rows, width), lambda f, p: (f, 0, 0)),
            pl.BlockSpec((depth, packed), lambda f, p: (0, 0)),
        ],
        [
            jax.ShapeDtypeStruct((groups, rows, kept), low),
            jax.ShapeDtypeStruct((groups, images, heads, tokens, tokens), low),
            jax.ShapeDtypeStruct((groups, rows, width), low),
            jax.ShapeDtypeStruct((depth, packed), low),
        ],
    )


def up_kernel(part_ref, second_ref, bias_ref, *refs):
    *pieces, activ_ref, slope_ref, full_ref, held, in_sems, out_sems = refs
    load_group(part_ref, pieces, held, in_sems, full_ref, out_sems)
    weight = held[pl.program_id(0)]
    block = 256
    for start in range(0, second_ref.shape[0], block):
        rows = slice(start, start + block)
        pre = matmul(second_ref[rows, :], weight) + bias_ref[0]
        below = 0.5 * (1.0 + lax.erf(pre * (1.0 / math.sqrt(2.0))))
        density = jnp.exp(-0.5 * pre * pre) * (1.0 / math.sqrt(2.0 * math.pi))
        activ_ref[0, rows, :] = (pre * below).astype(jnp.bfloat16)
        slope_ref[0, rows, :] = (below + pre * density).astype(jnp.bfloat16)
    finish_groups(held, full_ref, out_sems)


def up_forward(part_of, pieces, second, bias):
    _, groups, _, packed = piece_shape(pieces)
    rows, depth = second.shape
    wide = pl.BlockSpec((1, rows, packed), lambda f, p: (f, 0, 0))
    shape = jax.ShapeDtypeStruct((groups, rows, packed), jnp.bfloat16)
    return piece_call(
        up_kernel,
        "up_forward",
        part_of,
        pieces,
        [second, bias.reshape(groups, 1, packed)],
        [
            pl.BlockSpec((rows, depth), lambda f, p: (0, 0)),
            pl.BlockSpec((1, 1, packed), lambda f, p: (f, 0, 0)),
        ],
        [wide, wide],
        [shape, shape],
    )


def column_sum(value):
    return jnp.sum(value, axis=0, keepdims=True)


def down_back_kernel(
    grad_ref,
    hidden_ref,
    row_ref,
    activ_ref,
    slope_ref,
    up_ref,
    down_ref,
    pre_ref,
    out_ref,
    d_hidden_ref,
    d_low_ref,
    sum_ref,
    up_sum_ref,
    total,
    second,
):
    step = pl.program_id(0)
    weight = down_ref[...]
    d_activ = times_transposed(grad_ref[...], weight)
    d_pre = (d_activ * slope_ref[0].astype(jnp.float32)).astype(jnp.bfloat16)
    pre_ref[0] = d_pre
    up_sum_ref[0] = column_sum(d_pre.astype(jnp.float32))
    part = times_transposed(d_pre, up_ref[0])
    more = matmul(activ_ref[0], weight)

    @pl.when(step == 0)
    def _():
        second[...] = part
        total[...] = more

    @pl.when(step > 0)
    def _():
        second[...] += part
        total[...] += more

    @pl.when(step == pl.num_programs(0) - 1)
    def _():
        block = 64
        gain, shift = row_ref[0:1, :], row_ref[1:2, :]
        sum_ref[...] = jnp.zeros_like(sum_ref)

        def some_rows(at, carry):
            rows = pl.ds(pl.multiple_of(at * block, block), block)
            hidden = hidden_ref[rows, :]
            out_ref[rows, :] = (hidden + shift + total[rows, :]).astype(jnp.bfloat16)
            _, unit, inv = normalize(hidden, gain, 0.0)
            d_second = second[rows, :]
            grad = grad_ref[rows, :].astype(jnp.float32)
            d_hidden = grad + norm_back(d_second, unit, inv, gain)
            d_low = d_hidden.astype(jnp.bfloat16)
            d_hidden_ref[rows, :] = d_hidden
            d_low_ref[rows, :] = d_low
            sum_ref[0:1, :] += column_sum(d_low.astype(jnp.float32))
            sum_ref[1:2, :] += column_sum(d_second * unit)
            sum_ref[2:3, :] += column_sum(d_second)
            sum_ref[3:4, :] += column_sum(grad)
            return carry

        lax.fori_loop(0, hidden_ref.shape[0] // block, some_rows, 0)


def down_back(grad, hidden, lines, activ, slope, up_full, down_full):
    groups, rows, packed = activ.shape
    depth = up_full.shape[1]
    whole = pl.BlockSpec((rows, depth), lambda f: (0, 0))
    mine = pl.BlockSpec((1, rows, packed), lambda f: (f, 0, 0))
    few = pl.BlockSpec((8, depth), lambda f: (0, 0))
    return pl.pallas_call(
        down_back_kernel,
        grid=(groups,),
        in_specs=[
            whole,
            whole,
            few,
            mine,
            mine,
            pl.BlockSpec((1, depth, packed), lambda f: (f, 0, 0)),
            pl.BlockSpec((packed, depth), lambda f: (f, 0)),
        ],
        out_specs=[
            mine,
            whole,
            whole,
            whole,
            few,
            pl.BlockSpec((1, 1, packed), lambda f: (f, 0, 0)),
        ],
        out_shape=[
            jax.ShapeDtypeStruct((groups, rows, packed), jnp.bfloat16),
            jax.ShapeDtypeStruct((rows, depth), jnp.bfloat16),
            jax.ShapeDtypeStruct((rows, depth), jnp.float32),
            jax.ShapeDtypeStruct((rows, depth), jnp.bfloat16),
            jax.ShapeDtypeStruct((8, depth), jnp.float32),
            jax.ShapeDtypeStruct((groups, 1, packed), jnp.float32),
        ],
        scratch_shapes=[
            pltpu.VMEM((rows, depth), jnp.float32),
            pltpu.VMEM((rows, depth), jnp.float32),
        ],
        compiler_params=params(),
        cost_estimate=lasting(33),
        name="down_back",
    )(grad, hidden, lines, activ, slope, up_full, down_full)


def attend_back_kernel(
    hidden_ref, proj_ref, qkv_ref, probs_ref, out_ref, pairs_ref, time_ref
):
    images, heads = probs_ref.shape[1], probs_ref.shape[2]
    tokens = probs_ref.shape[3]
    width = proj_ref.shape[0]
    size = width // heads
    scale = 1.0 / math.sqrt(size)
    for image in range(images):
        rows = slice(image * tokens, (image + 1) * tokens)
        both = qkv_ref[0, rows, :]
        grads = times_transposed(hidden_ref[rows, :], proj_ref[...]).astype(jnp.bfloat16)
        d_query, d_keys, d_values = [], [], []
        for head in range(heads):
            at = head * size
            query = both[:, at : at + size]
            keys = both[:, width + at : width + at + size]
            values = both[:, 2 * width + at : 2 * width + at + size]
            grad = grads[:, at : at + size]
            probs_low = probs_ref[0, image, head]
            probs = probs_low.astype(jnp.float32)
            d_values.append(contract_rows(probs_low, grad))
            d_probs = times_transposed(grad, values)
            moved = probs * d_probs
            d_scores = moved - probs * jnp.sum(moved, axis=-1, keepdims=True)
            d_low = d_scores.astype(jnp.bfloat16)
            if image == 0:
                pairs_ref[head] = d_low.astype(jnp.float32)
            else:
                pairs_ref[head] += d_low.astype(jnp.float32)
            d_query.append(matmul(d_low, keys) * scale)
            d_keys.append(contract_rows(d_low, query) * scale)
        packed = jnp.concatenate(d_query + d_keys + d_values, axis=1).astype(jnp.bfloat16)
        out_ref[0, rows, : 3 * width] = packed
        time_ref[0, image : image + 1, :] = column_sum(packed.astype(jnp.float32))
    for group in range(hidden_ref.shape[1] // width):

        @pl.when(pl.program_id(0) == group)
        def _(group=group):
            out_ref[0, :, 3 * width :] = hidden_ref[:, group * width : (group + 1) * width]


def attend_back(hidden, proj, qkv, probs):
    rows, packed = hidden.shape
    groups, images, heads, tokens, _ = probs.shape
    kept = qkv.shape[2]
    width = packed // groups
    return pl.pallas_call(
        attend_back_kernel,
        grid=(groups,),
        in_specs=[
            pl.BlockSpec((rows, packed), lambda f: (0, 0)),
            pl.BlockSpec((width, packed), lambda f: (f, 0)),
            pl.BlockSpec((1, rows, kept), lambda f: (f, 0, 0)),
            pl.BlockSpec((1, images, heads, tokens, tokens), lambda f: (f, 0, 0, 0, 0)),
        ],
        out_specs=[
            pl.BlockSpec((1, rows, packed), lambda f: (f, 0, 0)),
            pl.BlockSpec((heads, tokens, tokens), lambda f: (f, 0, 0)),
            pl.BlockSpec((1, images, 3 * width), lambda f: (f, 0, 0)),
        ],
        out_shape=[
            jax.ShapeDtypeStruct((groups, rows, packed), jnp.bfloat16),
            jax.ShapeDtypeStruct((groups * heads, tokens, tokens), jnp.float32),
            jax.ShapeDtypeStruct((groups, images, 3 * width), jnp.float32),
        ],
        compiler_params=params(),
        cost_estimate=lasting(19),
        name="attend_back",
    )(hidden, proj, qkv, probs)


def input_grad_kernel(
    right_ref, weight_ref, image_ref, d_hidden_ref, row_ref, out_ref, sum_ref, total
):
    step = pl.program_id(0)
    cut = 3 * (right_ref.shape[2] // 4)
    kept = -(-cut // LANES) * LANES
    lane = lax.broadcasted_iota(jnp.int32, (1, kept), 1)
    right = right_ref[0, :, :kept]
    right = jnp.where(lane < cut, right.astype(jnp.float32), 0.0).astype(jnp.bfloat16)
    part = times_transposed(right, weight_ref[0, :, :kept])

    @pl.when(step == 0)
    def _():
        total[...] = part

    @pl.when(step > 0)
    def _():
        total[...] += part

    @pl.when(step == pl.num_programs(0) - 1)
    def _():
        block = 64
        gain = row_ref[0:1, :]
        sum_ref[...] = jnp.zeros_like(sum_ref)

        def some_rows(at, carry):
            rows = pl.ds(pl.multiple_of(at * block, block), block)
            _, unit, inv = normalize(image_ref[rows, :].astype(jnp.float32), gain, 0.0)
            d_normed = total[rows, :]
            d_input = d_hidden_ref[rows, :] + norm_back(d_normed, unit, inv, gain)
            out_ref[rows, :] = d_input.astype(jnp.bfloat16)
            sum_ref[0:1, :] += column_sum(d_normed * unit)
            sum_ref[1:2, :] += column_sum(d_normed)
            return carry

        lax.fori_loop(0, image_ref.shape[0] // block, some_rows, 0)


def input_grad(right, weight, images, d_hidden, lines):
    groups, rows, packed = right.shape
    whole = pl.BlockSpec((rows, packed), lambda f: (0, 0))
    few = pl.BlockSpec((8, packed), lambda f: (0, 0))
    return pl.pallas_call(
        input_grad_kernel,
        grid=(groups,),
        in_specs=[
            pl.BlockSpec((1, rows, packed), lambda f: (f, 0, 0)),
            pl.BlockSpec((1, packed, packed), lambda f: (f, 0, 0)),
            whole,
            whole,
            few,
        ],
        out_specs=[whole, few],
        out_shape=[
            jax.ShapeDtypeStruct((rows, packed), jnp.bfloat16),
            jax.ShapeDtypeStruct((8, packed), jnp.float32),
        ],
        scratch_shapes=[pltpu.VMEM((rows, packed), jnp.float32)],
        compiler_params=params(),
        cost_estimate=lasting(1),
        name="input_grad",
    )(right, weight, images, d_hidden, lines)


def store_slot(slot, own_ref, send_ref, at, value):
    half = own_ref.shape[0]

    @pl.when(slot < half)
    def _():
        own_ref[(slot,) + at] = value

    @pl.when(slot >= half)
    def _():
        send_ref[(slot - half,) + at] = value


def pair_grad_kernel(slot_ref, one_ref, two_ref, right_ref, own_ref, send_ref):
    cut = 3 * (right_ref.shape[2] // 4)
    below = cut // LANES * LANES
    above = below + LANES
    rows = own_ref.shape[2]
    right = right_ref[0]
    lane = lax.broadcasted_iota(jnp.int32, (rows, LANES), 1)
    first = matmul(one_ref[...], right[:, :above])
    last = matmul(two_ref[...], right[:, below:])
    for part in range(2 * own_ref.shape[0]):
        at = slice(part * rows, (part + 1) * rows)
        value = jnp.concatenate(
            [
                first[at, :below],
                jnp.where(lane < cut - below, first[at, below:], last[at, :LANES]),
                last[at, LANES:],
            ],
            axis=1,
        ).astype(jnp.bfloat16)
        store_slot(slot_ref[part], own_ref, send_ref, (0,), value)


def one_grad_kernel(slot_ref, one_ref, right_ref, own_ref, send_ref):
    rows = own_ref.shape[2]
    first = matmul(one_ref[...], right_ref[0])
    for part in range(2 * own_ref.shape[0]):
        value = first[part * rows : (part + 1) * rows].astype(jnp.bfloat16)
        store_slot(slot_ref[part], own_ref, send_ref, (0,), value)


def slot_grad(kernel, slots, lefts, right, parts, name):
    groups, rows, packed = right.shape
    depth = lefts[0].shape[0]
    half = jax.ShapeDtypeStruct((parts // 2, groups, depth // parts, packed), jnp.bfloat16)
    out = pl.BlockSpec((parts // 2, 1, depth // parts, packed), lambda f, s: (0, f, 0, 0))
    return pl.pallas_call(
        kernel,
        grid_spec=pltpu.PrefetchScalarGridSpec(
            num_scalar_prefetch=1,
            grid=(groups,),
            in_specs=[pl.BlockSpec((depth, rows), lambda f, s: (0, 0)) for _ in lefts]
            + [pl.BlockSpec((1, rows, packed), lambda f, s: (f, 0, 0))],
            out_specs=[out, out],
        ),
        out_shape=[half, half],
        compiler_params=params(),
        cost_estimate=lasting(18),
        name=name,
    )(slots, *lefts, right)


def down_grad_kernel(slot_ref, left_ref, right_ref, own_ref, send_ref):
    half, groups, rows, packed = own_ref.shape
    width = packed // groups
    value = contract_rows(left_ref[0], right_ref[...]).astype(jnp.bfloat16)
    each = 2 * half // groups
    fold = value.shape[0] // (each * rows)
    for part in range(each):
        slot = slot_ref[pl.program_id(0) * each + part]
        base = part * fold * rows
        for f in range(groups):
            block = jnp.concatenate(
                [
                    value[base + g * rows : base + (g + 1) * rows, f * width : (f + 1) * width]
                    for g in range(fold)
                ],
                axis=1,
            )
            store_slot(slot, own_ref, send_ref, (f,), block)


def down_slot_grad(slots, left, right, parts, part_rows):
    groups, rows, packed = left.shape
    half = jax.ShapeDtypeStruct((parts // 2, groups, part_rows, packed), jnp.bfloat16)
    out = pl.BlockSpec((parts // 2, groups, part_rows, packed), lambda f, s: (0, 0, 0, 0))
    return pl.pallas_call(
        down_grad_kernel,
        grid_spec=pltpu.PrefetchScalarGridSpec(
            num_scalar_prefetch=1,
            grid=(groups,),
            in_specs=[
                pl.BlockSpec((1, rows, packed), lambda f, s: (f, 0, 0)),
                pl.BlockSpec((rows, packed), lambda f, s: (0, 0)),
            ],
            out_specs=[out, out],
        ),
        out_shape=[half, half],
        compiler_params=params(),
        cost_estimate=lasting(18),
        name="down_grad",
    )(slots, left, right)


def add_kernel(one_ref, two_ref, three_ref, four_ref, came_ref, *outs):
    places = ((outs[0], (0,)), (outs[1], (0,)), (outs[2], (1, 0)), (outs[2], (0, 0)))
    for k, (mine, (out, at)) in enumerate(
        zip((one_ref, two_ref, three_ref, four_ref), places)
    ):
        total = mine[0, 0].astype(jnp.float32) + came_ref[k, 0].astype(jnp.float32)
        out[at] = total.astype(jnp.bfloat16)


def add_halves(own, came):
    half, groups, rows, packed = own.shape
    single = pl.BlockSpec((1, rows, packed), lambda f: (f, 0, 0))
    one = jax.ShapeDtypeStruct((groups, rows, packed), jnp.bfloat16)
    return pl.pallas_call(
        add_kernel,
        grid=(groups,),
        in_specs=[
            pl.BlockSpec((1, 1, rows, packed), lambda f, k=k: (k, f, 0, 0)) for k in range(half)
        ]
        + [pl.BlockSpec((half, 1, rows, packed), lambda f: (0, f, 0, 0))],
        out_specs=[single, single, pl.BlockSpec((2, 1, rows, packed), lambda f: (0, f, 0, 0))],
        out_shape=[one, one, jax.ShapeDtypeStruct((2, groups, rows, packed), jnp.bfloat16)],
        compiler_params=params(),
        cost_estimate=lasting(7),
        name="add_halves",
    )(*([own] * half), came)


def unpack_kernel(part_ref, *refs):
    *pieces, out_ref, held, sems = refs
    pieces = piece_list(pieces)
    step = pl.program_id(0)
    _, groups, rows, packed = held.shape
    width = packed // groups

    @pl.when(step == 0)
    def _():
        for j, piece in enumerate(pieces):
            pltpu.make_async_copy(piece, held.at[j], sems.at[j]).start()

    pltpu.make_async_copy(pieces[0], held.at[step], sems.at[step]).wait()
    for g in range(out_ref.shape[0] // rows):
        out_ref[g * rows : (g + 1) * rows, :] = jnp.concatenate(
            [held[step, f][:, g * width : (g + 1) * width] for f in range(groups)], axis=1
        )


def unpack_pieces(part_of, pieces, fold):
    parts, groups, rows, width = piece_shape(pieces)
    return pl.pallas_call(
        unpack_kernel,
        grid_spec=pltpu.PrefetchScalarGridSpec(
            num_scalar_prefetch=1,
            grid=(parts,),
            in_specs=[pl.BlockSpec(memory_space=pl.ANY)] * len(pieces),
            out_specs=pl.BlockSpec((fold * rows, width), lambda j, p: (p[j], 0)),
            scratch_shapes=[
                pltpu.VMEM((parts, groups, rows, width), pieces[0].dtype),
                pltpu.SemaphoreType.DMA((parts,)),
            ],
        ),
        out_shape=jax.ShapeDtypeStruct((parts * fold * rows, width), pieces[0].dtype),
        compiler_params=params(),
        cost_estimate=lasting(9),
        name="unpack_pieces",
    )(part_of, *pieces)


NEAR = ((0, 2, 4, 6), (0, 4, 2, 6))


def is_cube():
    return lax.axis_size("dp") == 8 and lax.axis_size("fsdp") == 4


def part_tables():
    part_of = np.zeros((8, 8), np.int32)
    slot_of = np.zeros((8, 8), np.int32)
    for part in range(8):
        core = part & 1
        order = [part ^ m for m in NEAR[core]] + [part ^ 1 ^ m for m in NEAR[1 - core]]
        part_of[part] = order
        for slot, other in enumerate(order):
            slot_of[part, other] = slot
    own = lax.axis_index("dp")
    pick = lambda table: lax.dynamic_slice(jnp.asarray(table), (own, 0), (1, 8))[0]
    return pick(part_of), pick(slot_of)


def swap(value, hop):
    return lax.ppermute(value, "dp", [(i, i ^ NEAR[i & 1][hop]) for i in range(8)])


def swap_core(value):
    return lax.ppermute(value, "dp", [(i, i ^ 1) for i in range(8)])


def after(value, *others):
    return lax.optimization_barrier((value, *others))[0]


class Gather:
    def __init__(self, group, ahead=None, *gates):
        own, again = group, group
        if ahead is not None:
            own = after(own, ahead.second)
            again = after(again, ahead.third, *gates)
        self.first = swap(own, 1)
        self.second = swap(again, 2)
        self.third = swap(self.first, 2)
        self.near = [group, self.first, self.second, self.third]

    def pieces(self, *gates):
        late = [after(piece, *gates) if gates else piece for piece in self.near[2:]]
        return self.near + [swap_core(piece) for piece in self.near[:2] + late]


class Scatter:
    def __init__(self, own, send):
        self.own = own
        self.came = swap_core(send)

    def near(self, *gates):
        self.zero, self.one, self.sent = add_halves(after(self.own, *gates), self.came)
        return self.sent

    def send(self, *gates):
        self.far = swap(after(self.sent, *gates), 2)

    def back(self, *gates):
        one = after(self.one, *gates) if gates else self.one
        one = one.astype(jnp.float32) + self.far[0].astype(jnp.float32)
        one = one.astype(jnp.bfloat16)
        self.last = swap(one, 1)
        return one

    def total(self, *gates):
        zero = after(self.zero, *gates)
        total = zero.astype(jnp.float32) + self.far[1].astype(jnp.float32)
        self.sum = (total + self.last.astype(jnp.float32)).astype(jnp.bfloat16)
        return self.sum

    def end(self):
        return lax.psum_scatter(self.sum, "fsdp", scatter_dimension=0, tiled=False)


def swap_bit(value, axis, bit):
    size = lax.axis_size(axis)
    return lax.ppermute(value, axis, [(i, i ^ (1 << bit)) for i in range(size)])


def bit_of(axis, bit):
    return (lax.axis_index(axis) >> bit) & 1 == 1


def small_gather(value, axis):
    if not is_cube():
        return lax.all_gather(value, axis, axis=0, tiled=True)
    for bit in range(lax.axis_size(axis).bit_length() - 1):
        other = swap_bit(value, axis, bit)
        value = jnp.where(
            bit_of(axis, bit),
            jnp.concatenate([other, value], axis=0),
            jnp.concatenate([value, other], axis=0),
        )
    return value


def gather_links_first(value, axis):
    if not is_cube():
        return lax.all_gather(value, axis, axis=0, tiled=True)
    bits = lax.axis_size(axis).bit_length() - 1
    rest = value.shape
    for done, bit in enumerate(reversed(range(bits))):
        other = swap_bit(value, axis, bit)
        value = jnp.where(
            bit_of(axis, bit),
            jnp.stack([other, value], axis=done),
            jnp.stack([value, other], axis=done),
        )
    return value.reshape(-1, *rest[1:])


def small_scatter(value, axis):
    if not is_cube():
        return lax.psum_scatter(value, axis, scatter_dimension=0, tiled=True)
    for bit in reversed(range(lax.axis_size(axis).bit_length() - 1)):
        half = value.shape[0] // 2
        high = bit_of(axis, bit)
        keep = jnp.where(high, value[half:], value[:half])
        value = keep + swap_bit(jnp.where(high, value[:half], value[half:]), axis, bit)
    return value


def small_sum(value, axis):
    if not is_cube():
        return lax.psum(value, axis)
    for bit in range(lax.axis_size(axis).bit_length() - 1):
        value = value + swap_bit(value, axis, bit)
    return value


def gather_shards(shard):
    rows, width = shard.shape
    groups, parts = lax.axis_size("fsdp"), lax.axis_size("dp")
    full = lax.all_gather(shard, ("fsdp", "dp"), axis=0, tiled=True)
    return full.reshape(groups, parts, rows, width)


def scatter_sum(terms):
    groups, parts, rows, width = terms.shape
    return lax.psum_scatter(
        terms.reshape(groups * parts * rows, width),
        ("fsdp", "dp"),
        scatter_dimension=0,
        tiled=True,
    )


def pack_down(natural, groups, parts, rows):
    total, width = natural.shape
    split = natural.reshape(parts, total // (parts * rows), rows, groups, width // groups)
    return split.transpose(3, 0, 2, 1, 4).reshape(groups, parts, rows, width)


def unpack_down(packed, fold):
    groups, parts, rows, width = packed.shape
    split = packed.reshape(groups, parts, rows, fold, width // fold)
    return split.transpose(1, 3, 2, 0, 4).reshape(parts * fold * rows, width)


def body(
    images,
    time_vector,
    timesteps,
    offset_index,
    query_weight,
    key_weight,
    value_weight,
    tquery_weight,
    tvalue_weight,
    proj_weight,
    proj_bias,
    first_gain,
    first_shift,
    second_gain,
    second_shift,
    up_weight,
    down_weight,
    up_bias,
    down_bias,
    bias_table,
    cotangent,
):
    low = jnp.bfloat16
    wide = jnp.float32
    count, tokens, width = images.shape
    rows = count * tokens
    groups, parts = lax.axis_size("fsdp"), lax.axis_size("dp")
    shard_rows, shard_cols = query_weight.shape
    group_heads, table_rows = bias_table.shape
    heads = group_heads * groups
    fold = down_weight.shape[0] // shard_rows
    own_part = lax.axis_index("dp")
    own_group = lax.axis_index("fsdp")

    wire_attn = jnp.concatenate([query_weight, key_weight, value_weight, proj_weight], axis=1)
    wire_down = jnp.concatenate(
        [down_weight[g * shard_rows : (g + 1) * shard_rows] for g in range(fold)], axis=1
    )
    small = jnp.concatenate(
        [
            proj_bias,
            first_gain,
            first_shift,
            second_gain,
            second_shift,
            down_bias,
            up_bias,
            bias_table.reshape(-1),
        ]
    )
    small = jnp.pad(small, (0, -small.shape[0] % 1024)).reshape(-1, LANES)
    time_low = (time_vector.astype(wide) + sinusoid(timesteps, width)).astype(low)
    both = jnp.concatenate([small, time_low.reshape(-1, LANES)], axis=0)
    both = small_gather(both[None], "fsdp")
    small_all = both[:, : small.shape[0]].reshape(groups, -1)

    def vector_of(slot):
        return small_all[:, slot * shard_cols : (slot + 1) * shard_cols].reshape(-1).astype(wide)

    proj_b, gain_one, shift_one, gain_two, shift_two, down_b = (vector_of(i) for i in range(6))
    at = 6 * shard_cols
    up_b = small_all[:, at : at + up_bias.shape[0]].astype(wide)
    at = at + up_bias.shape[0]
    table = small_all[:, at : at + group_heads * table_rows].reshape(heads, table_rows)
    table = jnp.pad(table, ((0, 0), (0, 8 * LANES - table_rows)))
    bias = position_bias(offset_index, table)

    time_rows = both[:, small.shape[0] :].reshape(groups * count, width)
    time_weight = gather_links_first(
        jnp.concatenate([tquery_weight, tvalue_weight], axis=1), "dp"
    )
    time_part = small_gather(matmul(time_rows, time_weight)[None], "fsdp")
    time_own = lax.dynamic_slice(
        time_part, (0, own_group * count, 0), (groups, count, 2 * shard_cols)
    )
    gap = jnp.zeros((groups, count, shard_cols), wide)
    kept = -(-3 * shard_cols // LANES) * LANES
    time_add = jnp.concatenate(
        [
            time_own[:, :, :shard_cols],
            gap,
            time_own[:, :, shard_cols:],
            gap[:, :, : kept - 3 * shard_cols],
        ],
        axis=2,
    )

    cube = is_cube()
    if cube:
        part_of, slot_of = part_tables()
        attn_group = lax.all_gather(wire_attn, "fsdp", axis=0, tiled=False)
        up_group = lax.all_gather(after(up_weight, both), "fsdp", axis=0, tiled=False)
        down_group = lax.all_gather(after(wire_down, both), "fsdp", axis=0, tiled=False)
        attn_move = Gather(after(attn_group, time_weight))
        up_move = Gather(after(up_group, bias), attn_move)
        attn_pieces = attn_move.pieces()
    else:
        part_of = jnp.zeros((1,), jnp.int32)
        attn_pieces = [gather_shards(wire_attn).reshape(groups, width, width)]
        up_pieces = [gather_shards(up_weight).reshape(groups, width, width)]
        down_full = unpack_down(gather_shards(wire_down), fold)

    x_rows = images.reshape(rows, width).astype(wide)
    normed, _, _ = normalize(x_rows, gain_one, shift_one)
    normed_low = normed.astype(low)
    qkv, probs, mixed_split, proj_full, attn_full = attend(
        part_of, attn_pieces, normed_low, time_add, bias, count, tokens
    )
    if cube:
        up_pieces = up_move.pieces(mixed_split)
        down_move = Gather(down_group, up_move, mixed_split)
        mixed_split = after(mixed_split, down_move.first)
    mixed = mixed_split.transpose(1, 0, 2).reshape(rows, width)
    hidden = x_rows + (matmul(mixed, proj_full) + proj_b)
    second, _, _ = normalize(hidden, gain_two, shift_two)
    second_low = second.astype(low)
    grad_low = cotangent.reshape(rows, width)
    wire = (groups, parts, shard_rows, width)
    activ, slope, up_full = up_forward(part_of, up_pieces, second_low, up_b)
    grad_cols = grad_low
    if cube:
        down_pieces = down_move.pieces(activ)
        down_full = unpack_pieces(part_of, down_pieces, fold)
        own, send = down_slot_grad(
            slot_of,
            after(activ, *down_pieces),
            grad_low,
            parts,
            shard_rows,
        )
        down_move = Scatter(own, send)
        grad_cols = after(grad_low, down_move.near(down_full))
        down_move.send()
    def lines_of(*values):
        return jnp.concatenate([jnp.stack(values), jnp.zeros((8 - len(values), width), wide)])

    d_pre, layer_out, d_hidden, d_hidden_low, down_sums, up_sums = down_back(
        grad_cols, hidden, lines_of(gain_two, down_b), activ, slope, up_full, down_full
    )
    layer_out = layer_out.reshape(count, tokens, width)
    d_hidden_cols = d_hidden_low
    if cube:
        d_hidden_cols = after(d_hidden_low, down_move.back())
    d_packed, pairs, d_time = attend_back(d_hidden_cols, proj_full, qkv, probs)
    attn_back = attn_full
    if cube:
        normed_t = after(normed_low.T, down_move.last)
        own, send = slot_grad(
            pair_grad_kernel, slot_of, [normed_t, mixed.T], d_packed, parts, "pair_grad"
        )
        attn_move = Scatter(own, after(send, down_move.total()))
        down_sum = down_move.end()
        second_t = after(second_low.T, attn_move.near())
        attn_move.send()
        own, send = slot_grad(one_grad_kernel, slot_of, [second_t], d_pre, parts, "up_grad")
        attn_back = after(attn_full, send)
    else:
        grad_down = jnp.concatenate([contract_rows(a, grad_low) for a in activ], axis=0)
        down_sum = scatter_sum(pack_down(grad_down.astype(low), groups, parts, shard_rows))
        grad_up = jnp.stack([contract_rows(second_low, d).astype(low) for d in d_pre])
        up_sum = scatter_sum(grad_up.reshape(wire))
        cut = 3 * shard_cols
        grad_attn = jnp.stack(
            [
                jnp.concatenate(
                    [contract_rows(normed_low, d[:, :cut]), contract_rows(mixed, d[:, cut:])],
                    axis=1,
                )
                for d in d_packed
            ]
        )
        attn_sum = scatter_sum(grad_attn.astype(low).reshape(wire))

    images_grad, input_sums = input_grad(
        d_packed, attn_back, images.reshape(rows, width), d_hidden, lines_of(gain_one)
    )
    images_grad = images_grad.reshape(count, tokens, width)

    if cube:
        attn_one = attn_move.back(images_grad)
        up_move = Scatter(own, after(send, attn_one, down_sum))
        up_pair = up_move.near(attn_one)
        up_move.send()
        attn_total = attn_move.total()
        pairs = after(pairs, up_pair, attn_total)
    table_sum = table_gradient(offset_index, pairs)
    if cube:
        d_time = after(d_time, table_sum)
        up_one = up_move.back()
        up_total = up_move.total()
    d_time = jnp.concatenate(
        [d_time[:, :, :shard_cols], d_time[:, :, 2 * shard_cols : 3 * shard_cols]], axis=2
    ).astype(low)
    d_time = d_time.transpose(1, 0, 2).reshape(count, groups * 2 * shard_cols)
    d_time_rows = small_gather(d_time, "fsdp")
    d_time_cols = lax.dynamic_slice(
        d_time_rows, (0, own_group * 2 * shard_cols), (groups * count, 2 * shard_cols)
    )
    time_grads = contract_rows(time_rows, d_time_cols).astype(low)
    if cube:
        time_grads = after(time_grads, up_total)
    time_grads = small_scatter(time_grads, "dp")
    back = times_transposed(d_time_cols, time_weight).reshape(-1, LANES)

    vectors = jnp.concatenate(
        [down_sums[:4], input_sums[:2], up_sums.reshape(groups, width)]
    ).reshape(-1, LANES)
    flat = jnp.concatenate([vectors, table_sum, back], axis=0)
    ends = (vectors.shape[0], vectors.shape[0] + table_sum.shape[0])
    flat = small_sum(flat, "fsdp")
    time_grad = lax.dynamic_slice(
        flat[ends[1] :].reshape(groups * count, width), (own_group * count, 0), (count, width)
    )
    flat = flat[: ends[1]]
    if cube:
        flat = after(flat, attn_total, up_one)
    flat = small_sum(flat, "dp")
    vectors = flat[: ends[0]].reshape(-1, width)
    own = lax.dynamic_slice(vectors, (0, own_group * shard_cols), (6, shard_cols))
    proj_bg, gain2_g, shift2_g, down_bg, gain1_g, shift1_g = (own[i] for i in range(6))
    up_bg = lax.dynamic_slice(vectors, (6 + own_group, 0), (1, width))[0]
    table_grad = lax.dynamic_slice(
        flat[ends[0] : ends[1]], (own_group * group_heads * 8, 0), (group_heads * 8, LANES)
    )
    table_grad = table_grad.reshape(group_heads, 8 * LANES)[:, :table_rows]

    if cube:
        down_sum = after(down_sum, up_total)
        attn_sum = after(attn_move.end(), up_total)
        up_sum = up_move.end()
    time_grads = time_grads.astype(wide)
    tquery_grad, tvalue_grad = time_grads[:, :shard_cols], time_grads[:, shard_cols:]
    attn_sum = attn_sum.astype(wide)
    query_grad, key_grad, value_grad, proj_grad = (
        attn_sum[:, i * shard_cols : (i + 1) * shard_cols] for i in range(4)
    )
    down_sum = down_sum.astype(wide)
    down_grad = jnp.concatenate(
        [down_sum[:, g * shard_cols : (g + 1) * shard_cols] for g in range(fold)], axis=0
    )
    return (
        layer_out,
        images_grad,
        time_grad,
        query_grad,
        key_grad,
        value_grad,
        tquery_grad,
        tvalue_grad,
        proj_grad,
        proj_bg,
        gain1_g,
        shift1_g,
        gain2_g,
        shift2_g,
        up_sum.astype(wide),
        down_grad,
        up_bg,
        down_bg,
        table_grad,
    )


def solution(mesh):
    rows = P(BOTH, None, None)
    matrix = P("dp", "fsdp")
    vector = P("fsdp")
    table = P("fsdp", None)
    return jax.shard_map(
        body,
        mesh=mesh,
        in_specs=(
            (rows, P(BOTH, None), P(BOTH), P())
            + (matrix,) * 6
            + (vector,) * 5
            + (matrix,) * 2
            + (vector,) * 2
            + (table, rows)
        ),
        out_specs=(
            (rows, rows, P(BOTH, None))
            + (matrix,) * 6
            + (vector,) * 5
            + (matrix,) * 2
            + (vector,) * 2
            + (table,)
        ),
        check_vma=False,
    )
```

```python
import math

import jax
import jax.numpy as jnp
import numpy as np
from jax import lax
from jax.experimental import pallas as pl
from jax.experimental.pallas import tpu as pltpu
from jax.sharding import PartitionSpec as P

LANES = 128
BOTH = ("dp", "fsdp")
VMEM_LIMIT = 58 * 1024 * 1024


def lasting(microseconds):
    return pl.CostEstimate(
        flops=int(microseconds * 1e9), transcendentals=0, bytes_accessed=1
    )


def sinusoid(steps, model_width):
    half_width = model_width // 2
    frequency = jnp.exp(
        -math.log(10000.0) * jnp.arange(half_width).astype(jnp.float32) / half_width
    )
    angles = steps.astype(jnp.float32)[:, None] * frequency[None, :]
    return jnp.concatenate([jnp.sin(angles), jnp.cos(angles)], axis=1)


def matmul(left, right):
    return jnp.dot(left, right, preferred_element_type=jnp.float32)


def contract_rows(left, right):
    return lax.dot_general(
        left, right, (((0,), (0,)), ((), ())), preferred_element_type=jnp.float32
    )


def times_transposed(left, right):
    return lax.dot_general(
        left, right, (((1,), (1,)), ((), ())), preferred_element_type=jnp.float32
    )


def normalize(values, gain, shift):
    row_mean = jnp.mean(values, axis=-1, keepdims=True)
    centered = values - row_mean
    inv_std = lax.rsqrt(jnp.mean(centered * centered, axis=-1, keepdims=True) + 1e-06)
    unit_rows = centered * inv_std
    return (unit_rows * gain + shift, unit_rows, inv_std)


def norm_back(grad_rows, unit_rows, inv_std, gain):
    scaled = grad_rows * gain
    return inv_std * (
        scaled
        - jnp.mean(scaled, axis=-1, keepdims=True)
        - unit_rows * jnp.mean(scaled * unit_rows, axis=-1, keepdims=True)
    )


def gelu_slope(pre_act):
    return 0.5 * (1.0 + lax.erf(pre_act * (1.0 / math.sqrt(2.0)))) + pre_act * jnp.exp(
        -0.5 * pre_act * pre_act
    ) * (1.0 / math.sqrt(2.0 * math.pi))


def params(count=1):
    return pltpu.CompilerParams(
        dimension_semantics=("arbitrary",) * count, vmem_limit_bytes=VMEM_LIMIT
    )


def bias_kernel(index_ref, table_ref, bias_ref):
    heads, rows, tokens = bias_ref.shape
    chunks = table_ref.shape[2] // LANES
    pieces = [
        [
            jnp.broadcast_to(table_ref[h, :, c * LANES : (c + 1) * LANES], (8, LANES))
            for c in range(chunks)
        ]
        for h in range(heads)
    ]

    def some_rows(step, carry):
        at = pl.multiple_of(step * 8, 8)
        for col in range(tokens // LANES):
            lanes = slice(col * LANES, (col + 1) * LANES)
            index = index_ref[pl.ds(at, 8), lanes]
            low = index & (LANES - 1)
            high = index >> 7
            hits = [high == c for c in range(chunks)]
            for h in range(heads):
                found = jnp.take_along_axis(pieces[h][0], low, axis=1)
                for c in range(1, chunks):
                    found = jnp.where(
                        hits[c], jnp.take_along_axis(pieces[h][c], low, axis=1), found
                    )
                bias_ref[h, pl.ds(at, 8), lanes] = found
        return carry

    lax.fori_loop(0, rows // 8, some_rows, 0)


def position_bias(index, table):
    heads, padded = table.shape
    tokens = index.shape[0]
    group = heads // 4
    return pl.pallas_call(
        bias_kernel,
        grid=(4,),
        in_specs=[
            pl.BlockSpec((tokens, tokens), lambda f: (0, 0)),
            pl.BlockSpec((group, 1, padded), lambda f: (f, 0, 0)),
        ],
        out_specs=pl.BlockSpec((group, tokens, tokens), lambda f: (f, 0, 0)),
        out_shape=jax.ShapeDtypeStruct((heads, tokens, tokens), jnp.float32),
        compiler_params=params(),
        cost_estimate=lasting(20),
        name="position_bias",
    )(index, table.astype(jnp.float32).reshape(heads, 1, padded))


def table_kernel(index_ref, pairs_ref, out_ref):
    heads = pairs_ref.shape[0]
    tokens = index_ref.shape[1]
    rows = index_ref.shape[0]

    @pl.when(pl.program_id(0) == 0)
    def _():
        out_ref[...] = jnp.zeros_like(out_ref)

    sub = lax.broadcasted_iota(jnp.int32, (8, tokens), 0)
    lane_of = lax.broadcasted_iota(jnp.int32, (LANES, tokens), 0)

    def row_terms(row):
        index = index_ref[pl.ds(row, 1), :]
        low = jnp.broadcast_to(index & (LANES - 1), (LANES, tokens))
        high = jnp.broadcast_to(index >> 7, (8, tokens))
        hit = sub == high
        left = jnp.concatenate(
            [
                jnp.where(hit, jnp.broadcast_to(pairs_ref[h, pl.ds(row, 1), :], (8, tokens)), 0.0)
                for h in range(heads)
            ],
            axis=0,
        ).astype(jnp.bfloat16)
        right = jnp.where(lane_of == low, 1.0, 0.0).astype(jnp.bfloat16)
        return left, right

    def some_rows(step, total):
        terms = [row_terms(step * 4 + k) for k in range(4)]
        left = jnp.concatenate([t[0] for t in terms], axis=1)
        right = jnp.concatenate([t[1] for t in terms], axis=1)
        return total + times_transposed(left, right)

    out_ref[...] += lax.fori_loop(
        0, rows // 4, some_rows, jnp.zeros((heads * 8, LANES), jnp.float32)
    )


def table_gradient(index, pairs):
    heads, tokens, _ = pairs.shape
    block = 64
    return pl.pallas_call(
        table_kernel,
        grid=(tokens // block,),
        in_specs=[
            pl.BlockSpec((block, tokens), lambda i: (i, 0)),
            pl.BlockSpec((heads, block, tokens), lambda i: (0, i, 0)),
        ],
        out_specs=pl.BlockSpec((heads * 8, LANES), lambda i: (0, 0)),
        out_shape=jax.ShapeDtypeStruct((heads * 8, LANES), jnp.float32),
        compiler_params=params(),
        cost_estimate=lasting(18),
        name="table_gradient",
    )(index, pairs)


def piece_list(refs):
    out = []
    for ref in refs:
        out.extend([ref] if len(ref.shape) == 3 else [ref.at[k] for k in range(ref.shape[0])])
    return out


def piece_shape(refs):
    count = sum(1 if len(ref.shape) == 3 else ref.shape[0] for ref in refs)
    return (count, *refs[0].shape)


def load_group(part_ref, refs, held, in_sems, full_ref, out_sems):
    step = pl.program_id(0)
    pieces = piece_list(refs)
    rows = pieces[0].shape[1]

    def copy(group, j):
        at = pl.multiple_of(part_ref[j] * rows, 16)
        return pltpu.make_async_copy(
            pieces[j].at[group], held.at[group, pl.ds(at, rows)], in_sems.at[group, j]
        )

    @pl.when(step == 0)
    def _():
        for group in range(held.shape[0]):
            for j in range(len(pieces)):
                copy(group, j).start()

    for j in range(len(pieces)):
        copy(step, j).wait()
    pltpu.make_async_copy(held.at[step], full_ref.at[step], out_sems.at[step]).start()


def finish_groups(held, full_ref, out_sems):
    @pl.when(pl.program_id(0) == held.shape[0] - 1)
    def _():
        for group in range(held.shape[0]):
            pltpu.make_async_copy(held.at[group], full_ref.at[group], out_sems.at[group]).wait()


def piece_call(kernel, name, part_of, pieces, inputs, in_specs, out_specs, out_shapes):
    parts, groups, rows, packed = piece_shape(pieces)
    depth = rows * parts
    full = jax.ShapeDtypeStruct((groups, depth, packed), pieces[0].dtype)
    anywhere = pl.BlockSpec(memory_space=pl.ANY)
    return pl.pallas_call(
        kernel,
        grid_spec=pltpu.PrefetchScalarGridSpec(
            num_scalar_prefetch=1,
            grid=(groups,),
            in_specs=in_specs + [anywhere] * len(pieces),
            out_specs=out_specs + [anywhere],
            scratch_shapes=[
                pltpu.VMEM((groups, depth, packed), pieces[0].dtype),
                pltpu.SemaphoreType.DMA((groups, parts)),
                pltpu.SemaphoreType.DMA((groups,)),
            ],
        ),
        out_shape=out_shapes + [full],
        compiler_params=params(),
        cost_estimate=lasting(13),
        name=name,
    )(part_of, *inputs, *pieces)


def attend_kernel(part_ref, normed_ref, add_ref, bias_ref, *refs):
    *pieces, qkv_ref, probs_ref, mixed_ref, proj_ref, full_ref, held, in_sems, out_sems = refs
    images, heads = probs_ref.shape[1], probs_ref.shape[2]
    tokens = probs_ref.shape[3]
    width = mixed_ref.shape[2]
    size = width // heads
    scale = 1.0 / math.sqrt(size)
    kept = qkv_ref.shape[2]
    step = pl.program_id(0)
    load_group(part_ref, pieces, held, in_sems, full_ref, out_sems)
    for image in range(images):
        rows = slice(image * tokens, (image + 1) * tokens)
        acc = matmul(normed_ref[rows, :], held[step, :, :kept])
        qkv_ref[0, rows, :] = (acc + add_ref[0, image : image + 1, :]).astype(jnp.bfloat16)
    for image in range(images):
        rows = slice(image * tokens, (image + 1) * tokens)
        both = qkv_ref[0, rows, :]
        outs = []
        for head in range(heads):
            at = head * size
            query = both[:, at : at + size]
            keys = both[:, width + at : width + at + size]
            values = both[:, 2 * width + at : 2 * width + at + size]
            scores = times_transposed(query, keys) * scale + bias_ref[head]
            peak = jnp.max(scores, axis=-1, keepdims=True)
            expo = jnp.exp(scores - peak)
            total = jnp.sum(expo, axis=-1, keepdims=True)
            probs = (expo / total).astype(jnp.bfloat16)
            probs_ref[0, image, head] = probs
            outs.append(matmul(probs, values))
        mixed_ref[0, rows, :] = jnp.concatenate(outs, axis=1).astype(jnp.bfloat16)
    for group in range(held.shape[0]):

        @pl.when(step == group)
        def _(group=group):
            proj_ref[:, group * width : (group + 1) * width] = held[group, :, 3 * width :]

    finish_groups(held, full_ref, out_sems)


def attend(part_of, pieces, normed, add, bias, images, tokens):
    parts, groups, part_rows, packed = piece_shape(pieces)
    depth = part_rows * parts
    heads = bias.shape[0] // groups
    width = packed // groups
    kept = add.shape[2]
    rows = images * tokens
    low = jnp.bfloat16
    return piece_call(
        attend_kernel,
        "attend",
        part_of,
        pieces,
        [normed, add, bias],
        [
            pl.BlockSpec((rows, depth), lambda f, p: (0, 0)),
            pl.BlockSpec((1, images, kept), lambda f, p: (f, 0, 0)),
            pl.BlockSpec((heads, tokens, tokens), lambda f, p: (f, 0, 0)),
        ],
        [
            pl.BlockSpec((1, rows, kept), lambda f, p: (f, 0, 0)),
            pl.BlockSpec((1, images, heads, tokens, tokens), lambda f, p: (f, 0, 0, 0, 0)),
            pl.BlockSpec((1, rows, width), lambda f, p: (f, 0, 0)),
            pl.BlockSpec((depth, packed), lambda f, p: (0, 0)),
        ],
        [
            jax.ShapeDtypeStruct((groups, rows, kept), low),
            jax.ShapeDtypeStruct((groups, images, heads, tokens, tokens), low),
            jax.ShapeDtypeStruct((groups, rows, width), low),
            jax.ShapeDtypeStruct((depth, packed), low),
        ],
    )


def up_kernel(part_ref, second_ref, bias_ref, *refs):
    *pieces, activ_ref, slope_ref, full_ref, held, in_sems, out_sems = refs
    load_group(part_ref, pieces, held, in_sems, full_ref, out_sems)
    weight = held[pl.program_id(0)]
    block = 256
    for start in range(0, second_ref.shape[0], block):
        rows = slice(start, start + block)
        pre = matmul(second_ref[rows, :], weight) + bias_ref[0]
        below = 0.5 * (1.0 + lax.erf(pre * (1.0 / math.sqrt(2.0))))
        density = jnp.exp(-0.5 * pre * pre) * (1.0 / math.sqrt(2.0 * math.pi))
        activ_ref[0, rows, :] = (pre * below).astype(jnp.bfloat16)
        slope_ref[0, rows, :] = (below + pre * density).astype(jnp.bfloat16)
    finish_groups(held, full_ref, out_sems)


def up_forward(part_of, pieces, second, bias):
    _, groups, _, packed = piece_shape(pieces)
    rows, depth = second.shape
    wide = pl.BlockSpec((1, rows, packed), lambda f, p: (f, 0, 0))
    shape = jax.ShapeDtypeStruct((groups, rows, packed), jnp.bfloat16)
    return piece_call(
        up_kernel,
        "up_forward",
        part_of,
        pieces,
        [second, bias.reshape(groups, 1, packed)],
        [
            pl.BlockSpec((rows, depth), lambda f, p: (0, 0)),
            pl.BlockSpec((1, 1, packed), lambda f, p: (f, 0, 0)),
        ],
        [wide, wide],
        [shape, shape],
    )


def column_sum(value):
    return jnp.sum(value, axis=0, keepdims=True)


def down_back_kernel(
    grad_ref,
    hidden_ref,
    row_ref,
    activ_ref,
    slope_ref,
    up_ref,
    down_ref,
    pre_ref,
    out_ref,
    d_hidden_ref,
    d_low_ref,
    sum_ref,
    up_sum_ref,
    total,
    second,
):
    step = pl.program_id(0)
    weight = down_ref[...]
    d_activ = times_transposed(grad_ref[...], weight)
    d_pre = (d_activ * slope_ref[0].astype(jnp.float32)).astype(jnp.bfloat16)
    pre_ref[0] = d_pre
    up_sum_ref[0] = column_sum(d_pre.astype(jnp.float32))
    part = times_transposed(d_pre, up_ref[0])
    more = matmul(activ_ref[0], weight)

    @pl.when(step == 0)
    def _():
        second[...] = part
        total[...] = more

    @pl.when(step > 0)
    def _():
        second[...] += part
        total[...] += more

    @pl.when(step == pl.num_programs(0) - 1)
    def _():
        block = 64
        gain, shift = row_ref[0:1, :], row_ref[1:2, :]
        sum_ref[...] = jnp.zeros_like(sum_ref)

        def some_rows(at, carry):
            rows = pl.ds(pl.multiple_of(at * block, block), block)
            hidden = hidden_ref[rows, :]
            out_ref[rows, :] = (hidden + shift + total[rows, :]).astype(jnp.bfloat16)
            _, unit, inv = normalize(hidden, gain, 0.0)
            d_second = second[rows, :]
            grad = grad_ref[rows, :].astype(jnp.float32)
            d_hidden = grad + norm_back(d_second, unit, inv, gain)
            d_low = d_hidden.astype(jnp.bfloat16)
            d_hidden_ref[rows, :] = d_hidden
            d_low_ref[rows, :] = d_low
            sum_ref[0:1, :] += column_sum(d_low.astype(jnp.float32))
            sum_ref[1:2, :] += column_sum(d_second * unit)
            sum_ref[2:3, :] += column_sum(d_second)
            sum_ref[3:4, :] += column_sum(grad)
            return carry

        lax.fori_loop(0, hidden_ref.shape[0] // block, some_rows, 0)


def down_back(grad, hidden, lines, activ, slope, up_full, down_full):
    groups, rows, packed = activ.shape
    depth = up_full.shape[1]
    whole = pl.BlockSpec((rows, depth), lambda f: (0, 0))
    mine = pl.BlockSpec((1, rows, packed), lambda f: (f, 0, 0))
    few = pl.BlockSpec((8, depth), lambda f: (0, 0))
    return pl.pallas_call(
        down_back_kernel,
        grid=(groups,),
        in_specs=[
            whole,
            whole,
            few,
            mine,
            mine,
            pl.BlockSpec((1, depth, packed), lambda f: (f, 0, 0)),
            pl.BlockSpec((packed, depth), lambda f: (f, 0)),
        ],
        out_specs=[
            mine,
            whole,
            whole,
            whole,
            few,
            pl.BlockSpec((1, 1, packed), lambda f: (f, 0, 0)),
        ],
        out_shape=[
            jax.ShapeDtypeStruct((groups, rows, packed), jnp.bfloat16),
            jax.ShapeDtypeStruct((rows, depth), jnp.bfloat16),
            jax.ShapeDtypeStruct((rows, depth), jnp.float32),
            jax.ShapeDtypeStruct((rows, depth), jnp.bfloat16),
            jax.ShapeDtypeStruct((8, depth), jnp.float32),
            jax.ShapeDtypeStruct((groups, 1, packed), jnp.float32),
        ],
        scratch_shapes=[
            pltpu.VMEM((rows, depth), jnp.float32),
            pltpu.VMEM((rows, depth), jnp.float32),
        ],
        compiler_params=params(),
        cost_estimate=lasting(33),
        name="down_back",
    )(grad, hidden, lines, activ, slope, up_full, down_full)


def attend_back_kernel(
    hidden_ref, proj_ref, qkv_ref, probs_ref, out_ref, pairs_ref, time_ref
):
    images, heads = probs_ref.shape[1], probs_ref.shape[2]
    tokens = probs_ref.shape[3]
    width = proj_ref.shape[0]
    size = width // heads
    scale = 1.0 / math.sqrt(size)
    for image in range(images):
        rows = slice(image * tokens, (image + 1) * tokens)
        both = qkv_ref[0, rows, :]
        grads = times_transposed(hidden_ref[rows, :], proj_ref[...]).astype(jnp.bfloat16)
        d_query, d_keys, d_values = [], [], []
        for head in range(heads):
            at = head * size
            query = both[:, at : at + size]
            keys = both[:, width + at : width + at + size]
            values = both[:, 2 * width + at : 2 * width + at + size]
            grad = grads[:, at : at + size]
            probs_low = probs_ref[0, image, head]
            probs = probs_low.astype(jnp.float32)
            d_values.append(contract_rows(probs_low, grad))
            d_probs = times_transposed(grad, values)
            moved = probs * d_probs
            d_scores = moved - probs * jnp.sum(moved, axis=-1, keepdims=True)
            d_low = d_scores.astype(jnp.bfloat16)
            if image == 0:
                pairs_ref[head] = d_low.astype(jnp.float32)
            else:
                pairs_ref[head] += d_low.astype(jnp.float32)
            d_query.append(matmul(d_low, keys) * scale)
            d_keys.append(contract_rows(d_low, query) * scale)
        packed = jnp.concatenate(d_query + d_keys + d_values, axis=1).astype(jnp.bfloat16)
        out_ref[0, rows, : 3 * width] = packed
        time_ref[0, image : image + 1, :] = column_sum(packed.astype(jnp.float32))
    for group in range(hidden_ref.shape[1] // width):

        @pl.when(pl.program_id(0) == group)
        def _(group=group):
            out_ref[0, :, 3 * width :] = hidden_ref[:, group * width : (group + 1) * width]


def attend_back(hidden, proj, qkv, probs):
    rows, packed = hidden.shape
    groups, images, heads, tokens, _ = probs.shape
    kept = qkv.shape[2]
    width = packed // groups
    return pl.pallas_call(
        attend_back_kernel,
        grid=(groups,),
        in_specs=[
            pl.BlockSpec((rows, packed), lambda f: (0, 0)),
            pl.BlockSpec((width, packed), lambda f: (f, 0)),
            pl.BlockSpec((1, rows, kept), lambda f: (f, 0, 0)),
            pl.BlockSpec((1, images, heads, tokens, tokens), lambda f: (f, 0, 0, 0, 0)),
        ],
        out_specs=[
            pl.BlockSpec((1, rows, packed), lambda f: (f, 0, 0)),
            pl.BlockSpec((heads, tokens, tokens), lambda f: (f, 0, 0)),
            pl.BlockSpec((1, images, 3 * width), lambda f: (f, 0, 0)),
        ],
        out_shape=[
            jax.ShapeDtypeStruct((groups, rows, packed), jnp.bfloat16),
            jax.ShapeDtypeStruct((groups * heads, tokens, tokens), jnp.float32),
            jax.ShapeDtypeStruct((groups, images, 3 * width), jnp.float32),
        ],
        compiler_params=params(),
        cost_estimate=lasting(19),
        name="attend_back",
    )(hidden, proj, qkv, probs)


def input_grad_kernel(
    right_ref, weight_ref, image_ref, d_hidden_ref, row_ref, out_ref, sum_ref, total
):
    step = pl.program_id(0)
    cut = 3 * (right_ref.shape[2] // 4)
    kept = -(-cut // LANES) * LANES
    lane = lax.broadcasted_iota(jnp.int32, (1, kept), 1)
    right = right_ref[0, :, :kept]
    right = jnp.where(lane < cut, right.astype(jnp.float32), 0.0).astype(jnp.bfloat16)
    part = times_transposed(right, weight_ref[0, :, :kept])

    @pl.when(step == 0)
    def _():
        total[...] = part

    @pl.when(step > 0)
    def _():
        total[...] += part

    @pl.when(step == pl.num_programs(0) - 1)
    def _():
        block = 64
        gain = row_ref[0:1, :]
        sum_ref[...] = jnp.zeros_like(sum_ref)

        def some_rows(at, carry):
            rows = pl.ds(pl.multiple_of(at * block, block), block)
            _, unit, inv = normalize(image_ref[rows, :].astype(jnp.float32), gain, 0.0)
            d_normed = total[rows, :]
            d_input = d_hidden_ref[rows, :] + norm_back(d_normed, unit, inv, gain)
            out_ref[rows, :] = d_input.astype(jnp.bfloat16)
            sum_ref[0:1, :] += column_sum(d_normed * unit)
            sum_ref[1:2, :] += column_sum(d_normed)
            return carry

        lax.fori_loop(0, image_ref.shape[0] // block, some_rows, 0)


def input_grad(right, weight, images, d_hidden, lines):
    groups, rows, packed = right.shape
    whole = pl.BlockSpec((rows, packed), lambda f: (0, 0))
    few = pl.BlockSpec((8, packed), lambda f: (0, 0))
    return pl.pallas_call(
        input_grad_kernel,
        grid=(groups,),
        in_specs=[
            pl.BlockSpec((1, rows, packed), lambda f: (f, 0, 0)),
            pl.BlockSpec((1, packed, packed), lambda f: (f, 0, 0)),
            whole,
            whole,
            few,
        ],
        out_specs=[whole, few],
        out_shape=[
            jax.ShapeDtypeStruct((rows, packed), jnp.bfloat16),
            jax.ShapeDtypeStruct((8, packed), jnp.float32),
        ],
        scratch_shapes=[pltpu.VMEM((rows, packed), jnp.float32)],
        compiler_params=params(),
        cost_estimate=lasting(1),
        name="input_grad",
    )(right, weight, images, d_hidden, lines)


def store_slot(slot, own_ref, send_ref, at, value):
    half = own_ref.shape[0]

    @pl.when(slot < half)
    def _():
        own_ref[(slot,) + at] = value

    @pl.when(slot >= half)
    def _():
        send_ref[(slot - half,) + at] = value


def pair_grad_kernel(slot_ref, one_ref, two_ref, right_ref, own_ref, send_ref):
    cut = 3 * (right_ref.shape[2] // 4)
    below = cut // LANES * LANES
    above = below + LANES
    rows = own_ref.shape[2]
    right = right_ref[0]
    lane = lax.broadcasted_iota(jnp.int32, (rows, LANES), 1)
    first = matmul(one_ref[...], right[:, :above])
    last = matmul(two_ref[...], right[:, below:])
    for part in range(2 * own_ref.shape[0]):
        at = slice(part * rows, (part + 1) * rows)
        value = jnp.concatenate(
            [
                first[at, :below],
                jnp.where(lane < cut - below, first[at, below:], last[at, :LANES]),
                last[at, LANES:],
            ],
            axis=1,
        ).astype(jnp.bfloat16)
        store_slot(slot_ref[part], own_ref, send_ref, (0,), value)


def one_grad_kernel(slot_ref, one_ref, right_ref, own_ref, send_ref):
    rows = own_ref.shape[2]
    first = matmul(one_ref[...], right_ref[0])
    for part in range(2 * own_ref.shape[0]):
        value = first[part * rows : (part + 1) * rows].astype(jnp.bfloat16)
        store_slot(slot_ref[part], own_ref, send_ref, (0,), value)


def slot_grad(kernel, slots, lefts, right, parts, name):
    groups, rows, packed = right.shape
    depth = lefts[0].shape[0]
    half = jax.ShapeDtypeStruct((parts // 2, groups, depth // parts, packed), jnp.bfloat16)
    out = pl.BlockSpec((parts // 2, 1, depth // parts, packed), lambda f, s: (0, f, 0, 0))
    return pl.pallas_call(
        kernel,
        grid_spec=pltpu.PrefetchScalarGridSpec(
            num_scalar_prefetch=1,
            grid=(groups,),
            in_specs=[pl.BlockSpec((depth, rows), lambda f, s: (0, 0)) for _ in lefts]
            + [pl.BlockSpec((1, rows, packed), lambda f, s: (f, 0, 0))],
            out_specs=[out, out],
        ),
        out_shape=[half, half],
        compiler_params=params(),
        cost_estimate=lasting(18),
        name=name,
    )(slots, *lefts, right)


def down_grad_kernel(slot_ref, left_ref, right_ref, own_ref, send_ref):
    half, groups, rows, packed = own_ref.shape
    width = packed // groups
    value = contract_rows(left_ref[0], right_ref[...]).astype(jnp.bfloat16)
    each = 2 * half // groups
    fold = value.shape[0] // (each * rows)
    for part in range(each):
        slot = slot_ref[pl.program_id(0) * each + part]
        base = part * fold * rows
        for f in range(groups):
            block = jnp.concatenate(
                [
                    value[base + g * rows : base + (g + 1) * rows, f * width : (f + 1) * width]
                    for g in range(fold)
                ],
                axis=1,
            )
            store_slot(slot, own_ref, send_ref, (f,), block)


def down_slot_grad(slots, left, right, parts, part_rows):
    groups, rows, packed = left.shape
    half = jax.ShapeDtypeStruct((parts // 2, groups, part_rows, packed), jnp.bfloat16)
    out = pl.BlockSpec((parts // 2, groups, part_rows, packed), lambda f, s: (0, 0, 0, 0))
    return pl.pallas_call(
        down_grad_kernel,
        grid_spec=pltpu.PrefetchScalarGridSpec(
            num_scalar_prefetch=1,
            grid=(groups,),
            in_specs=[
                pl.BlockSpec((1, rows, packed), lambda f, s: (f, 0, 0)),
                pl.BlockSpec((rows, packed), lambda f, s: (0, 0)),
            ],
            out_specs=[out, out],
        ),
        out_shape=[half, half],
        compiler_params=params(),
        cost_estimate=lasting(18),
        name="down_grad",
    )(slots, left, right)


def add_kernel(one_ref, two_ref, three_ref, four_ref, came_ref, *outs):
    places = ((outs[0], (0,)), (outs[1], (0,)), (outs[2], (1, 0)), (outs[2], (0, 0)))
    for k, (mine, (out, at)) in enumerate(
        zip((one_ref, two_ref, three_ref, four_ref), places)
    ):
        total = mine[0, 0].astype(jnp.float32) + came_ref[k, 0].astype(jnp.float32)
        out[at] = total.astype(jnp.bfloat16)


def add_halves(own, came):
    half, groups, rows, packed = own.shape
    single = pl.BlockSpec((1, rows, packed), lambda f: (f, 0, 0))
    one = jax.ShapeDtypeStruct((groups, rows, packed), jnp.bfloat16)
    return pl.pallas_call(
        add_kernel,
        grid=(groups,),
        in_specs=[
            pl.BlockSpec((1, 1, rows, packed), lambda f, k=k: (k, f, 0, 0)) for k in range(half)
        ]
        + [pl.BlockSpec((half, 1, rows, packed), lambda f: (0, f, 0, 0))],
        out_specs=[single, single, pl.BlockSpec((2, 1, rows, packed), lambda f: (0, f, 0, 0))],
        out_shape=[one, one, jax.ShapeDtypeStruct((2, groups, rows, packed), jnp.bfloat16)],
        compiler_params=params(),
        cost_estimate=lasting(7),
        name="add_halves",
    )(*([own] * half), came)


def unpack_kernel(part_ref, *refs):
    *pieces, out_ref, held, sems = refs
    pieces = piece_list(pieces)
    step = pl.program_id(0)
    _, groups, rows, packed = held.shape
    width = packed // groups

    @pl.when(step == 0)
    def _():
        for j, piece in enumerate(pieces):
            pltpu.make_async_copy(piece, held.at[j], sems.at[j]).start()

    pltpu.make_async_copy(pieces[0], held.at[step], sems.at[step]).wait()
    for g in range(out_ref.shape[0] // rows):
        out_ref[g * rows : (g + 1) * rows, :] = jnp.concatenate(
            [held[step, f][:, g * width : (g + 1) * width] for f in range(groups)], axis=1
        )


def unpack_pieces(part_of, pieces, fold):
    parts, groups, rows, width = piece_shape(pieces)
    return pl.pallas_call(
        unpack_kernel,
        grid_spec=pltpu.PrefetchScalarGridSpec(
            num_scalar_prefetch=1,
            grid=(parts,),
            in_specs=[pl.BlockSpec(memory_space=pl.ANY)] * len(pieces),
            out_specs=pl.BlockSpec((fold * rows, width), lambda j, p: (p[j], 0)),
            scratch_shapes=[
                pltpu.VMEM((parts, groups, rows, width), pieces[0].dtype),
                pltpu.SemaphoreType.DMA((parts,)),
            ],
        ),
        out_shape=jax.ShapeDtypeStruct((parts * fold * rows, width), pieces[0].dtype),
        compiler_params=params(),
        cost_estimate=lasting(9),
        name="unpack_pieces",
    )(part_of, *pieces)


NEAR = ((0, 2, 4, 6), (0, 4, 2, 6))


def is_cube():
    return lax.axis_size("dp") == 8 and lax.axis_size("fsdp") == 4


def part_tables():
    part_of = np.zeros((8, 8), np.int32)
    slot_of = np.zeros((8, 8), np.int32)
    for part in range(8):
        core = part & 1
        order = [part ^ m for m in NEAR[core]] + [part ^ 1 ^ m for m in NEAR[1 - core]]
        part_of[part] = order
        for slot, other in enumerate(order):
            slot_of[part, other] = slot
    own = lax.axis_index("dp")
    pick = lambda table: lax.dynamic_slice(jnp.asarray(table), (own, 0), (1, 8))[0]
    return pick(part_of), pick(slot_of)


def swap(value, hop):
    return lax.ppermute(value, "dp", [(i, i ^ NEAR[i & 1][hop]) for i in range(8)])


def swap_core(value):
    return lax.ppermute(value, "dp", [(i, i ^ 1) for i in range(8)])


def after(value, *others):
    return lax.optimization_barrier((value, *others))[0]


class Gather:
    def __init__(self, group, ahead=None, *gates):
        own, again = group, group
        if ahead is not None:
            own = after(own, ahead.second)
            again = after(again, ahead.third, *gates)
        self.first = swap(own, 1)
        self.second = swap(again, 2)
        self.third = swap(self.first, 2)
        self.near = [group, self.first, self.second, self.third]

    def pieces(self, *gates):
        late = [after(piece, *gates) if gates else piece for piece in self.near[2:]]
        return self.near + [swap_core(piece) for piece in self.near[:2] + late]


class Scatter:
    def __init__(self, own, send):
        self.own = own
        self.came = swap_core(send)

    def near(self, *gates):
        self.zero, self.one, self.sent = add_halves(after(self.own, *gates), self.came)
        return self.sent

    def send(self, *gates):
        self.far = swap(after(self.sent, *gates), 2)

    def back(self, *gates):
        one = after(self.one, *gates) if gates else self.one
        one = one.astype(jnp.float32) + self.far[0].astype(jnp.float32)
        one = one.astype(jnp.bfloat16)
        self.last = swap(one, 1)
        return one

    def total(self, *gates):
        zero = after(self.zero, *gates)
        total = zero.astype(jnp.float32) + self.far[1].astype(jnp.float32)
        self.sum = (total + self.last.astype(jnp.float32)).astype(jnp.bfloat16)
        return self.sum

    def end(self):
        return lax.psum_scatter(self.sum, "fsdp", scatter_dimension=0, tiled=False)


def swap_bit(value, axis, bit):
    size = lax.axis_size(axis)
    return lax.ppermute(value, axis, [(i, i ^ (1 << bit)) for i in range(size)])


def bit_of(axis, bit):
    return (lax.axis_index(axis) >> bit) & 1 == 1


def small_gather(value, axis):
    if not is_cube():
        return lax.all_gather(value, axis, axis=0, tiled=True)
    for bit in range(lax.axis_size(axis).bit_length() - 1):
        other = swap_bit(value, axis, bit)
        value = jnp.where(
            bit_of(axis, bit),
            jnp.concatenate([other, value], axis=0),
            jnp.concatenate([value, other], axis=0),
        )
    return value


def gather_links_first(value, axis):
    if not is_cube():
        return lax.all_gather(value, axis, axis=0, tiled=True)
    bits = lax.axis_size(axis).bit_length() - 1
    rest = value.shape
    for done, bit in enumerate(reversed(range(bits))):
        other = swap_bit(value, axis, bit)
        value = jnp.where(
            bit_of(axis, bit),
            jnp.stack([other, value], axis=done),
            jnp.stack([value, other], axis=done),
        )
    return value.reshape(-1, *rest[1:])


def small_scatter(value, axis):
    if not is_cube():
        return lax.psum_scatter(value, axis, scatter_dimension=0, tiled=True)
    for bit in reversed(range(lax.axis_size(axis).bit_length() - 1)):
        half = value.shape[0] // 2
        high = bit_of(axis, bit)
        keep = jnp.where(high, value[half:], value[:half])
        value = keep + swap_bit(jnp.where(high, value[:half], value[half:]), axis, bit)
    return value


def scatter_core_first(value, axis):
    if not is_cube():
        return lax.psum_scatter(value, axis, scatter_dimension=0, tiled=True)
    bits = lax.axis_size(axis).bit_length() - 1
    value = value.reshape((2,) * bits + (-1, value.shape[1]))
    for bit in range(bits):
        place = bits - 1 - bit
        low, high = (lax.index_in_dim(value, side, place, keepdims=False) for side in range(2))
        on = bit_of(axis, bit)
        value = jnp.where(on, high, low) + swap_bit(jnp.where(on, low, high), axis, bit)
    return value


def small_sum(value, axis):
    if not is_cube():
        return lax.psum(value, axis)
    for bit in range(lax.axis_size(axis).bit_length() - 1):
        value = value + swap_bit(value, axis, bit)
    return value


def gather_shards(shard):
    rows, width = shard.shape
    groups, parts = lax.axis_size("fsdp"), lax.axis_size("dp")
    full = lax.all_gather(shard, ("fsdp", "dp"), axis=0, tiled=True)
    return full.reshape(groups, parts, rows, width)


def scatter_sum(terms):
    groups, parts, rows, width = terms.shape
    return lax.psum_scatter(
        terms.reshape(groups * parts * rows, width),
        ("fsdp", "dp"),
        scatter_dimension=0,
        tiled=True,
    )


def pack_down(natural, groups, parts, rows):
    total, width = natural.shape
    split = natural.reshape(parts, total // (parts * rows), rows, groups, width // groups)
    return split.transpose(3, 0, 2, 1, 4).reshape(groups, parts, rows, width)


def unpack_down(packed, fold):
    groups, parts, rows, width = packed.shape
    split = packed.reshape(groups, parts, rows, fold, width // fold)
    return split.transpose(1, 3, 2, 0, 4).reshape(parts * fold * rows, width)


def body(
    images,
    time_vector,
    timesteps,
    offset_index,
    query_weight,
    key_weight,
    value_weight,
    tquery_weight,
    tvalue_weight,
    proj_weight,
    proj_bias,
    first_gain,
    first_shift,
    second_gain,
    second_shift,
    up_weight,
    down_weight,
    up_bias,
    down_bias,
    bias_table,
    cotangent,
):
    low = jnp.bfloat16
    wide = jnp.float32
    count, tokens, width = images.shape
    rows = count * tokens
    groups, parts = lax.axis_size("fsdp"), lax.axis_size("dp")
    shard_rows, shard_cols = query_weight.shape
    group_heads, table_rows = bias_table.shape
    heads = group_heads * groups
    fold = down_weight.shape[0] // shard_rows
    own_part = lax.axis_index("dp")
    own_group = lax.axis_index("fsdp")

    wire_attn = jnp.concatenate([query_weight, key_weight, value_weight, proj_weight], axis=1)
    wire_down = jnp.concatenate(
        [down_weight[g * shard_rows : (g + 1) * shard_rows] for g in range(fold)], axis=1
    )
    small = jnp.concatenate(
        [
            proj_bias,
            first_gain,
            first_shift,
            second_gain,
            second_shift,
            down_bias,
            up_bias,
            bias_table.reshape(-1),
        ]
    )
    small = jnp.pad(small, (0, -small.shape[0] % 1024)).reshape(-1, LANES)
    time_low = (time_vector.astype(wide) + sinusoid(timesteps, width)).astype(low)
    both = jnp.concatenate([small, time_low.reshape(-1, LANES)], axis=0)
    both = small_gather(both[None], "fsdp")
    small_all = both[:, : small.shape[0]].reshape(groups, -1)

    def vector_of(slot):
        return small_all[:, slot * shard_cols : (slot + 1) * shard_cols].reshape(-1).astype(wide)

    proj_b, gain_one, shift_one, gain_two, shift_two, down_b = (vector_of(i) for i in range(6))
    at = 6 * shard_cols
    up_b = small_all[:, at : at + up_bias.shape[0]].astype(wide)
    at = at + up_bias.shape[0]
    table = small_all[:, at : at + group_heads * table_rows].reshape(heads, table_rows)
    table = jnp.pad(table, ((0, 0), (0, 8 * LANES - table_rows)))
    bias = position_bias(offset_index, table)

    time_rows = both[:, small.shape[0] :].reshape(groups * count, width)
    time_weight = gather_links_first(
        jnp.concatenate([tquery_weight, tvalue_weight], axis=1), "dp"
    )
    time_part = small_gather(matmul(time_rows, time_weight)[None], "fsdp")
    time_own = lax.dynamic_slice(
        time_part, (0, own_group * count, 0), (groups, count, 2 * shard_cols)
    )
    gap = jnp.zeros((groups, count, shard_cols), wide)
    kept = -(-3 * shard_cols // LANES) * LANES
    time_add = jnp.concatenate(
        [
            time_own[:, :, :shard_cols],
            gap,
            time_own[:, :, shard_cols:],
            gap[:, :, : kept - 3 * shard_cols],
        ],
        axis=2,
    )

    cube = is_cube()
    if cube:
        part_of, slot_of = part_tables()
        attn_group = lax.all_gather(wire_attn, "fsdp", axis=0, tiled=False)
        up_group = lax.all_gather(after(up_weight, both), "fsdp", axis=0, tiled=False)
        down_group = lax.all_gather(after(wire_down, both), "fsdp", axis=0, tiled=False)
        attn_move = Gather(after(attn_group, time_weight))
        up_move = Gather(after(up_group, bias), attn_move)
        attn_pieces = attn_move.pieces()
    else:
        part_of = jnp.zeros((1,), jnp.int32)
        attn_pieces = [gather_shards(wire_attn).reshape(groups, width, width)]
        up_pieces = [gather_shards(up_weight).reshape(groups, width, width)]
        down_full = unpack_down(gather_shards(wire_down), fold)

    x_rows = images.reshape(rows, width).astype(wide)
    normed, _, _ = normalize(x_rows, gain_one, shift_one)
    normed_low = normed.astype(low)
    qkv, probs, mixed_split, proj_full, attn_full = attend(
        part_of, attn_pieces, normed_low, time_add, bias, count, tokens
    )
    if cube:
        up_pieces = up_move.pieces(mixed_split)
        down_move = Gather(down_group, up_move, mixed_split)
        mixed_split = after(mixed_split, down_move.first)
    mixed = mixed_split.transpose(1, 0, 2).reshape(rows, width)
    hidden = x_rows + (matmul(mixed, proj_full) + proj_b)
    second, _, _ = normalize(hidden, gain_two, shift_two)
    second_low = second.astype(low)
    grad_low = cotangent.reshape(rows, width)
    wire = (groups, parts, shard_rows, width)
    activ, slope, up_full = up_forward(part_of, up_pieces, second_low, up_b)
    grad_cols = grad_low
    if cube:
        down_pieces = down_move.pieces(activ)
        down_full = unpack_pieces(part_of, down_pieces, fold)
        own, send = down_slot_grad(
            slot_of,
            after(activ, *down_pieces),
            grad_low,
            parts,
            shard_rows,
        )
        down_move = Scatter(own, send)
        grad_cols = after(grad_low, down_move.near(down_full))
        down_move.send()
    def lines_of(*values):
        return jnp.concatenate([jnp.stack(values), jnp.zeros((8 - len(values), width), wide)])

    d_pre, layer_out, d_hidden, d_hidden_low, down_sums, up_sums = down_back(
        grad_cols, hidden, lines_of(gain_two, down_b), activ, slope, up_full, down_full
    )
    layer_out = layer_out.reshape(count, tokens, width)
    d_hidden_cols = d_hidden_low
    if cube:
        d_hidden_cols = after(d_hidden_low, down_move.back())
    d_packed, pairs, d_time = attend_back(d_hidden_cols, proj_full, qkv, probs)
    attn_back = attn_full
    if cube:
        normed_t = after(normed_low.T, down_move.last)
        own, send = slot_grad(
            pair_grad_kernel, slot_of, [normed_t, mixed.T], d_packed, parts, "pair_grad"
        )
        attn_move = Scatter(own, after(send, down_move.total()))
        down_sum = down_move.end()
        second_t = after(second_low.T, attn_move.near())
        attn_move.send()
        own, send = slot_grad(one_grad_kernel, slot_of, [second_t], d_pre, parts, "up_grad")
        attn_back = after(attn_full, send)
    else:
        grad_down = jnp.concatenate([contract_rows(a, grad_low) for a in activ], axis=0)
        down_sum = scatter_sum(pack_down(grad_down.astype(low), groups, parts, shard_rows))
        grad_up = jnp.stack([contract_rows(second_low, d).astype(low) for d in d_pre])
        up_sum = scatter_sum(grad_up.reshape(wire))
        cut = 3 * shard_cols
        grad_attn = jnp.stack(
            [
                jnp.concatenate(
                    [contract_rows(normed_low, d[:, :cut]), contract_rows(mixed, d[:, cut:])],
                    axis=1,
                )
                for d in d_packed
            ]
        )
        attn_sum = scatter_sum(grad_attn.astype(low).reshape(wire))

    images_grad, input_sums = input_grad(
        d_packed, attn_back, images.reshape(rows, width), d_hidden, lines_of(gain_one)
    )
    images_grad = images_grad.reshape(count, tokens, width)

    if cube:
        attn_one = attn_move.back(images_grad)
        up_move = Scatter(own, after(send, attn_one, down_sum))
        up_pair = up_move.near(attn_one)
        up_move.send()
        attn_total = attn_move.total()
        pairs = after(pairs, up_pair, attn_total)
    table_sum = table_gradient(offset_index, pairs)
    if cube:
        d_time = after(d_time, table_sum)
        up_one = up_move.back()
        up_total = up_move.total()
    d_time = jnp.concatenate(
        [d_time[:, :, :shard_cols], d_time[:, :, 2 * shard_cols : 3 * shard_cols]], axis=2
    ).astype(low)
    d_time = d_time.transpose(1, 0, 2).reshape(count, groups * 2 * shard_cols)
    d_time_rows = small_gather(d_time, "fsdp")
    d_time_cols = lax.dynamic_slice(
        d_time_rows, (0, own_group * 2 * shard_cols), (groups * count, 2 * shard_cols)
    )
    time_grads = contract_rows(time_rows, d_time_cols).astype(low)
    if cube:
        time_grads = after(time_grads, up_total)
    time_grads = scatter_core_first(time_grads, "dp")
    back = times_transposed(d_time_cols, time_weight).reshape(-1, LANES)

    vectors = jnp.concatenate(
        [down_sums[:4], input_sums[:2], up_sums.reshape(groups, width)]
    ).reshape(-1, LANES)
    flat = jnp.concatenate([vectors, table_sum, back], axis=0)
    ends = (vectors.shape[0], vectors.shape[0] + table_sum.shape[0])
    flat = small_sum(flat, "fsdp")
    time_grad = lax.dynamic_slice(
        flat[ends[1] :].reshape(groups * count, width), (own_group * count, 0), (count, width)
    )
    flat = flat[: ends[1]]
    if cube:
        flat = after(flat, attn_total, up_one)
    flat = small_sum(flat, "dp")
    vectors = flat[: ends[0]].reshape(-1, width)
    own = lax.dynamic_slice(vectors, (0, own_group * shard_cols), (6, shard_cols))
    proj_bg, gain2_g, shift2_g, down_bg, gain1_g, shift1_g = (own[i] for i in range(6))
    up_bg = lax.dynamic_slice(vectors, (6 + own_group, 0), (1, width))[0]
    table_grad = lax.dynamic_slice(
        flat[ends[0] : ends[1]], (own_group * group_heads * 8, 0), (group_heads * 8, LANES)
    )
    table_grad = table_grad.reshape(group_heads, 8 * LANES)[:, :table_rows]

    if cube:
        down_sum = after(down_sum, up_total)
        attn_sum = after(attn_move.end(), up_total)
        up_sum = up_move.end()
    time_grads = time_grads.astype(wide)
    tquery_grad, tvalue_grad = time_grads[:, :shard_cols], time_grads[:, shard_cols:]
    attn_sum = attn_sum.astype(wide)
    query_grad, key_grad, value_grad, proj_grad = (
        attn_sum[:, i * shard_cols : (i + 1) * shard_cols] for i in range(4)
    )
    down_sum = down_sum.astype(wide)
    down_grad = jnp.concatenate(
        [down_sum[:, g * shard_cols : (g + 1) * shard_cols] for g in range(fold)], axis=0
    )
    return (
        layer_out,
        images_grad,
        time_grad,
        query_grad,
        key_grad,
        value_grad,
        tquery_grad,
        tvalue_grad,
        proj_grad,
        proj_bg,
        gain1_g,
        shift1_g,
        gain2_g,
        shift2_g,
        up_sum.astype(wide),
        down_grad,
        up_bg,
        down_bg,
        table_grad,
    )


def solution(mesh):
    rows = P(BOTH, None, None)
    matrix = P("dp", "fsdp")
    vector = P("fsdp")
    table = P("fsdp", None)
    return jax.shard_map(
        body,
        mesh=mesh,
        in_specs=(
            (rows, P(BOTH, None), P(BOTH), P())
            + (matrix,) * 6
            + (vector,) * 5
            + (matrix,) * 2
            + (vector,) * 2
            + (table, rows)
        ),
        out_specs=(
            (rows, rows, P(BOTH, None))
            + (matrix,) * 6
            + (vector,) * 5
            + (matrix,) * 2
            + (vector,) * 2
            + (table,)
        ),
        check_vma=False,
    )
```
